32 devices in a mesh: section: 2 (over core), dp: 16 (over z, y, x).
Axes of the slice: x: 2, y: 2, z: 4, core: 2. Of those that a mesh axis runs over, the one named last changes fastest.
Arguments:
- inputs: bfloat16 [9728, 256], P('dp'), may hold values from -6 to 6
- cotangent: bfloat16 [9728, 256], P('dp'), may hold values from -6 to 6
- vectors: float32 [2, 3328], P('section'), as said below
- kernels: float32 [2, 9, 256], P('section'), may hold values from -2 to 2
- w_qkv: float32 [2, 256, 768], P('section'), may hold values from -0.375 to 0.375
- w_proj: float32 [2, 256, 256], P('section'), may hold values from -0.75 to 0.75
- w_fc1: float32 [2, 256, 1024], P('section'), may hold values from -0.375 to 0.375
- w_fc2: float32 [2, 1024, 256], P('section'), may hold values from -0.1875 to 0.1875
- momentum_vectors: float32 [2, 3328], P('section'), may hold values from -0.09375 to 0.09375
- momentum_kernels: float32 [2, 9, 256], P('section'), may hold values from -0.046875 to 0.046875
- momentum_qkv: float32 [2, 256, 768], P('section'), may hold values from -0.02734375 to 0.02734375
- momentum_proj: float32 [2, 256, 256], P('section'), may hold values from -0.02734375 to 0.02734375
- momentum_fc1: float32 [2, 256, 1024], P('section'), may hold values from -0.02734375 to 0.02734375
- momentum_fc2: float32 [2, 1024, 256], P('section'), may hold values from -0.02734375 to 0.02734375
- average_vectors: float32 [2, 3328], P('section'), as said below
- average_kernels: float32 [2, 9, 256], P('section'), may hold values from -2 to 2
- average_qkv: float32 [2, 256, 768], P('section'), may hold values from -0.375 to 0.375
- average_proj: float32 [2, 256, 256], P('section'), may hold values from -0.75 to 0.75
- average_fc1: float32 [2, 256, 1024], P('section'), may hold values from -0.375 to 0.375
- average_fc2: float32 [2, 1024, 256], P('section'), may hold values from -0.1875 to 0.1875
Outputs:
- block_outputs: float32 [2, 9728, 256], P('section', 'dp')
- input_grads: float32 [2, 9728, 256], P('section', 'dp')
- grad_vectors: float32 [2, 3328], P('section')
- grad_kernels: float32 [2, 9, 256], P('section')
- grad_qkv: float32 [2, 256, 768], P('section')
- grad_proj: float32 [2, 256, 256], P('section')
- grad_fc1: float32 [2, 256, 1024], P('section')
- grad_fc2: float32 [2, 1024, 256], P('section')
- grad_norm: float32 [], replicated
- new_momentum_vectors: float32 [2, 3328], P('section')
- new_momentum_kernels: float32 [2, 9, 256], P('section')
- new_momentum_qkv: float32 [2, 256, 768], P('section')
- new_momentum_proj: float32 [2, 256, 256], P('section')
- new_momentum_fc1: float32 [2, 256, 1024], P('section')
- new_momentum_fc2: float32 [2, 1024, 256], P('section')
- new_vectors: float32 [2, 3328], P('section')
- new_kernels: float32 [2, 9, 256], P('section')
- new_w_qkv: float32 [2, 256, 768], P('section')
- new_w_proj: float32 [2, 256, 256], P('section')
- new_w_fc1: float32 [2, 256, 1024], P('section')
- new_w_fc2: float32 [2, 1024, 256], P('section')
- new_average_vectors: float32 [2, 3328], P('section')
- new_average_kernels: float32 [2, 9, 256], P('section')
- new_average_qkv: float32 [2, 256, 768], P('section')
- new_average_proj: float32 [2, 256, 256], P('section')
- new_average_fc1: float32 [2, 256, 1024], P('section')
- new_average_fc2: float32 [2, 1024, 256], P('section')
- copy_qkv: bfloat16 [2, 256, 768], P('section')
- copy_proj: bfloat16 [2, 256, 256], P('section')
- copy_fc1: bfloat16 [2, 256, 1024], P('section')
- copy_fc2: bfloat16 [2, 1024, 256], P('section')
The draws below stay inside these ranges and needn't reach their ends.
Inputs may be any that keep to these rules, and one draw needn't show every extreme that they name: `vectors`: gains are positive. `average_vectors`: gains are positive.
All inputs are finite; a program needn't handle non-finite values.
Results may differ from the reference program's by a relative error of at most 0.022.
The reference program's roundings to bfloat16 on the way count: a program that leaves them out, or rounds other values in their place, can miss the bound.
Values may be sent and summed in bfloat16 or wider, within the bound.
No kernel may reach another device: no remote copies, remote signals or barrier semaphores. Data moves between devices by JAX's collectives and lax.ppermute only.
A program may use at most 128 MiB of HBM per device.

```python
import jax
import jax.numpy as jnp
from jax import lax

D = 256
HEADS = 8
FF = 1024
BIG_SIDE = 14
SMALL_SIDE = 6
BIG_MB = 1
SMALL_MB = 3
STEP = 8
MB_TOK = 304
TOKENS = 9728
VEC = 3328
NPARAM = 1584128


def vector_draw(key):
    first_key, second_key = jax.random.split(key)
    segment_rise = jnp.arange(2, dtype=jnp.float32)[:, None]
    gains = (1.0 + 0.7 * segment_rise) * jax.random.uniform(first_key, (2, 2 * D), jnp.float32, 0.8, 1.2)
    biases = 0.2 * jax.random.normal(second_key, (2, 7 * D + FF), jnp.float32)
    return jnp.concatenate([gains, biases], axis=1)


def draw_vectors(key, part):
    return vector_draw(jax.random.fold_in(key, 11))


def draw_average_vectors(key, part):
    return vector_draw(jax.random.fold_in(key, 23))


def level_of(rng, extent, pieces, smallest, top_value):
    factor_of, own = 1.0, jax.random.fold_in(rng, 6)
    for axis_at, parts in pieces:
        heights = jnp.exp(jax.random.uniform(jax.random.fold_in(own, axis_at), (parts,), jnp.float32, smallest / len(pieces), top_value / len(pieces)))
        factor_of = factor_of * jnp.repeat(heights, extent[axis_at] // parts).reshape([-1 if axis == axis_at else 1 for axis in range(len(extent))])
    return factor_of


def normal_values(rng, shape, scale, bound, cuts=(), kind=jnp.bfloat16):
    level = level_of(rng, shape, cuts, -0.22, 0.18) if cuts else 1.0
    values = jax.random.normal(rng, shape, jnp.float32) * scale * level
    return jnp.minimum(jnp.maximum(values, -bound), bound).astype(kind)


def setup_inputs(seed: int = 0) -> dict:
    streams_of = jax.random.split(jax.random.key(seed), 21)
    inputs = normal_values(streams_of[0], (TOKENS, D), 1.0, 6.0, ((0, 16),))
    cotangent = normal_values(streams_of[1], (TOKENS, D), 1.0, 6.0, ((0, 16),))
    vectors = draw_vectors(jax.random.fold_in(streams_of[20], 71), 0)
    kernels = normal_values(streams_of[3], (2, 9, D), 9 ** -0.5, 2.0, ((0, 2),), jnp.float32)
    w_qkv = normal_values(streams_of[4], (2, D, 3 * D), D ** -0.5, 0.375, ((0, 2),), jnp.float32)
    w_proj = normal_values(streams_of[5], (2, D, D), (D // 4) ** -0.5, 0.75, ((0, 2),), jnp.float32)
    w_fc1 = normal_values(streams_of[6], (2, D, FF), D ** -0.5, 0.375, ((0, 2),), jnp.float32)
    w_fc2 = normal_values(streams_of[7], (2, FF, D), FF ** -0.5, 0.1875, ((0, 2),), jnp.float32)
    momentum_vectors = normal_values(streams_of[8], (2, VEC), (20.0 * NPARAM ** -0.5), 0.09375, ((0, 2),), jnp.float32)
    momentum_kernels = normal_values(streams_of[9], (2, 9, D), (10.0 * NPARAM ** -0.5), 0.046875, ((0, 2),), jnp.float32)
    momentum_qkv = normal_values(streams_of[10], (2, D, 3 * D), (5.5 * NPARAM ** -0.5), 0.02734375, ((0, 2),), jnp.float32)
    momentum_proj = normal_values(streams_of[11], (2, D, D), (5.5 * NPARAM ** -0.5), 0.02734375, ((0, 2),), jnp.float32)
    momentum_fc1 = normal_values(streams_of[12], (2, D, FF), (5.5 * NPARAM ** -0.5), 0.02734375, ((0, 2),), jnp.float32)
    momentum_fc2 = normal_values(streams_of[13], (2, FF, D), (5.5 * NPARAM ** -0.5), 0.02734375, ((0, 2),), jnp.float32)
    average_vectors = draw_average_vectors(jax.random.fold_in(streams_of[20], 71), 0)
    average_kernels = normal_values(streams_of[15], (2, 9, D), 9 ** -0.5, 2.0, ((0, 2),), jnp.float32)
    average_qkv = normal_values(streams_of[16], (2, D, 3 * D), D ** -0.5, 0.375, ((0, 2),), jnp.float32)
    average_proj = normal_values(streams_of[17], (2, D, D), (D // 4) ** -0.5, 0.75, ((0, 2),), jnp.float32)
    average_fc1 = normal_values(streams_of[18], (2, D, FF), D ** -0.5, 0.375, ((0, 2),), jnp.float32)
    average_fc2 = normal_values(streams_of[19], (2, FF, D), FF ** -0.5, 0.1875, ((0, 2),), jnp.float32)
    return {"inputs": inputs, "cotangent": cotangent, "vectors": vectors, "kernels": kernels, "w_qkv": w_qkv, "w_proj": w_proj, "w_fc1": w_fc1, "w_fc2": w_fc2, "momentum_vectors": momentum_vectors, "momentum_kernels": momentum_kernels, "momentum_qkv": momentum_qkv, "momentum_proj": momentum_proj, "momentum_fc1": momentum_fc1, "momentum_fc2": momentum_fc2, "average_vectors": average_vectors, "average_kernels": average_kernels, "average_qkv": average_qkv, "average_proj": average_proj, "average_fc1": average_fc1, "average_fc2": average_fc2}


@jax.custom_vjp
def low(v):
    return lax.optimization_barrier(v.astype(jnp.bfloat16)).astype(jnp.float32)

@jax.custom_vjp
def low_back(v):
    return v

def low_keep(v):
    return (low(v), None)

def low_pass(kept, grad):
    return (grad,)

def back_keep(v):
    return (v, None)

def back_low(kept, grad):
    return (low(grad),)
low.defvjp(low_keep, low_pass)
low_back.defvjp(back_keep, back_low)
HIGHEST = lax.Precision.HIGHEST
CLIP_LIMIT = 5.0
LEARN_RATE = 4.0
MOMENTUM_DECAY = 0.9
WEIGHT_DECAY = 5e-05
NORM_EPS = 1e-05

def layer_norm(values, gain, offset):
    centre = values - lax.optimization_barrier(jnp.mean(values, axis=-1, keepdims=True))
    spread = lax.optimization_barrier(jnp.mean(centre * centre, axis=-1, keepdims=True))
    return centre * lax.rsqrt(spread + NORM_EPS) * gain + offset

def to_stripes(tokens, side, count):
    width = tokens.shape[-1]
    half = width // 2
    head_size = width // HEADS
    image = tokens.reshape(count, side, side, width)
    across = image[..., :half].reshape(count * (side // 2), 2 * side, HEADS // 2, head_size)
    along = image[..., half:].reshape(count, side, side // 2, 2, HEADS // 2, head_size)
    along = along.transpose(0, 2, 1, 3, 4, 5).reshape(count * (side // 2), 2 * side, HEADS // 2, head_size)
    return (across, along)

def from_stripes(across, along, side, count):
    first_half = across.reshape(count, side, side, -1)
    second_half = along.reshape(count, side // 2, side, 2, -1).transpose(0, 2, 1, 3, 4).reshape(count, side, side, -1)
    return jnp.concatenate([first_half, second_half], axis=-1).reshape(count * side * side, -1)

def lepe_terms(values, kernel, bias, side, count):
    width = values.shape[-1]
    half = width // 2
    image = values.reshape(count, side, side, width)
    padded = jnp.pad(image, ((0, 0), (1, 1), (1, 1), (0, 0)))
    rows_at = jnp.arange(side)[:, None]
    cols_at = jnp.arange(side)[None, :]
    result = jnp.zeros_like(image)
    for row_step in (-1, 0, 1):
        for col_step in (-1, 0, 1):
            inside = (rows_at + row_step >= 0) & (rows_at + row_step < side) & (cols_at + col_step >= 0) & (cols_at + col_step < side)
            same_row = (rows_at + row_step) // 2 == rows_at // 2
            same_col = (cols_at + col_step) // 2 == cols_at // 2
            mask_across = jnp.broadcast_to((inside & same_row)[:, :, None], (side, side, half))
            mask_along = jnp.broadcast_to((inside & same_col)[:, :, None], (side, side, width - half))
            masking = jnp.concatenate([mask_across, mask_along], axis=-1).astype(values.dtype)
            shifted = padded[:, 1 + row_step:1 + row_step + side, 1 + col_step:1 + col_step + side, :]
            result = result + shifted * masking * kernel[(row_step + 1) * 3 + col_step + 1]
    return result.reshape(count * side * side, width) + bias

def stripe_attention(query, keys, values):
    scale = query.shape[-1] ** (-0.5)
    scores = low_back(jnp.einsum('wqhd,wkhd->whqk', query, keys, precision=HIGHEST) * scale)
    weights = jax.nn.softmax(scores, axis=-1)
    return jnp.einsum('whqk,wkhd->wqhd', low(weights), values, precision=HIGHEST)

def mixing(query, keys, values, kernel, bias, side, count):
    query_parts = to_stripes(query, side, count)
    key_parts = to_stripes(keys, side, count)
    value_parts = to_stripes(values, side, count)
    across = stripe_attention(query_parts[0], key_parts[0], value_parts[0])
    along = stripe_attention(query_parts[1], key_parts[1], value_parts[1])
    return from_stripes(across, along, side, count) + lepe_terms(values, kernel, bias, side, count)

def block(inputs, vector, kernel, matrices):
    w_qkv_low, w_proj_low, w_fc1_low, w_fc2_low = matrices
    normed = low(layer_norm(inputs, vector[0:D], vector[2 * D:3 * D]))
    projected = jnp.dot(normed, w_qkv_low, precision=HIGHEST)
    query = low(low_back(projected[:, :D] + vector[4 * D:5 * D]))
    keys = low(low_back(projected[:, D:2 * D]))
    values = low(low_back(projected[:, 2 * D:] + vector[5 * D:6 * D]))
    split = BIG_MB * BIG_SIDE * BIG_SIDE
    large = mixing(query[:split], keys[:split], values[:split], kernel, vector[7 * D:8 * D], BIG_SIDE, BIG_MB)
    small = mixing(query[split:], keys[split:], values[split:], kernel, vector[7 * D:8 * D], SMALL_SIDE, SMALL_MB)
    mixed = low(low_back(jnp.concatenate([large, small], axis=0)))
    middle = inputs + low_back(jnp.dot(mixed, w_proj_low, precision=HIGHEST) + vector[6 * D:7 * D])
    normed_two = low(layer_norm(middle, vector[D:2 * D], vector[3 * D:4 * D]))
    hidden = low_back(jnp.dot(normed_two, w_fc1_low, precision=HIGHEST) + vector[9 * D:])
    activated = low(jax.nn.gelu(hidden, approximate=False))
    return middle + low_back(jnp.dot(activated, w_fc2_low, precision=HIGHEST) + vector[8 * D:9 * D])

def forward(inputs, stacked, probe):
    groups = inputs.reshape(-1, MB_TOK, D)

    def run_segment(segment, feed):
        vector = stacked[0][segment]
        kernel = stacked[1][segment]
        matrices = tuple((low(weight[segment]) for weight in stacked[2:]))

        def one_group(rows):
            return block(rows, vector, kernel, matrices)
        return lax.map(jax.checkpoint(one_group), feed)
    first_out = run_segment(0, groups)
    second_in = low(low_back(first_out)) + probe.reshape(groups.shape)
    second_out = run_segment(1, second_in)
    return (first_out.reshape(-1, D), second_out.reshape(-1, D))

def reference(inputs, cotangent, vectors, kernels, w_qkv, w_proj, w_fc1, w_fc2, momentum_vectors, momentum_kernels, momentum_qkv, momentum_proj, momentum_fc1, momentum_fc2, average_vectors, average_kernels, average_qkv, average_proj, average_fc1, average_fc2):
    start = inputs.astype(jnp.float32)
    stacked = (vectors, kernels, w_qkv, w_proj, w_fc1, w_fc2)
    probe = jnp.zeros_like(start)
    outputs, pull = jax.vjp(forward, start, stacked, probe)
    start_grad, grads, probe_grad = pull((jnp.zeros_like(outputs[0]), cotangent.astype(jnp.float32)))
    total = sum((jnp.sum(entry * entry) for entry in grads))
    norm_value = jnp.sqrt(total)
    factor = jnp.minimum(1.0, CLIP_LIMIT / (norm_value + 1e-06))
    ema_decay = min(0.9999, (1.0 + STEP) / (10.0 + STEP))
    moments_in = (momentum_vectors, momentum_kernels, momentum_qkv, momentum_proj, momentum_fc1, momentum_fc2)
    averages_in = (average_vectors, average_kernels, average_qkv, average_proj, average_fc1, average_fc2)
    clipped_list = []
    moment_list = []
    weight_list = []
    average_list = []
    for entry, weight, moment, average in zip(grads, stacked, moments_in, averages_in):
        clipped = entry * factor
        direction = clipped + WEIGHT_DECAY * weight
        moment_new = MOMENTUM_DECAY * moment + direction
        weight_new = weight - LEARN_RATE * (direction + MOMENTUM_DECAY * moment_new)
        average_new = ema_decay * average + (1.0 - ema_decay) * weight_new
        clipped_list.append(clipped)
        moment_list.append(moment_new)
        weight_list.append(weight_new)
        average_list.append(average_new)
    return (jnp.stack([outputs[0], outputs[1]]), jnp.stack([start_grad, probe_grad]), clipped_list[0], clipped_list[1], clipped_list[2], clipped_list[3], clipped_list[4], clipped_list[5], norm_value, moment_list[0], moment_list[1], moment_list[2], moment_list[3], moment_list[4], moment_list[5], weight_list[0], weight_list[1], weight_list[2], weight_list[3], weight_list[4], weight_list[5], average_list[0], average_list[1], average_list[2], average_list[3], average_list[4], average_list[5], weight_list[2].astype(jnp.bfloat16), weight_list[3].astype(jnp.bfloat16), weight_list[4].astype(jnp.bfloat16), weight_list[5].astype(jnp.bfloat16))
```

```python
import jax
import jax.numpy as jnp
import numpy as np
from jax import lax
from jax.experimental import pallas as pl
from jax.experimental.pallas import tpu as pltpu
from jax.sharding import PartitionSpec as P

D = 256
HALF = 128
HEADS = 8
HEAD = 32
FF = 1024
BIG_SIDE = 14
SMALL_SIDE = 6
BIG_MB = 1
SMALL_MB = 3
STEP = 8
MB_TOK = 304
VEC = 3328

NORM_EPS = 1e-05
CLIP_LIMIT = 5.0
LEARN_RATE = 4.0
MOMENTUM_DECAY = 0.9
WEIGHT_DECAY = 5e-05

F32 = jnp.float32
BF16 = jnp.bfloat16

GROUP = 128
GROUPS = ((0, 112), (112, 84), (196, 108))
KINDS = (0, 0, 1)
NGROUP = len(GROUPS)
ATT = NGROUP * GROUP
SCALE = HEAD ** -0.5
LOG2E = 1.4426950408889634
EXP_SCALE = SCALE * LOG2E
OFF = -1e30
ROWS = ((0, 80), (80, 80), (160, 80), (240, 64))
GRAD_ROWS = 3328
SMALL_ROW = 3072


def placement_tables():
    plain = np.zeros((ATT, MB_TOK), np.float32)
    turned = np.zeros((ATT, MB_TOK), np.float32)
    transposed = []
    base = 0
    for side, count in ((BIG_SIDE, BIG_MB), (SMALL_SIDE, SMALL_MB)):
        for _ in range(count):
            for row in range(side):
                for col in range(side):
                    transposed.append(base + col * side + row)
            base += side * side
    for group, (first, size) in enumerate(GROUPS):
        for at in range(size):
            plain[group * GROUP + at, first + at] = 1.0
            turned[group * GROUP + at, transposed[first + at]] = 1.0
    return plain, turned


def stripe_tables():
    shifts = np.zeros((2, 5 * GROUP, GROUP), np.float32)
    fence = np.full((2, GROUP, GROUP), OFF, np.float32)
    lower = np.zeros((2, GROUP, HALF), np.float32)
    for kind, (side, sizes) in enumerate(((BIG_SIDE, 112), (SMALL_SIDE, 108))):
        stripe = 2 * side
        for at in range(GROUP):
            own = at // stripe
            fence[kind, at, own * stripe : (own + 1) * stripe] = 0.0
        for at in range(sizes):
            own, inner = divmod(at, stripe)
            row, col = divmod(inner, side)
            lower[kind, at, :] = float(row)
            moves = ((row, col - 1), (row, col + 1), (1 - row, col - 1), (1 - row, col), (1 - row, col + 1))
            for move, (to_row, to_col) in enumerate(moves):
                if 0 <= to_col < side:
                    shifts[kind, move * GROUP + at, own * stripe + to_row * side + to_col] = 1.0
    return shifts, fence, lower


def dot(a, b):
    return jnp.dot(a, b, preferred_element_type=F32)


def dot_nt(a, b):
    return lax.dot_general(a, b, (((1,), (1,)), ((), ())), preferred_element_type=F32)


def dot_tn(a, b):
    return lax.dot_general(a, b, (((0,), (0,)), ((), ())), preferred_element_type=F32)


def head_masks():
    lane = lax.broadcasted_iota(jnp.int32, (1, HALF), 1) // HEAD
    return [(lane == head).astype(BF16) for head in range(HEADS // 2)]


def stacked_heads(rows, masks):
    return jnp.concatenate([rows * mask for mask in masks], axis=0)


def picked_heads(product):
    return jnp.concatenate(
        [
            product[HEAD * head : HEAD * (head + 1), GROUP * head : GROUP * (head + 1)]
            for head in range(HEADS // 2)
        ],
        axis=0,
    )


def turned_taps(taps):
    first = [taps[index : index + 1, :HALF] for index in range(9)]
    second = [taps[3 * (index % 3) + index // 3 :, HALF:][:1] for index in range(9)]
    return [jnp.concatenate([a, b], axis=1) for a, b in zip(first, second)]


def norm_forward(x, gain, offset):
    centre = x - jnp.mean(x, axis=-1, keepdims=True)
    spread = jnp.mean(centre * centre, axis=-1, keepdims=True)
    scale = lax.rsqrt(spread + NORM_EPS)
    hat = centre * scale
    return hat, scale, hat * gain + offset


def norm_backward(grad, hat, scale, gain):
    inner = grad * gain
    mean_inner = jnp.mean(inner, axis=-1, keepdims=True)
    mean_cross = jnp.mean(inner * hat, axis=-1, keepdims=True)
    return scale * (inner - mean_inner - hat * mean_cross)


def column_sum(x):
    return jnp.sum(x.astype(F32), axis=0, keepdims=True)


def vec_at(vec, index, width=1):
    return vec[:, index * D : (index + width) * D]


def forward_block(x_ref, out_ref, vec, taps, w, saved, tables, work):
    wq, wp, w1, w2 = w
    (hat1, scale1, normed, qkv, probs, mixed, hat2, scale2, normed2, slope, activ) = saved
    plain, turned, plain_t, turned_t, shifts, fence, lower = tables
    normed_nat, mixed_att, middle, hidden = work
    for start, size in ROWS:
        rows = pl.ds(start, size)
        hat, scale, y = norm_forward(x_ref[rows, :].astype(F32), vec_at(vec, 0), vec_at(vec, 2))
        hat1[rows, :] = hat
        scale1[rows, :] = jnp.broadcast_to(scale, (size, HALF))
        normed_nat[rows, :] = y.astype(BF16)
    base = normed_nat[...]
    biases = (vec_at(vec, 4), None, vec_at(vec, 5))
    for half, table in enumerate((plain, turned)):
        placed = dot(table[...], base).astype(BF16)
        normed[half] = placed
        lanes = slice(half * HALF, (half + 1) * HALF)
        for part in range(3):
            got = dot(placed, wq[:, part * D + half * HALF : part * D + (half + 1) * HALF])
            if biases[part] is not None:
                got = got + biases[part][:, lanes]
            qkv[part, :, lanes] = got.astype(BF16)
    masks = head_masks()
    taps9 = turned_taps(taps)
    bias = vec_at(vec, 7)
    for group in range(NGROUP):
        kind = KINDS[group]
        rows = pl.ds(group * GROUP, GROUP)
        v = qkv[2, rows, :]
        moved = dot(shifts[kind], v)
        low_row = lower[kind] > 0.5
        low_row = jnp.concatenate([low_row, low_row], axis=1)
        lepe = bias + taps9[4] * v.astype(F32)
        lepe = lepe + taps9[3] * moved[0:GROUP] + taps9[5] * moved[GROUP : 2 * GROUP]
        for step in range(3):
            tap = jnp.where(low_row, taps9[step], taps9[6 + step])
            lepe = lepe + tap * moved[(2 + step) * GROUP : (3 + step) * GROUP]
        fenced = fence[kind]
        for half in range(2):
            lanes = slice(half * HALF, (half + 1) * HALF)
            q_stack = stacked_heads(qkv[0, rows, lanes], masks)
            scores = dot_nt(qkv[1, rows, lanes], q_stack)
            low = []
            for head in range(HEADS // 2):
                s = scores[:, head * GROUP : (head + 1) * GROUP] + fenced
                p = jnp.exp2((s - jnp.max(s, axis=0, keepdims=True)) * EXP_SCALE)
                p = p * (1.0 / jnp.sum(p, axis=0, keepdims=True))
                probs[group * 2 + half, :, head * GROUP : (head + 1) * GROUP] = p
                low.append(p.astype(BF16))
            attended = picked_heads(dot(v[:, lanes].T, jnp.concatenate(low, axis=1))).T
            mixed_att[rows, lanes] = (attended + lepe[:, lanes]).astype(BF16)
    mixed[:, :HALF] = dot(plain_t[...], mixed_att[:, :HALF]).astype(BF16)
    mixed[:, HALF:] = dot(turned_t[...], mixed_att[:, HALF:]).astype(BF16)
    middle[...] = dot(mixed[...], wp[...])
    for start, size in ROWS:
        rows = pl.ds(start, size)
        mid = x_ref[rows, :].astype(F32) + middle[rows, :] + vec_at(vec, 6)
        middle[rows, :] = mid
        hat, scale, y = norm_forward(mid, vec_at(vec, 1), vec_at(vec, 3))
        hat2[rows, :] = hat
        scale2[rows, :] = jnp.broadcast_to(scale, (size, HALF))
        normed2[rows, :] = y.astype(BF16)
    hidden[...] = dot(normed2[...], w1[...])
    for start, size in ROWS:
        rows = pl.ds(start, size)
        for part in range(4):
            cols = slice(part * D, (part + 1) * D)
            h = hidden[rows, cols] + vec_at(vec, 9 + part)
            cdf = 0.5 * (1.0 + lax.erf(h * 0.7071067811865476))
            pdf = 0.3989422804014327 * jnp.exp(-0.5 * h * h)
            activ[rows, cols] = (h * cdf).astype(BF16)
            slope[rows, cols] = cdf + h * pdf
    out_ref[...] = dot(activ[...], w2[...])
    for start, size in ROWS:
        rows = pl.ds(start, size)
        out_ref[rows, :] = out_ref[rows, :] + middle[rows, :] + vec_at(vec, 8)


def backward_block(up_ref, grad_ref, vec, taps, w, saved, tables, work, gbuf, small):
    wq, wp, w1, w2 = w
    (hat1, scale1, normed, qkv, probs, mixed, hat2, scale2, normed2, slope, activ) = saved
    plain, turned, plain_t, turned_t, shifts, fence, lower = tables
    branch, gact, ghid, gmid, gmix, dqkv, dnat, gnorm = work
    branch[...] = up_ref[...].astype(BF16)
    gbuf[2048:3072, :] = dot_tn(activ[...], branch[...]).astype(BF16)
    sums = column_sum(branch[...])
    small[8:9, :] = sums
    gact[...] = dot_nt(branch[...], w2[...])
    parts = [jnp.zeros((1, D), F32) for _ in range(4)]
    for start, size in ROWS:
        rows = pl.ds(start, size)
        for part in range(4):
            cols = slice(part * D, (part + 1) * D)
            low = (gact[rows, cols] * slope[rows, cols]).astype(BF16)
            ghid[rows, cols] = low
            parts[part] = parts[part] + column_sum(low)
    for part in range(4):
        small[9 + part : 10 + part, :] = parts[part]
    for part in range(4):
        gbuf[1024 + part * D : 1024 + (part + 1) * D, :] = dot_tn(
            normed2[...], ghid[:, part * D : (part + 1) * D]
        ).astype(BF16)
    gnorm[...] = dot_nt(ghid[...], w1[...])
    gains, offsets, outs = (jnp.zeros((1, D), F32) for _ in range(3))
    for start, size in ROWS:
        rows = pl.ds(start, size)
        g = gnorm[rows, :]
        hat = hat2[rows, :]
        scale = scale2[rows, :]
        gains = gains + column_sum(g * hat)
        offsets = offsets + column_sum(g)
        full = jnp.concatenate([scale, scale], axis=1)
        total = up_ref[rows, :].astype(F32) + norm_backward(g, hat, full, vec_at(vec, 1))
        gmid[rows, :] = total
        low = total.astype(BF16)
        branch[rows, :] = low
        outs = outs + column_sum(low)
    small[1:2, :] = gains
    small[3:4, :] = offsets
    small[6:7, :] = outs
    gbuf[768:1024, :] = dot_tn(mixed[...], branch[...]).astype(BF16)
    low = dot_nt(branch[...], wp[...]).astype(BF16)
    gmix[0:MB_TOK, :] = low
    small[7:8, :] = column_sum(low)
    place_h = dot(plain[...], low[:, :HALF]).astype(BF16)
    place_v = dot(turned[...], low[:, HALF:]).astype(BF16)
    gmix[:, :HALF] = place_h
    gmix[:, HALF:] = place_v
    masks = head_masks()
    taps9 = turned_taps(taps)
    tap_sums = [jnp.zeros((1, D), F32) for _ in range(9)]
    for group in range(NGROUP):
        kind = KINDS[group]
        rows = pl.ds(group * GROUP, GROUP)
        g_low = gmix[rows, :]
        moved = dot(shifts[kind], g_low)
        low_row = lower[kind] > 0.5
        low_row = jnp.concatenate([low_row, low_row], axis=1)
        v32 = qkv[2, rows, :].astype(F32)
        g32 = g_low.astype(F32)
        tap_sums[4] = tap_sums[4] + column_sum(v32 * g32)
        left, right = moved[0:GROUP], moved[GROUP : 2 * GROUP]
        lepe = taps9[4] * g32 + taps9[3] * right + taps9[5] * left
        tap_sums[3] = tap_sums[3] + column_sum(v32 * right)
        tap_sums[5] = tap_sums[5] + column_sum(v32 * left)
        for step in range(3):
            at = moved[(4 - step) * GROUP : (5 - step) * GROUP]
            lepe = lepe + jnp.where(low_row, taps9[6 + step], taps9[step]) * at
            product = v32 * at
            tap_sums[6 + step] = tap_sums[6 + step] + column_sum(jnp.where(low_row, product, 0.0))
            tap_sums[step] = tap_sums[step] + column_sum(jnp.where(low_row, 0.0, product))
        for half in range(2):
            lanes = slice(half * HALF, (half + 1) * HALF)
            unit = group * 2 + half
            g_stack = stacked_heads(gmix[rows, lanes], masks)
            q_stack = stacked_heads(qkv[0, rows, lanes], masks)
            k = qkv[1, rows, lanes]
            gprobs = dot_nt(qkv[2, rows, lanes], g_stack)
            low_p, low_s = [], []
            for head in range(HEADS // 2):
                cols = slice(head * GROUP, (head + 1) * GROUP)
                p = probs[unit, :, cols]
                gp = gprobs[:, cols]
                down = jnp.sum(gp * p, axis=0, keepdims=True)
                low_s.append((p * (gp - down)).astype(BF16))
                low_p.append(p.astype(BF16))
            low_p = jnp.concatenate(low_p, axis=1)
            low_s = jnp.concatenate(low_s, axis=1)
            grad_v = dot(low_p, g_stack) + lepe[:, lanes]
            grad_k = dot(low_s, q_stack) * SCALE
            grad_q = picked_heads(dot(k.T, low_s)).T * SCALE
            dqkv[half, rows, 0:HALF] = grad_q.astype(BF16)
            dqkv[half, rows, HALF:D] = grad_k.astype(BF16)
            dqkv[half, rows, D : 3 * HALF] = grad_v.astype(BF16)
    for index in range(9):
        tap = index
        turned_index = 3 * (index % 3) + index // 3
        small[13 + index : 14 + index, :] = jnp.concatenate(
            [tap_sums[tap][:, :HALF], tap_sums[turned_index][:, HALF:]], axis=1
        )
    for half, table_t in enumerate((plain_t, turned_t)):
        lanes = slice(half * HALF, (half + 1) * HALF)
        both = dqkv[half]
        small[4:5, lanes] = column_sum(both[:, 0:HALF])
        small[5:6, lanes] = column_sum(both[:, D : 3 * HALF])
        grads = dot_tn(normed[half], both)
        for part in range(3):
            gbuf[part * D : (part + 1) * D, lanes] = grads[:, part * HALF : (part + 1) * HALF].astype(BF16)
        natural = dot(table_t[...], both).astype(BF16)
        for part in range(3):
            dnat[:, part * D + half * HALF : part * D + (half + 1) * HALF] = natural[
                :, part * HALF : (part + 1) * HALF
            ]
    gnorm[...] = dot_nt(dnat[...], wq[...])
    gains, offsets = (jnp.zeros((1, D), F32) for _ in range(2))
    for start, size in ROWS:
        rows = pl.ds(start, size)
        g = gnorm[rows, :]
        hat = hat1[rows, :]
        scale = scale1[rows, :]
        gains = gains + column_sum(g * hat)
        offsets = offsets + column_sum(g)
        full = jnp.concatenate([scale, scale], axis=1)
        grad_ref[rows, :] = gmid[rows, :] + norm_backward(g, hat, full, vec_at(vec, 0))
    small[0:1, :] = gains
    small[2:3, :] = offsets
    gbuf[SMALL_ROW : SMALL_ROW + 32, :] = small[...].astype(BF16)


SAVED = [
    ((MB_TOK, D), F32),
    ((MB_TOK, HALF), F32),
    ((2, ATT, D), BF16),
    ((3, ATT, D), BF16),
    ((2 * NGROUP, GROUP, 4 * GROUP), F32),
    ((MB_TOK, D), BF16),
    ((MB_TOK, D), F32),
    ((MB_TOK, HALF), F32),
    ((MB_TOK, D), BF16),
    ((MB_TOK, FF), F32),
    ((MB_TOK, FF), BF16),
]
FORWARD_WORK = [((MB_TOK, D), BF16), ((ATT, D), BF16), ((MB_TOK, D), F32), ((MB_TOK, FF), F32)]
BACKWARD_WORK = [
    ((MB_TOK, D), BF16),
    ((MB_TOK, FF), F32),
    ((MB_TOK, FF), BF16),
    ((MB_TOK, D), F32),
    ((ATT, D), BF16),
    ((2, ATT, 3 * HALF), BF16),
    ((MB_TOK, 3 * D), BF16),
    ((MB_TOK, D), F32),
]


def section_step(
    sec_ref, x_ref, c_ref, vec_own, vec_other, ker_own, ker_other, wide_own, wide_other, deep_own, deep_other, *refs
):
    tables, refs = refs[:7], refs[7:]
    (outs, grads, gsum), refs = refs[:3], refs[3:]
    count = len(SAVED)
    kept, refs = (refs[:count], refs[count : 2 * count]), refs[2 * count :]
    forward_work, refs = refs[: len(FORWARD_WORK)], refs[len(FORWARD_WORK) :]
    backward_work, refs = refs[: len(BACKWARD_WORK)], refs[len(BACKWARD_WORK) :]
    feed, small, wide, deep, sems = refs
    sec = sec_ref[0]
    copies = [
        pltpu.make_async_copy(wide_own, wide.at[sec], sems.at[0]),
        pltpu.make_async_copy(wide_other, wide.at[1 - sec], sems.at[1]),
        pltpu.make_async_copy(deep_own, deep.at[sec], sems.at[2]),
        pltpu.make_async_copy(deep_other, deep.at[1 - sec], sems.at[3]),
    ]
    for copy in copies:
        copy.start()
    small[...] = jnp.zeros_like(small)
    gsum[:, SMALL_ROW:, :] = jnp.zeros((2, GRAD_ROWS - SMALL_ROW, D), BF16)
    first = sec == 0
    vecs = (
        jnp.where(first, vec_own[...], vec_other[...]),
        jnp.where(first, vec_other[...], vec_own[...]),
    )
    taps = (
        jnp.where(first, ker_own[...], ker_other[...]),
        jnp.where(first, ker_other[...], ker_own[...]),
    )
    weights = [
        (wide.at[b, :, 0:768], wide.at[b, :, 768:1024], wide.at[b, :, 1024:2048], deep.at[b])
        for b in range(2)
    ]
    at = pl.multiple_of(sec * MB_TOK, 16)
    for copy in copies:
        copy.wait()
    slot = (sec, 1 - sec)
    x_own, c_own = x_ref.at[pl.ds(at, MB_TOK)], c_ref.at[pl.ds(at, MB_TOK)]
    out_refs = [outs.at[slot[b]] for b in range(2)]
    grad_refs = [grads.at[slot[b]] for b in range(2)]
    sum_refs = [gsum.at[slot[b]] for b in range(2)]
    forward_block(x_own, out_refs[0], vecs[0], taps[0], weights[0], kept[0], tables, forward_work)
    feed[...] = out_refs[0][...].astype(BF16)
    forward_block(feed, out_refs[1], vecs[1], taps[1], weights[1], kept[1], tables, forward_work)
    backward_block(
        c_own, grad_refs[1], vecs[1], taps[1], weights[1], kept[1], tables, backward_work, sum_refs[1], small
    )
    feed[...] = grad_refs[1][...].astype(BF16)
    backward_block(
        feed, grad_refs[0], vecs[0], taps[0], weights[0], kept[0], tables, backward_work, sum_refs[0], small
    )


def run_blocks(sec, x, c, vec_own, vec_other, ker_own, ker_other, wide_own, wide_other, deep_own, deep_other):
    plain, turned = placement_tables()
    shifts, fence, lower = stripe_tables()
    tables = (
        jnp.asarray(plain, BF16),
        jnp.asarray(turned, BF16),
        jnp.asarray(plain.T, BF16),
        jnp.asarray(turned.T, BF16),
        jnp.asarray(shifts, BF16),
        jnp.asarray(fence, F32),
        jnp.asarray(lower, F32),
    )
    vmem = pl.BlockSpec(memory_space=pltpu.VMEM)
    hbm = pl.BlockSpec(memory_space=pl.ANY)
    smem = pl.BlockSpec(memory_space=pltpu.SMEM)
    scratch = SAVED + SAVED + FORWARD_WORK + BACKWARD_WORK
    scratch = scratch + [((MB_TOK, D), BF16), ((32, D), F32), ((2, D, 2048), BF16), ((2, FF, D), BF16)]
    return pl.pallas_call(
        section_step,
        out_shape=[
            jax.ShapeDtypeStruct((2, MB_TOK, D), F32),
            jax.ShapeDtypeStruct((2, MB_TOK, D), F32),
            jax.ShapeDtypeStruct((2, GRAD_ROWS, D), BF16),
        ],
        in_specs=[smem] + [vmem] * 6 + [hbm] * 4 + [vmem] * 7,
        out_specs=[vmem] * 3,
        scratch_shapes=[pltpu.VMEM(shape, kind) for shape, kind in scratch] + [pltpu.SemaphoreType.DMA((4,))],
        compiler_params=pltpu.CompilerParams(vmem_limit_bytes=50 << 20),
        name="blocks",
    )(sec, x, c, vec_own, vec_other, ker_own, ker_other, wide_own, wide_other, deep_own, deep_other, *tables)


def square_sum(a_ref, b_ref, c_ref, out_ref):
    total = jnp.zeros((8, D), F32)
    for ref in (a_ref, b_ref, c_ref):
        step = 64
        for start in range(0, ref.shape[0], step):
            rows = ref[start : start + step, :].astype(F32)
            square = rows * rows
            for at in range(0, step, 8):
                total = total + square[at : at + 8]
    total = jnp.sum(jnp.sum(total, axis=0, keepdims=True), axis=1, keepdims=True)
    out_ref[...] = jnp.broadcast_to(total, (8, HALF))


def run_square_sum(a, b, c):
    vmem = pl.BlockSpec(memory_space=pltpu.VMEM)
    return pl.pallas_call(
        square_sum,
        out_shape=jax.ShapeDtypeStruct((8, HALF), F32),
        in_specs=[vmem] * 3,
        out_specs=vmem,
        compiler_params=pltpu.CompilerParams(vmem_limit_bytes=16 << 20),
        name="squares",
    )(a, b, c)


def updated(grad, weight, moment, average, factor):
    decay = min(0.9999, (1.0 + STEP) / (10.0 + STEP))
    clipped = grad * factor
    direction = clipped + WEIGHT_DECAY * weight
    moment_new = MOMENTUM_DECAY * moment + direction
    weight_new = weight - LEARN_RATE * (direction + MOMENTUM_DECAY * moment_new)
    average_new = decay * average + (1.0 - decay) * weight_new
    return clipped, moment_new, weight_new, average_new


def optimizer_step(*refs):
    (own, other), refs = refs[:2], refs[2:]
    grads, refs = refs[:10], refs[10:]
    states, refs = refs[:18], refs[18:]
    outs, (norm_ref,) = refs[:28], refs[28:]
    norm = jnp.sqrt(own[0:1, 0:1] + other[0:1, 0:1])
    factor = jnp.minimum(1.0, CLIP_LIMIT / (norm + 1e-06))

    def put(index, lanes, grad):
        weight, moment, average = (states[kind * 6 + index][:, lanes] for kind in range(3))
        new = updated(grad, weight, moment, average, factor)
        for kind in range(4):
            outs[kind * 6 + index][:, lanes] = new[kind]
        if index >= 2:
            outs[24 + index - 2][:, lanes] = new[2].astype(BF16)

    for part in range(3):
        put(2, slice(part * D, (part + 1) * D), grads[part][...].astype(F32))
    put(3, slice(0, D), grads[3][...].astype(F32))
    for part in range(4):
        put(4, slice(part * D, (part + 1) * D), grads[4 + part][...].astype(F32))
    put(5, slice(0, D), grads[8][...].astype(F32))

    @pl.when(pl.program_id(0) == 0)
    def _():
        rows = grads[9][...].astype(F32)
        for part in range(13):
            put(0, slice(part * D, (part + 1) * D), rows[part : part + 1, :])
        put(1, slice(0, D), rows[13:22, :])
        norm_ref[...] = jnp.broadcast_to(norm, (8, HALF))


STEPS = 8


def run_optimizer(own, other, a, b, c, states):
    rows = D // STEPS
    deep = FF // STEPS

    def fixed(shape):
        return pl.BlockSpec(shape, lambda i: (0, 0))

    def strip(first):
        return pl.BlockSpec((rows, D), lambda i: (first * STEPS + i, 0))

    grad_specs = [strip(0), strip(1), strip(2), strip(3)] + [strip(part) for part in range(4)]
    grad_specs += [pl.BlockSpec((deep, D), lambda i: (i, 0)), pl.BlockSpec((32, D), lambda i: (FF // 32, 0))]
    state_specs = [
        fixed((1, VEC)),
        fixed((9, D)),
        pl.BlockSpec((rows, 3 * D), lambda i: (i, 0)),
        pl.BlockSpec((rows, D), lambda i: (i, 0)),
        pl.BlockSpec((rows, FF), lambda i: (i, 0)),
        pl.BlockSpec((deep, D), lambda i: (i, 0)),
    ]
    shapes = [(1, VEC), (9, D), (D, 3 * D), (D, D), (D, FF), (FF, D)]
    return pl.pallas_call(
        optimizer_step,
        grid=(STEPS,),
        out_shape=[jax.ShapeDtypeStruct(shape, F32) for shape in shapes] * 4
        + [jax.ShapeDtypeStruct(shape, BF16) for shape in shapes[2:]]
        + [jax.ShapeDtypeStruct((8, HALF), F32)],
        in_specs=[fixed((8, HALF))] * 2 + grad_specs + state_specs * 3,
        out_specs=state_specs * 4 + state_specs[2:] + [fixed((8, HALF))],
        compiler_params=pltpu.CompilerParams(vmem_limit_bytes=32 << 20),
        name="optimizer",
    )(own, other, a, a, a, a, b, b, b, b, c, c, *states)


def swapped(value):
    return lax.ppermute(value, "section", [(0, 1), (1, 0)])


def exchange_orders(bits):
    if bits == 4:
        return ((0, 1, 2, 3), (1, 2, 0, 3), (2, 0, 1, 3))
    turn = max(1, bits // 3)
    every = tuple(range(bits))
    return tuple(every[turn * part :] + every[: turn * part] for part in range(3))


def exchanged(value, bit, size):
    return lax.ppermute(value, "dp", [(index, index ^ (1 << bit)) for index in range(size)])


def summed_over_dp(parts):
    size = lax.axis_size("dp")
    bits = size.bit_length() - 1
    if size != 1 << bits or any(part.shape[0] % size for part in parts):
        return [lax.psum(part.astype(F32), "dp").astype(BF16) for part in parts]
    index = lax.axis_index("dp")
    orders = exchange_orders(bits)
    shapes = [part.shape for part in parts]
    held = [part.reshape((2,) * bits + (part.shape[0] // size, D)) for part in parts]
    for step in range(bits):
        kept, came = [], []
        for value, order in zip(held, orders):
            mine = (index >> order[step]) & 1
            kept.append(lax.dynamic_index_in_dim(value, mine, 0, keepdims=False))
            came.append(exchanged(lax.dynamic_index_in_dim(value, 1 - mine, 0, keepdims=False), order[step], size))
        held = [(a.astype(F32) + b.astype(F32)).astype(BF16) for a, b in zip(kept, came)]
    for step in reversed(range(bits)):
        grown = []
        for value, order in zip(held, orders):
            low = ((index >> order[step]) & 1) == 0
            came = exchanged(value, order[step], size)
            grown.append(jnp.stack([jnp.where(low, value, came), jnp.where(low, came, value)]))
        held = grown
    return [value.reshape(shape) for value, shape in zip(held, shapes)]


def per_device(inputs, cotangent, *states):
    states = [array.reshape(array.shape[-2:]) if array.ndim == 3 else array for array in states]
    vectors, kernels, w_qkv, w_proj, w_fc1, w_fc2 = states[:6]
    section = lax.axis_index("section")
    wide = jnp.concatenate([w_qkv, w_proj, w_fc1], axis=1).astype(BF16)
    deep = w_fc2.astype(BF16)
    outs, grads, sums = run_blocks(
        section.astype(jnp.int32).reshape(1),
        inputs,
        cotangent,
        vectors,
        swapped(vectors),
        kernels,
        swapped(kernels),
        wide,
        swapped(wide),
        deep,
        swapped(deep),
    )
    came = swapped(sums[1])
    total = (sums[0].astype(F32) + came.astype(F32)).astype(BF16)
    a, b, c = summed_over_dp([total[0:1024], total[1024:2048], total[2048:]])
    squares = run_square_sum(a, b, c)
    new = run_optimizer(squares, swapped(squares), a, b, c, states)
    first = section == 0

    def both_rows(value):
        own, came = value[0], swapped(value[1])
        return jnp.stack([jnp.where(first, own, came), jnp.where(first, came, own)]).reshape(1, 2 * MB_TOK, D)

    def whole(arrays):
        return [array if array.shape == (1, VEC) else array[None] for array in arrays]

    return (
        both_rows(outs),
        both_rows(grads),
        *whole(new[0:6]),
        new[28][0, 0],
        *whole(new[6:28]),
    )


def solution(mesh):
    rows = P("dp", None)
    state = (P("section", None),) + (P("section", None, None),) * 5
    return jax.shard_map(
        per_device,
        mesh=mesh,
        in_specs=(rows, rows) + state * 3,
        out_specs=(P("section", "dp", None),) * 2 + state + (P(),) + state * 3 + state[2:],
        check_vma=False,
    )
```

```python
import jax
import jax.numpy as jnp
import numpy as np
from jax import lax
from jax.experimental import pallas as pl
from jax.experimental.pallas import tpu as pltpu
from jax.sharding import PartitionSpec as P

D = 256
HALF = 128
HEADS = 8
HEAD = 32
FF = 1024
BIG_SIDE = 14
SMALL_SIDE = 6
BIG_MB = 1
SMALL_MB = 3
STEP = 8
MB_TOK = 304
VEC = 3328

NORM_EPS = 1e-05
CLIP_LIMIT = 5.0
LEARN_RATE = 4.0
MOMENTUM_DECAY = 0.9
WEIGHT_DECAY = 5e-05

F32 = jnp.float32
BF16 = jnp.bfloat16

GROUP = 128
GROUPS = ((0, 112), (112, 84), (196, 108))
KINDS = (0, 0, 1)
NGROUP = len(GROUPS)
ATT = NGROUP * GROUP
SCALE = HEAD ** -0.5
LOG2E = 1.4426950408889634
EXP_SCALE = SCALE * LOG2E
OFF = -1e30
ROWS = ((0, 80), (80, 80), (160, 80), (240, 64))
PARTS = (1152, 1152, 1152)


def placement_tables():
    plain = np.zeros((ATT, MB_TOK), np.float32)
    turned = np.zeros((ATT, MB_TOK), np.float32)
    transposed = []
    base = 0
    for side, count in ((BIG_SIDE, BIG_MB), (SMALL_SIDE, SMALL_MB)):
        for _ in range(count):
            for row in range(side):
                for col in range(side):
                    transposed.append(base + col * side + row)
            base += side * side
    for group, (first, size) in enumerate(GROUPS):
        for at in range(size):
            plain[group * GROUP + at, first + at] = 1.0
            turned[group * GROUP + at, transposed[first + at]] = 1.0
    return plain, turned


def stripe_tables():
    shifts = np.zeros((2, 5 * GROUP, GROUP), np.float32)
    fence = np.full((2, GROUP, GROUP), OFF, np.float32)
    lower = np.zeros((2, GROUP, HALF), np.float32)
    for kind, (side, sizes) in enumerate(((BIG_SIDE, 112), (SMALL_SIDE, 108))):
        stripe = 2 * side
        for at in range(GROUP):
            own = at // stripe
            fence[kind, at, own * stripe : (own + 1) * stripe] = 0.0
        for at in range(sizes):
            own, inner = divmod(at, stripe)
            row, col = divmod(inner, side)
            lower[kind, at, :] = float(row)
            moves = ((row, col - 1), (row, col + 1), (1 - row, col - 1), (1 - row, col), (1 - row, col + 1))
            for move, (to_row, to_col) in enumerate(moves):
                if 0 <= to_col < side:
                    shifts[kind, move * GROUP + at, own * stripe + to_row * side + to_col] = 1.0
    return shifts, fence, lower


def kept_in(arrays, spaces):
    return [pltpu.with_memory_space_constraint(array, space) for array, space in zip(arrays, spaces)]


def dot(a, b):
    return jnp.dot(a, b, preferred_element_type=F32)


def dot_nt(a, b):
    return lax.dot_general(a, b, (((1,), (1,)), ((), ())), preferred_element_type=F32)


def dot_tn(a, b):
    return lax.dot_general(a, b, (((0,), (0,)), ((), ())), preferred_element_type=F32)


def head_masks():
    lane = lax.broadcasted_iota(jnp.int32, (1, HALF), 1) // HEAD
    return [(lane == head).astype(BF16) for head in range(HEADS // 2)]


def stacked_heads(rows, masks):
    return jnp.concatenate([rows * mask for mask in masks], axis=0)


def picked_heads(product):
    return jnp.concatenate(
        [
            product[HEAD * head : HEAD * (head + 1), GROUP * head : GROUP * (head + 1)]
            for head in range(HEADS // 2)
        ],
        axis=0,
    )


def turned_taps(taps):
    turned = [3 * (index % 3) + index // 3 for index in range(9)]
    return [
        jnp.concatenate(
            [taps[:, index * D : index * D + HALF], taps[:, turned[index] * D + HALF : (turned[index] + 1) * D]],
            axis=1,
        )
        for index in range(9)
    ]


def norm_forward(x, gain, offset):
    centre = x - jnp.mean(x, axis=-1, keepdims=True)
    spread = jnp.mean(centre * centre, axis=-1, keepdims=True)
    scale = lax.rsqrt(spread + NORM_EPS)
    hat = centre * scale
    return hat, scale, hat * gain + offset


def norm_backward(grad, hat, scale, gain):
    inner = grad * gain
    mean_inner = jnp.mean(inner, axis=-1, keepdims=True)
    mean_cross = jnp.mean(inner * hat, axis=-1, keepdims=True)
    return scale * (inner - mean_inner - hat * mean_cross)


def column_sum(x):
    return jnp.sum(x.astype(F32), axis=0, keepdims=True)


def vec_at(vec, index, width=1):
    return vec[:, index * D : (index + width) * D]


def forward_block(x_ref, out_ref, vec_ref, taps_ref, w, saved, tables, work, need):
    wq, wp, w1, w2 = w
    (hat1, scale1, normed, qkv, probs, mixed, hat2, scale2, normed2, slope, activ) = saved
    plain, turned, plain_t, turned_t, shifts, fence, lower = tables
    normed_nat, mixed_att, middle, hidden = work
    need("x", "vec")
    vec = vec_ref[...]
    for start, size in ROWS:
        rows = pl.ds(start, size)
        hat, scale, y = norm_forward(x_ref[rows, :].astype(F32), vec_at(vec, 0), vec_at(vec, 2))
        hat1[rows, :] = hat
        scale1[rows, :] = jnp.broadcast_to(scale, (size, HALF))
        normed_nat[rows, :] = y.astype(BF16)
    need("place", "wide")
    base = normed_nat[...]
    biases = (vec_at(vec, 4), None, vec_at(vec, 5))
    for half, table in enumerate((plain, turned)):
        placed = dot(table[...], base).astype(BF16)
        normed[half] = placed
        lanes = slice(half * HALF, (half + 1) * HALF)
        for part in range(3):
            got = dot(placed, wq[:, part * D + half * HALF : part * D + (half + 1) * HALF])
            if biases[part] is not None:
                got = got + biases[part][:, lanes]
            qkv[part, :, lanes] = got.astype(BF16)
    masks = head_masks()
    need("stripe")
    taps9 = turned_taps(taps_ref[...])
    bias = vec_at(vec, 7)
    for group in range(NGROUP):
        kind = KINDS[group]
        rows = pl.ds(group * GROUP, GROUP)
        v = qkv[2, rows, :]
        moved = dot(shifts[kind], v)
        low_row = lower[kind] > 0.5
        low_row = jnp.concatenate([low_row, low_row], axis=1)
        lepe = bias + taps9[4] * v.astype(F32)
        lepe = lepe + taps9[3] * moved[0:GROUP] + taps9[5] * moved[GROUP : 2 * GROUP]
        for step in range(3):
            tap = jnp.where(low_row, taps9[step], taps9[6 + step])
            lepe = lepe + tap * moved[(2 + step) * GROUP : (3 + step) * GROUP]
        fenced = fence[kind]
        for half in range(2):
            lanes = slice(half * HALF, (half + 1) * HALF)
            q_stack = stacked_heads(qkv[0, rows, lanes], masks)
            scores = dot_nt(qkv[1, rows, lanes], q_stack)
            low = []
            for head in range(HEADS // 2):
                s = scores[:, head * GROUP : (head + 1) * GROUP] + fenced
                p = jnp.exp2((s - jnp.max(s, axis=0, keepdims=True)) * EXP_SCALE)
                p = p * (1.0 / jnp.sum(p, axis=0, keepdims=True))
                probs[group * 2 + half, :, head * GROUP : (head + 1) * GROUP] = p
                low.append(p.astype(BF16))
            attended = picked_heads(dot(v[:, lanes].T, jnp.concatenate(low, axis=1))).T
            mixed_att[rows, lanes] = (attended + lepe[:, lanes]).astype(BF16)
    need("place_t")
    mixed[:, :HALF] = dot(plain_t[...], mixed_att[:, :HALF]).astype(BF16)
    mixed[:, HALF:] = dot(turned_t[...], mixed_att[:, HALF:]).astype(BF16)
    middle[...] = dot(mixed[...], wp[...])
    for start, size in ROWS:
        rows = pl.ds(start, size)
        mid = x_ref[rows, :].astype(F32) + middle[rows, :] + vec_at(vec, 6)
        middle[rows, :] = mid
        hat, scale, y = norm_forward(mid, vec_at(vec, 1), vec_at(vec, 3))
        hat2[rows, :] = hat
        scale2[rows, :] = jnp.broadcast_to(scale, (size, HALF))
        normed2[rows, :] = y.astype(BF16)
    hidden[...] = dot(normed2[...], w1[...])
    for start, size in ROWS:
        rows = pl.ds(start, size)
        for part in range(4):
            cols = slice(part * D, (part + 1) * D)
            h = hidden[rows, cols] + vec_at(vec, 9 + part)
            cdf = 0.5 * (1.0 + lax.erf(h * 0.7071067811865476))
            pdf = 0.3989422804014327 * jnp.exp(-0.5 * h * h)
            activ[rows, cols] = (h * cdf).astype(BF16)
            slope[rows, cols] = cdf + h * pdf
    need("deep")
    out_ref[...] = dot(activ[...], w2[...])
    for start, size in ROWS:
        rows = pl.ds(start, size)
        out_ref[rows, :] = out_ref[rows, :] + middle[rows, :] + vec_at(vec, 8)


def backward_block(up_ref, grad_ref, vec_ref, taps_ref, w, saved, tables, work, sums, small):
    wq, wp, w1, w2 = w
    (hat1, scale1, normed, qkv, probs, mixed, hat2, scale2, normed2, slope, activ) = saved
    plain, turned, plain_t, turned_t, shifts, fence, lower = tables
    branch, gact, ghid, gmid, gmix, dqkv, dnat, gnorm = work
    early, inner, outer = sums
    vec = vec_ref[...]
    branch[...] = up_ref[...].astype(BF16)
    outer[0:FF, :] = dot_tn(activ[...], branch[...]).astype(BF16)
    sums = column_sum(branch[...])
    small[8:9, :] = sums
    gact[...] = dot_nt(branch[...], w2[...])
    parts = [jnp.zeros((1, D), F32) for _ in range(4)]
    for start, size in ROWS:
        rows = pl.ds(start, size)
        for part in range(4):
            cols = slice(part * D, (part + 1) * D)
            low = (gact[rows, cols] * slope[rows, cols]).astype(BF16)
            ghid[rows, cols] = low
            parts[part] = parts[part] + column_sum(low)
    for part in range(4):
        small[9 + part : 10 + part, :] = parts[part]
    for part in range(4):
        inner[part * D : (part + 1) * D, :] = dot_tn(
            normed2[...], ghid[:, part * D : (part + 1) * D]
        ).astype(BF16)
    gnorm[...] = dot_nt(ghid[...], w1[...])
    gains, offsets, outs = (jnp.zeros((1, D), F32) for _ in range(3))
    for start, size in ROWS:
        rows = pl.ds(start, size)
        g = gnorm[rows, :]
        hat = hat2[rows, :]
        scale = scale2[rows, :]
        gains = gains + column_sum(g * hat)
        offsets = offsets + column_sum(g)
        full = jnp.concatenate([scale, scale], axis=1)
        total = up_ref[rows, :].astype(F32) + norm_backward(g, hat, full, vec_at(vec, 1))
        gmid[rows, :] = total
        low = total.astype(BF16)
        branch[rows, :] = low
        outs = outs + column_sum(low)
    small[1:2, :] = gains
    small[3:4, :] = offsets
    small[6:7, :] = outs
    early[3 * D : 4 * D, :] = dot_tn(mixed[...], branch[...]).astype(BF16)
    low = dot_nt(branch[...], wp[...]).astype(BF16)
    gmix[0:MB_TOK, :] = low
    small[7:8, :] = column_sum(low)
    place_h = dot(plain[...], low[:, :HALF]).astype(BF16)
    place_v = dot(turned[...], low[:, HALF:]).astype(BF16)
    gmix[:, :HALF] = place_h
    gmix[:, HALF:] = place_v
    masks = head_masks()
    taps9 = turned_taps(taps_ref[...])
    tap_sums = [jnp.zeros((1, D), F32) for _ in range(9)]
    for group in range(NGROUP):
        kind = KINDS[group]
        rows = pl.ds(group * GROUP, GROUP)
        g_low = gmix[rows, :]
        moved = dot(shifts[kind], g_low)
        low_row = lower[kind] > 0.5
        low_row = jnp.concatenate([low_row, low_row], axis=1)
        v32 = qkv[2, rows, :].astype(F32)
        g32 = g_low.astype(F32)
        tap_sums[4] = tap_sums[4] + column_sum(v32 * g32)
        left, right = moved[0:GROUP], moved[GROUP : 2 * GROUP]
        lepe = taps9[4] * g32 + taps9[3] * right + taps9[5] * left
        tap_sums[3] = tap_sums[3] + column_sum(v32 * right)
        tap_sums[5] = tap_sums[5] + column_sum(v32 * left)
        for step in range(3):
            at = moved[(4 - step) * GROUP : (5 - step) * GROUP]
            lepe = lepe + jnp.where(low_row, taps9[6 + step], taps9[step]) * at
            product = v32 * at
            tap_sums[6 + step] = tap_sums[6 + step] + column_sum(jnp.where(low_row, product, 0.0))
            tap_sums[step] = tap_sums[step] + column_sum(jnp.where(low_row, 0.0, product))
        for half in range(2):
            lanes = slice(half * HALF, (half + 1) * HALF)
            unit = group * 2 + half
            g_stack = stacked_heads(gmix[rows, lanes], masks)
            q_stack = stacked_heads(qkv[0, rows, lanes], masks)
            k = qkv[1, rows, lanes]
            gprobs = dot_nt(qkv[2, rows, lanes], g_stack)
            low_p, low_s = [], []
            for head in range(HEADS // 2):
                cols = slice(head * GROUP, (head + 1) * GROUP)
                p = probs[unit, :, cols]
                gp = gprobs[:, cols]
                down = jnp.sum(gp * p, axis=0, keepdims=True)
                low_s.append((p * (gp - down)).astype(BF16))
                low_p.append(p.astype(BF16))
            low_p = jnp.concatenate(low_p, axis=1)
            low_s = jnp.concatenate(low_s, axis=1)
            grad_v = dot(low_p, g_stack) + lepe[:, lanes]
            grad_k = dot(low_s, q_stack) * SCALE
            grad_q = picked_heads(dot(k.T, low_s)).T * SCALE
            dqkv[half, rows, 0:HALF] = grad_q.astype(BF16)
            dqkv[half, rows, HALF:D] = grad_k.astype(BF16)
            dqkv[half, rows, D : 3 * HALF] = grad_v.astype(BF16)
    for index in range(9):
        tap = index
        turned_index = 3 * (index % 3) + index // 3
        small[13 + index : 14 + index, :] = jnp.concatenate(
            [tap_sums[tap][:, :HALF], tap_sums[turned_index][:, HALF:]], axis=1
        )
    for half, table_t in enumerate((plain_t, turned_t)):
        lanes = slice(half * HALF, (half + 1) * HALF)
        both = dqkv[half]
        small[4:5, lanes] = column_sum(both[:, 0:HALF])
        small[5:6, lanes] = column_sum(both[:, D : 3 * HALF])
        grads = dot_tn(normed[half], both)
        for part in range(3):
            early[part * D : (part + 1) * D, lanes] = grads[:, part * HALF : (part + 1) * HALF].astype(BF16)
        natural = dot(table_t[...], both).astype(BF16)
        for part in range(3):
            dnat[:, part * D + half * HALF : part * D + (half + 1) * HALF] = natural[
                :, part * HALF : (part + 1) * HALF
            ]
    gnorm[...] = dot_nt(dnat[...], wq[...])
    gains, offsets = (jnp.zeros((1, D), F32) for _ in range(2))
    for start, size in ROWS:
        rows = pl.ds(start, size)
        g = gnorm[rows, :]
        hat = hat1[rows, :]
        scale = scale1[rows, :]
        gains = gains + column_sum(g * hat)
        offsets = offsets + column_sum(g)
        full = jnp.concatenate([scale, scale], axis=1)
        grad_ref[rows, :] = gmid[rows, :] + norm_backward(g, hat, full, vec_at(vec, 0))
    small[0:1, :] = gains
    small[2:3, :] = offsets
    outer[FF : FF + 32, :] = small[...].astype(BF16)


SAVED = [
    ((MB_TOK, D), F32),
    ((MB_TOK, HALF), F32),
    ((2, ATT, D), BF16),
    ((3, ATT, D), BF16),
    ((2 * NGROUP, GROUP, 4 * GROUP), F32),
    ((MB_TOK, D), BF16),
    ((MB_TOK, D), F32),
    ((MB_TOK, HALF), F32),
    ((MB_TOK, D), BF16),
    ((MB_TOK, FF), F32),
    ((MB_TOK, FF), BF16),
]
FORWARD_WORK = [((MB_TOK, D), BF16), ((ATT, D), BF16), ((MB_TOK, D), F32), ((MB_TOK, FF), F32)]
BACKWARD_WORK = [
    ((MB_TOK, D), BF16),
    ((MB_TOK, FF), F32),
    ((MB_TOK, FF), BF16),
    ((MB_TOK, D), F32),
    ((ATT, D), BF16),
    ((2, ATT, 3 * HALF), BF16),
    ((MB_TOK, 3 * D), BF16),
    ((MB_TOK, D), F32),
]


INPUTS = [
    ((MB_TOK, D), BF16),
    ((MB_TOK, D), BF16),
    ((2, 1, VEC), F32),
    ((2, 1, 9 * D), F32),
    ((2, D, 8 * D), BF16),
    ((2, FF, D), BF16),
    ((ATT, MB_TOK), BF16),
    ((ATT, MB_TOK), BF16),
    ((MB_TOK, ATT), BF16),
    ((MB_TOK, ATT), BF16),
    ((2, 5 * GROUP, GROUP), BF16),
    ((2, GROUP, GROUP), F32),
    ((2, GROUP, HALF), F32),
]
RESULTS = [((2, MB_TOK, D), F32), ((2, MB_TOK, D), F32)] + [((2, rows, D), BF16) for rows in PARTS]
OTHER_WORK = [((MB_TOK, D), BF16), ((32, D), F32)]


def section_step(sec_ref, *refs):
    def take(count):
        nonlocal refs
        taken, refs = refs[:count], refs[count:]
        return taken

    x_in, c_in, vec_own, vec_other, ker_own, ker_other, wide_own, wide_other, deep_own, deep_other = take(10)
    table_in = take(7)
    sent = [take(2) for _ in RESULTS]
    held = take(len(INPUTS))
    results = take(len(RESULTS))
    kept = (take(len(SAVED)), take(len(SAVED)))
    forward_work = take(len(FORWARD_WORK))
    backward_work = take(len(BACKWARD_WORK))
    feed, small, in_sems, out_sems = refs
    x, c, vecs, taps, wide, deep = held[:6]
    tables = held[6:]
    sec = sec_ref[0]
    at = pl.multiple_of(sec * MB_TOK, 16)
    moves = [
        ("x", x_in.at[pl.ds(at, MB_TOK)], x),
        ("vec", vec_own, vecs.at[sec]),
        ("vec", vec_other, vecs.at[1 - sec]),
        ("place", table_in[0], tables[0]),
        ("place", table_in[1], tables[1]),
        ("wide", wide_own, wide.at[sec]),
        ("wide", wide_other, wide.at[1 - sec]),
        ("stripe", table_in[4], tables[4]),
        ("stripe", table_in[5], tables[5]),
        ("stripe", table_in[6], tables[6]),
        ("stripe", ker_own, taps.at[sec]),
        ("stripe", ker_other, taps.at[1 - sec]),
        ("place_t", table_in[2], tables[2]),
        ("place_t", table_in[3], tables[3]),
        ("deep", deep_own, deep.at[sec]),
        ("deep", deep_other, deep.at[1 - sec]),
        ("c", c_in.at[pl.ds(at, MB_TOK)], c),
    ]
    pending = {}
    for index, (name, source, target) in enumerate(moves):
        copy = pltpu.make_async_copy(source, target, in_sems.at[index])
        copy.start()
        pending.setdefault(name, []).append(copy)

    def need(*names):
        for name in names:
            for copy in pending.pop(name, []):
                copy.wait()

    leaving = []

    def leave(index):
        for which, slot in enumerate((sec, 1 - sec)):
            copy = pltpu.make_async_copy(results[index].at[slot], sent[index][which], out_sems.at[2 * index + which])
            copy.start()
            leaving.append(copy)

    outs, grads, early, inner, outer = results
    small[...] = jnp.zeros_like(small)
    for part, rows in zip((early, inner, outer), PARTS):
        part[:, FF:, :] = jnp.zeros((2, rows - FF, D), BF16)
    weights = [
        (wide.at[b, :, 0 : 3 * D], wide.at[b, :, 3 * D : 4 * D], wide.at[b, :, 4 * D : 8 * D], deep.at[b])
        for b in range(2)
    ]
    sums = [(early.at[b], inner.at[b], outer.at[b]) for b in range(2)]

    def forward(b, source):
        forward_block(
            source, outs.at[b], vecs.at[b], taps.at[b], weights[b], kept[b], tables, forward_work, need
        )

    def backward(b, source):
        backward_block(
            source, grads.at[b], vecs.at[b], taps.at[b], weights[b], kept[b], tables, backward_work, sums[b], small
        )

    forward(0, x)
    feed[...] = outs[0].astype(BF16)
    forward(1, feed)
    leave(0)
    need("c")
    backward(1, c)
    feed[...] = grads[1].astype(BF16)
    backward(0, feed)
    for index in range(1, len(RESULTS)):
        leave(index)
    for copy in leaving:
        copy.wait()


def run_blocks(sec, *arrays):
    plain, turned = placement_tables()
    shifts, fence, lower = stripe_tables()
    tables = (
        jnp.asarray(plain, BF16),
        jnp.asarray(turned, BF16),
        jnp.asarray(plain.T, BF16),
        jnp.asarray(turned.T, BF16),
        jnp.asarray(shifts, BF16),
        jnp.asarray(fence, F32),
        jnp.asarray(lower, F32),
    )
    spaces = [pltpu.HBM] * 3 + [pltpu.VMEM, pltpu.HBM] * 3 + [pltpu.VMEM] + [pltpu.HBM] * 7
    smem = pl.BlockSpec(memory_space=pltpu.SMEM)
    scratch = INPUTS + RESULTS + SAVED + SAVED + FORWARD_WORK + BACKWARD_WORK + OTHER_WORK
    out_shape = [pltpu.VMEM(shape[1:], kind) for shape, kind in RESULTS for _ in range(2)]
    return pl.pallas_call(
        section_step,
        out_shape=out_shape,
        in_specs=[smem] + [pl.BlockSpec(memory_space=space) for space in spaces],
        out_specs=[pl.BlockSpec(memory_space=pl.ANY)] * len(out_shape),
        scratch_shapes=[pltpu.VMEM(shape, kind) for shape, kind in scratch]
        + [pltpu.SemaphoreType.DMA((17,)), pltpu.SemaphoreType.DMA((2 * len(RESULTS),))],
        compiler_params=pltpu.CompilerParams(vmem_limit_bytes=34 << 20),
        name="blocks",
    )(sec, *kept_in(arrays + tables, spaces))


NARROW = (((D, 3 * D), 0), ((D, D), 3 * D), ((D, FF), 4 * D), ((FF, D), None))


def narrowed(*refs):
    sources, (wide_out, deep_out), held, made, (in_sems, out_sems) = (
        refs[:4],
        refs[4:6],
        refs[6:10],
        refs[10:14],
        refs[14:],
    )
    coming = [pltpu.make_async_copy(sources[k], held[k], in_sems.at[k]) for k in range(4)]
    for copy in coming:
        copy.start()
    going = []
    for k, (shape, first) in enumerate(NARROW):
        coming[k].wait()
        made[k][...] = held[k][...].astype(BF16)
        target = deep_out if first is None else wide_out.at[:, pl.ds(first, shape[1])]
        copy = pltpu.make_async_copy(made[k], target, out_sems.at[k])
        copy.start()
        going.append(copy)
    for copy in going:
        copy.wait()


def run_narrowed(*weights):
    hbm = pl.BlockSpec(memory_space=pltpu.HBM)
    return pl.pallas_call(
        narrowed,
        out_shape=[pltpu.HBM((D, 8 * D), BF16), pltpu.HBM((FF, D), BF16)],
        in_specs=[hbm] * 4,
        out_specs=[hbm] * 2,
        scratch_shapes=[pltpu.VMEM(shape, F32) for shape, _ in NARROW]
        + [pltpu.VMEM(shape, BF16) for shape, _ in NARROW]
        + [pltpu.SemaphoreType.DMA((4,)), pltpu.SemaphoreType.DMA((4,))],
        compiler_params=pltpu.CompilerParams(vmem_limit_bytes=8 << 20),
        name="narrowed",
    )(*kept_in(weights, [pltpu.HBM] * 4))


def square_sum(a_ref, b_ref, c_ref, out_ref):
    total = jnp.zeros((8, D), F32)
    for ref in (a_ref, b_ref, c_ref):
        step = 64
        for start in range(0, ref.shape[0], step):
            rows = ref[start : start + step, :].astype(F32)
            square = rows * rows
            for at in range(0, step, 8):
                total = total + square[at : at + 8]
    total = jnp.sum(jnp.sum(total, axis=0, keepdims=True), axis=1, keepdims=True)
    out_ref[...] = jnp.broadcast_to(total, (8, HALF))


def run_square_sum(a, b, c):
    vmem = pl.BlockSpec(memory_space=pltpu.VMEM)
    return pl.pallas_call(
        square_sum,
        out_shape=jax.ShapeDtypeStruct((8, HALF), F32),
        in_specs=[vmem] * 3,
        out_specs=vmem,
        compiler_params=pltpu.CompilerParams(vmem_limit_bytes=16 << 20),
        name="squares",
    )(a, b, c)


def updated(grad, weight, moment, average, factor):
    decay = min(0.9999, (1.0 + STEP) / (10.0 + STEP))
    clipped = grad * factor
    direction = clipped + WEIGHT_DECAY * weight
    moment_new = MOMENTUM_DECAY * moment + direction
    weight_new = weight - LEARN_RATE * (direction + MOMENTUM_DECAY * moment_new)
    average_new = decay * average + (1.0 - decay) * weight_new
    return clipped, moment_new, weight_new, average_new


STEPS = 8


def optimizer_step(sec_ref, *refs):
    rows_in, refs = refs[:4], refs[4:]
    (own, other), refs = refs[:2], refs[2:]
    grads, refs = refs[:10], refs[10:]
    states, refs = refs[:18], refs[18:]
    outs, (norm_ref, *rows_out, sems) = refs[:28], refs[28:]
    sec = sec_ref[0]
    moves = []
    for index in range(4):
        first = pl.multiple_of((sec if index % 2 == 0 else 1 - sec) * MB_TOK, 8)
        target = rows_out[index // 2].at[pl.ds(first, MB_TOK)]
        moves.append(pltpu.make_async_copy(rows_in[index], target, sems.at[index]))

    @pl.when(pl.program_id(0) == 0)
    def _():
        for move in moves:
            move.start()

    norm = jnp.sqrt(own[0:1, 0:1] + other[0:1, 0:1])
    factor = jnp.minimum(1.0, CLIP_LIMIT / (norm + 1e-06))

    def put(index, lanes, grad):
        weight, moment, average = (states[kind * 6 + index][:, lanes] for kind in range(3))
        new = updated(grad, weight, moment, average, factor)
        for kind in range(4):
            outs[kind * 6 + index][:, lanes] = new[kind]
        if index >= 2:
            outs[24 + index - 2][:, lanes] = new[2].astype(BF16)

    for part in range(3):
        put(2, slice(part * D, (part + 1) * D), grads[part][...].astype(F32))
    put(3, slice(0, D), grads[3][...].astype(F32))
    for part in range(4):
        put(4, slice(part * D, (part + 1) * D), grads[4 + part][...].astype(F32))
    put(5, slice(0, D), grads[8][...].astype(F32))

    @pl.when(pl.program_id(0) == 0)
    def _():
        rows = grads[9][...].astype(F32)
        for part in range(13):
            put(0, slice(part * D, (part + 1) * D), rows[part : part + 1, :])
        for part in range(9):
            put(1, slice(part * D, (part + 1) * D), rows[13 + part : 14 + part, :])
        norm_ref[...] = norm

    @pl.when(pl.program_id(0) == STEPS - 1)
    def _():
        for move in moves:
            move.wait()


def run_optimizer(sec, rows_in, own, other, a, b, c, states):
    rows = D // STEPS
    deep = FF // STEPS

    def fixed(shape):
        return pl.BlockSpec(shape, lambda i: (0, 0))

    def strip(first):
        return pl.BlockSpec((rows, D), lambda i: (first * STEPS + i, 0))

    grad_specs = [strip(0), strip(1), strip(2), strip(3)] + [strip(part) for part in range(4)]
    grad_specs += [pl.BlockSpec((deep, D), lambda i: (i, 0)), pl.BlockSpec((32, D), lambda i: (FF // 32, 0))]
    state_specs = [
        fixed((1, VEC)),
        fixed((1, 9 * D)),
        pl.BlockSpec((rows, 3 * D), lambda i: (i, 0)),
        pl.BlockSpec((rows, D), lambda i: (i, 0)),
        pl.BlockSpec((rows, FF), lambda i: (i, 0)),
        pl.BlockSpec((deep, D), lambda i: (i, 0)),
    ]
    shapes = [(1, VEC), (1, 9 * D), (D, 3 * D), (D, D), (D, FF), (FF, D)]
    anywhere = pl.BlockSpec(memory_space=pltpu.HBM)
    spaces = [pltpu.VMEM] * 4
    return pl.pallas_call(
        optimizer_step,
        grid=(STEPS,),
        out_shape=[jax.ShapeDtypeStruct(shape, F32) for shape in shapes] * 4
        + [jax.ShapeDtypeStruct(shape, BF16) for shape in shapes[2:]]
        + [jax.ShapeDtypeStruct((1, 1), F32)]
        + [jax.ShapeDtypeStruct((2 * MB_TOK, D), F32)] * 2,
        in_specs=[pl.BlockSpec(memory_space=pltpu.SMEM)]
        + [pl.BlockSpec(memory_space=space) for space in spaces]
        + [fixed((8, HALF))] * 2
        + grad_specs
        + state_specs * 3,
        out_specs=state_specs * 4 + state_specs[2:] + [fixed((1, 1))] + [anywhere] * 2,
        scratch_shapes=[pltpu.SemaphoreType.DMA((4,))],
        compiler_params=pltpu.CompilerParams(vmem_limit_bytes=24 << 20),
        name="optimizer",
    )(sec, *kept_in(rows_in, spaces), own, other, a, a, a, a, b, b, b, b, c, c, *states)


def swapped(value):
    return lax.ppermute(value, "section", [(0, 1), (1, 0)])


def exchange_orders(bits):
    if bits == 4:
        return ((0, 1, 2, 3), (1, 2, 0, 3), (2, 0, 1, 3))
    turn = max(1, bits // 3)
    every = tuple(range(bits))
    return tuple(every[turn * part :] + every[: turn * part] for part in range(3))


def exchanged(value, bit, size):
    return lax.ppermute(value, "dp", [(index, index ^ (1 << bit)) for index in range(size)])


def exchange_bits():
    size = lax.axis_size("dp")
    bits = size.bit_length() - 1
    if size != 1 << bits or any(rows % size for rows in PARTS):
        return []
    index = lax.axis_index("dp")
    return [((index >> bit) & 1) == 0 for bit in range(bits)]


def summed_over_dp(parts, clear):
    size = lax.axis_size("dp")
    bits = len(clear)
    if not bits:
        return [lax.psum(part.astype(F32), "dp").astype(BF16) for part in parts]
    orders = exchange_orders(bits)
    shapes = [part.shape for part in parts]
    held = [part.reshape((2,) * bits + (part.shape[0] // size, D)) for part in parts]
    for step in range(bits):
        kept, came = [], []
        for value, order in zip(held, orders):
            low = clear[order[step]]
            kept.append(jnp.where(low, value[0], value[1]))
            came.append(exchanged(jnp.where(low, value[1], value[0]), order[step], size))
        held = [(a.astype(F32) + b.astype(F32)).astype(BF16) for a, b in zip(kept, came)]
    for step in reversed(range(bits)):
        grown = []
        for value, order in zip(held, orders):
            low = clear[order[step]]
            came = exchanged(value, order[step], size)
            grown.append(jnp.stack([jnp.where(low, value, came), jnp.where(low, came, value)]))
        held = grown
    return [value.reshape(shape) for value, shape in zip(held, shapes)]


def per_device(inputs, cotangent, *states):
    states = [array.reshape(1, 9 * D) if array.shape == (1, 9, D) else array for array in states]
    states = [array.reshape(array.shape[1:]) if array.ndim == 3 else array for array in states]
    vectors, kernels = states[:2]
    section = lax.axis_index("section").astype(jnp.int32).reshape(1)
    section, *clear = lax.optimization_barrier((section, *exchange_bits()))
    wide, deep = run_narrowed(*states[2:6])
    results = run_blocks(
        section,
        inputs,
        cotangent,
        vectors,
        swapped(vectors),
        kernels,
        swapped(kernels),
        wide,
        swapped(wide),
        deep,
        swapped(deep),
    )
    totals = [
        (own.astype(F32) + swapped(other).astype(F32)).astype(BF16)
        for own, other in zip(results[4::2], results[5::2])
    ]
    a, b, c = summed_over_dp(lax.optimization_barrier(totals), clear)
    squares = run_square_sum(a, b, c)
    rows_in = (results[0], swapped(results[1]), results[2], swapped(results[3]))
    new = run_optimizer(section, rows_in, squares, swapped(squares), a, b, c, states)

    def whole(arrays):
        return [
            array if array.shape == (1, VEC) else array.reshape(1, 9, D) if array.shape == (1, 9 * D) else array[None]
            for array in arrays
        ]

    return (new[29][None], new[30][None], *whole(new[0:6]), new[28].reshape(()), *whole(new[6:28]))


def solution(mesh):
    rows = P("dp", None)
    state = (P("section", None),) + (P("section", None, None),) * 5
    return jax.shard_map(
        per_device,
        mesh=mesh,
        in_specs=(rows, rows) + state * 3,
        out_specs=(P("section", "dp", None),) * 2 + state + (P(),) + state * 3 + state[2:],
        check_vma=False,
    )
```

```python
import jax
import jax.numpy as jnp
import numpy as np
from jax import lax
from jax.experimental import pallas as pl
from jax.experimental.pallas import tpu as pltpu
from jax.sharding import PartitionSpec as P

D = 256
HALF = 128
HEADS = 8
HEAD = 32
FF = 1024
BIG_SIDE = 14
SMALL_SIDE = 6
BIG_MB = 1
SMALL_MB = 3
STEP = 8
MB_TOK = 304
VEC = 3328

NORM_EPS = 1e-05
CLIP_LIMIT = 5.0
LEARN_RATE = 4.0
MOMENTUM_DECAY = 0.9
WEIGHT_DECAY = 5e-05

F32 = jnp.float32
BF16 = jnp.bfloat16

GROUP = 128
GROUPS = ((0, 112), (112, 84), (196, 108))
KINDS = (0, 0, 1)
NGROUP = len(GROUPS)
ATT = NGROUP * GROUP
SCALE = HEAD ** -0.5
LOG2E = 1.4426950408889634
EXP_SCALE = SCALE * LOG2E
OFF = -1e30
ROWS = ((0, 80), (80, 80), (160, 80), (240, 64))
PARTS = (1024, 1024, 1088)


def placement_tables():
    plain = np.zeros((ATT, MB_TOK), np.float32)
    turned = np.zeros((ATT, MB_TOK), np.float32)
    transposed = []
    base = 0
    for side, count in ((BIG_SIDE, BIG_MB), (SMALL_SIDE, SMALL_MB)):
        for _ in range(count):
            for row in range(side):
                for col in range(side):
                    transposed.append(base + col * side + row)
            base += side * side
    for group, (first, size) in enumerate(GROUPS):
        for at in range(size):
            plain[group * GROUP + at, first + at] = 1.0
            turned[group * GROUP + at, transposed[first + at]] = 1.0
    return plain, turned


def stripe_tables():
    shifts = np.zeros((2, 5 * GROUP, GROUP), np.float32)
    fence = np.full((2, GROUP, GROUP), OFF, np.float32)
    lower = np.zeros((2, GROUP, HALF), np.float32)
    for kind, (side, sizes) in enumerate(((BIG_SIDE, 112), (SMALL_SIDE, 108))):
        stripe = 2 * side
        for at in range(GROUP):
            own = at // stripe
            fence[kind, at, own * stripe : (own + 1) * stripe] = 0.0
        for at in range(sizes):
            own, inner = divmod(at, stripe)
            row, col = divmod(inner, side)
            lower[kind, at, :] = float(row)
            moves = ((row, col - 1), (row, col + 1), (1 - row, col - 1), (1 - row, col), (1 - row, col + 1))
            for move, (to_row, to_col) in enumerate(moves):
                if 0 <= to_col < side:
                    shifts[kind, move * GROUP + at, own * stripe + to_row * side + to_col] = 1.0
    return shifts, fence, lower


def kept_in(arrays, spaces):
    return [pltpu.with_memory_space_constraint(array, space) for array, space in zip(arrays, spaces)]


def dot(a, b):
    return jnp.dot(a, b, preferred_element_type=F32)


def dot_nt(a, b):
    return lax.dot_general(a, b, (((1,), (1,)), ((), ())), preferred_element_type=F32)


def dot_tn(a, b):
    return lax.dot_general(a, b, (((0,), (0,)), ((), ())), preferred_element_type=F32)


def head_masks():
    lane = lax.broadcasted_iota(jnp.int32, (1, HALF), 1) // HEAD
    return [(lane == head).astype(BF16) for head in range(HEADS // 2)]


def stacked_heads(rows, masks):
    return jnp.concatenate([rows * mask for mask in masks], axis=0)


def picked_heads(product):
    return jnp.concatenate(
        [
            product[HEAD * head : HEAD * (head + 1), GROUP * head : GROUP * (head + 1)]
            for head in range(HEADS // 2)
        ],
        axis=0,
    )


def turned_taps(taps):
    turned = [3 * (index % 3) + index // 3 for index in range(9)]
    return [
        jnp.concatenate(
            [taps[:, index * D : index * D + HALF], taps[:, turned[index] * D + HALF : (turned[index] + 1) * D]],
            axis=1,
        )
        for index in range(9)
    ]


def norm_forward(x, gain, offset):
    centre = x - jnp.mean(x, axis=-1, keepdims=True)
    spread = jnp.mean(centre * centre, axis=-1, keepdims=True)
    scale = lax.rsqrt(spread + NORM_EPS)
    hat = centre * scale
    return hat, scale, hat * gain + offset


def norm_backward(grad, hat, scale, gain):
    inner = grad * gain
    mean_inner = jnp.mean(inner, axis=-1, keepdims=True)
    mean_cross = jnp.mean(inner * hat, axis=-1, keepdims=True)
    return scale * (inner - mean_inner - hat * mean_cross)


def column_sum(x):
    return jnp.sum(x.astype(F32), axis=0, keepdims=True)


def vec_at(vec, index, width=1):
    return vec[:, index * D : (index + width) * D]


def forward_block(x_ref, out_ref, vec_ref, taps_ref, w, saved, tables, work, need):
    wq, wp, w1, w2 = w
    (hat1, scale1, normed, qkv, probs, mixed, hat2, scale2, normed2, slope, activ) = saved
    plain, turned, plain_t, turned_t, shifts, fence, lower = tables
    normed_nat, mixed_att, middle, hidden = work
    need("x", "vec")
    vec = vec_ref[...]
    for start, size in ROWS:
        rows = pl.ds(start, size)
        hat, scale, y = norm_forward(x_ref[rows, :].astype(F32), vec_at(vec, 0), vec_at(vec, 2))
        hat1[rows, :] = hat
        scale1[rows, :] = jnp.broadcast_to(scale, (size, HALF))
        normed_nat[rows, :] = y.astype(BF16)
    need("place", "wide")
    base = normed_nat[...]
    biases = (vec_at(vec, 4), None, vec_at(vec, 5))
    for half, table in enumerate((plain, turned)):
        placed = dot(table[...], base).astype(BF16)
        normed[half] = placed
        lanes = slice(half * HALF, (half + 1) * HALF)
        for part in range(3):
            got = dot(placed, wq[:, part * D + half * HALF : part * D + (half + 1) * HALF])
            if biases[part] is not None:
                got = got + biases[part][:, lanes]
            qkv[part, :, lanes] = got.astype(BF16)
    masks = head_masks()
    need("stripe")
    taps9 = turned_taps(taps_ref[...])
    bias = vec_at(vec, 7)
    for group in range(NGROUP):
        kind = KINDS[group]
        rows = pl.ds(group * GROUP, GROUP)
        v = qkv[2, rows, :]
        moved = dot(shifts[kind], v)
        low_row = lower[kind] > 0.5
        low_row = jnp.concatenate([low_row, low_row], axis=1)
        lepe = bias + taps9[4] * v.astype(F32)
        lepe = lepe + taps9[3] * moved[0:GROUP] + taps9[5] * moved[GROUP : 2 * GROUP]
        for step in range(3):
            tap = jnp.where(low_row, taps9[step], taps9[6 + step])
            lepe = lepe + tap * moved[(2 + step) * GROUP : (3 + step) * GROUP]
        fenced = fence[kind]
        for half in range(2):
            lanes = slice(half * HALF, (half + 1) * HALF)
            q_stack = stacked_heads(qkv[0, rows, lanes], masks)
            scores = dot_nt(qkv[1, rows, lanes], q_stack)
            low = []
            for head in range(HEADS // 2):
                s = scores[:, head * GROUP : (head + 1) * GROUP] + fenced
                p = jnp.exp2((s - jnp.max(s, axis=0, keepdims=True)) * EXP_SCALE)
                p = p * (1.0 / jnp.sum(p, axis=0, keepdims=True))
                probs[group * 2 + half, :, head * GROUP : (head + 1) * GROUP] = p
                low.append(p.astype(BF16))
            attended = picked_heads(dot(v[:, lanes].T, jnp.concatenate(low, axis=1))).T
            mixed_att[rows, lanes] = (attended + lepe[:, lanes]).astype(BF16)
    need("place_t")
    mixed[:, :HALF] = dot(plain_t[...], mixed_att[:, :HALF]).astype(BF16)
    mixed[:, HALF:] = dot(turned_t[...], mixed_att[:, HALF:]).astype(BF16)
    middle[...] = dot(mixed[...], wp[...])
    for start, size in ROWS:
        rows = pl.ds(start, size)
        mid = x_ref[rows, :].astype(F32) + middle[rows, :] + vec_at(vec, 6)
        middle[rows, :] = mid
        hat, scale, y = norm_forward(mid, vec_at(vec, 1), vec_at(vec, 3))
        hat2[rows, :] = hat
        scale2[rows, :] = jnp.broadcast_to(scale, (size, HALF))
        normed2[rows, :] = y.astype(BF16)
    hidden[...] = dot(normed2[...], w1[...])
    for start, size in ROWS:
        rows = pl.ds(start, size)
        for part in range(4):
            cols = slice(part * D, (part + 1) * D)
            h = hidden[rows, cols] + vec_at(vec, 9 + part)
            cdf = 0.5 * (1.0 + lax.erf(h * 0.7071067811865476))
            pdf = 0.3989422804014327 * jnp.exp(-0.5 * h * h)
            activ[rows, cols] = (h * cdf).astype(BF16)
            slope[rows, cols] = cdf + h * pdf
    need("deep")
    out_ref[...] = dot(activ[...], w2[...])
    for start, size in ROWS:
        rows = pl.ds(start, size)
        out_ref[rows, :] = out_ref[rows, :] + middle[rows, :] + vec_at(vec, 8)


def backward_block(up_ref, grad_ref, vec_ref, taps_ref, w, saved, tables, work, sums, small):
    wq, wp, w1, w2 = w
    (hat1, scale1, normed, qkv, probs, mixed, hat2, scale2, normed2, slope, activ) = saved
    plain, turned, plain_t, turned_t, shifts, fence, lower = tables
    branch, gact, ghid, gmid, gmix, dqkv, dnat, gnorm = work
    early, inner, outer = sums
    vec = vec_ref[...]
    branch[...] = up_ref[...].astype(BF16)
    outer[0:FF, :] = dot_tn(activ[...], branch[...]).astype(BF16)
    sums = column_sum(branch[...])
    small[8:9, :] = sums
    gact[...] = dot_nt(branch[...], w2[...])
    parts = [jnp.zeros((1, D), F32) for _ in range(4)]
    for start, size in ROWS:
        rows = pl.ds(start, size)
        for part in range(4):
            cols = slice(part * D, (part + 1) * D)
            low = (gact[rows, cols] * slope[rows, cols]).astype(BF16)
            ghid[rows, cols] = low
            parts[part] = parts[part] + column_sum(low)
    for part in range(4):
        small[9 + part : 10 + part, :] = parts[part]
    for part in range(4):
        inner[part * D : (part + 1) * D, :] = dot_tn(
            normed2[...], ghid[:, part * D : (part + 1) * D]
        ).astype(BF16)
    gnorm[...] = dot_nt(ghid[...], w1[...])
    gains, offsets, outs = (jnp.zeros((1, D), F32) for _ in range(3))
    for start, size in ROWS:
        rows = pl.ds(start, size)
        g = gnorm[rows, :]
        hat = hat2[rows, :]
        scale = scale2[rows, :]
        gains = gains + column_sum(g * hat)
        offsets = offsets + column_sum(g)
        full = jnp.concatenate([scale, scale], axis=1)
        total = up_ref[rows, :].astype(F32) + norm_backward(g, hat, full, vec_at(vec, 1))
        gmid[rows, :] = total
        low = total.astype(BF16)
        branch[rows, :] = low
        outs = outs + column_sum(low)
    small[1:2, :] = gains
    small[3:4, :] = offsets
    small[6:7, :] = outs
    early[3 * D : 4 * D, :] = dot_tn(mixed[...], branch[...]).astype(BF16)
    low = dot_nt(branch[...], wp[...]).astype(BF16)
    gmix[0:MB_TOK, :] = low
    small[7:8, :] = column_sum(low)
    place_h = dot(plain[...], low[:, :HALF]).astype(BF16)
    place_v = dot(turned[...], low[:, HALF:]).astype(BF16)
    gmix[:, :HALF] = place_h
    gmix[:, HALF:] = place_v
    masks = head_masks()
    taps9 = turned_taps(taps_ref[...])
    tap_sums = [jnp.zeros((1, D), F32) for _ in range(9)]
    for group in range(NGROUP):
        kind = KINDS[group]
        rows = pl.ds(group * GROUP, GROUP)
        g_low = gmix[rows, :]
        moved = dot(shifts[kind], g_low)
        low_row = lower[kind] > 0.5
        low_row = jnp.concatenate([low_row, low_row], axis=1)
        v32 = qkv[2, rows, :].astype(F32)
        g32 = g_low.astype(F32)
        tap_sums[4] = tap_sums[4] + column_sum(v32 * g32)
        left, right = moved[0:GROUP], moved[GROUP : 2 * GROUP]
        lepe = taps9[4] * g32 + taps9[3] * right + taps9[5] * left
        tap_sums[3] = tap_sums[3] + column_sum(v32 * right)
        tap_sums[5] = tap_sums[5] + column_sum(v32 * left)
        for step in range(3):
            at = moved[(4 - step) * GROUP : (5 - step) * GROUP]
            lepe = lepe + jnp.where(low_row, taps9[6 + step], taps9[step]) * at
            product = v32 * at
            tap_sums[6 + step] = tap_sums[6 + step] + column_sum(jnp.where(low_row, product, 0.0))
            tap_sums[step] = tap_sums[step] + column_sum(jnp.where(low_row, 0.0, product))
        for half in range(2):
            lanes = slice(half * HALF, (half + 1) * HALF)
            unit = group * 2 + half
            g_stack = stacked_heads(gmix[rows, lanes], masks)
            q_stack = stacked_heads(qkv[0, rows, lanes], masks)
            k = qkv[1, rows, lanes]
            gprobs = dot_nt(qkv[2, rows, lanes], g_stack)
            low_p, low_s = [], []
            for head in range(HEADS // 2):
                cols = slice(head * GROUP, (head + 1) * GROUP)
                p = probs[unit, :, cols]
                gp = gprobs[:, cols]
                down = jnp.sum(gp * p, axis=0, keepdims=True)
                low_s.append((p * (gp - down)).astype(BF16))
                low_p.append(p.astype(BF16))
            low_p = jnp.concatenate(low_p, axis=1)
            low_s = jnp.concatenate(low_s, axis=1)
            grad_v = dot(low_p, g_stack) + lepe[:, lanes]
            grad_k = dot(low_s, q_stack) * SCALE
            grad_q = picked_heads(dot(k.T, low_s)).T * SCALE
            dqkv[half, rows, 0:HALF] = grad_q.astype(BF16)
            dqkv[half, rows, HALF:D] = grad_k.astype(BF16)
            dqkv[half, rows, D : 3 * HALF] = grad_v.astype(BF16)
    for index in range(9):
        tap = index
        turned_index = 3 * (index % 3) + index // 3
        small[13 + index : 14 + index, :] = jnp.concatenate(
            [tap_sums[tap][:, :HALF], tap_sums[turned_index][:, HALF:]], axis=1
        )
    for half, table_t in enumerate((plain_t, turned_t)):
        lanes = slice(half * HALF, (half + 1) * HALF)
        both = dqkv[half]
        small[4:5, lanes] = column_sum(both[:, 0:HALF])
        small[5:6, lanes] = column_sum(both[:, D : 3 * HALF])
        grads = dot_tn(normed[half], both)
        for part in range(3):
            early[part * D : (part + 1) * D, lanes] = grads[:, part * HALF : (part + 1) * HALF].astype(BF16)
        natural = dot(table_t[...], both).astype(BF16)
        for part in range(3):
            dnat[:, part * D + half * HALF : part * D + (half + 1) * HALF] = natural[
                :, part * HALF : (part + 1) * HALF
            ]
    gnorm[...] = dot_nt(dnat[...], wq[...])
    gains, offsets = (jnp.zeros((1, D), F32) for _ in range(2))
    for start, size in ROWS:
        rows = pl.ds(start, size)
        g = gnorm[rows, :]
        hat = hat1[rows, :]
        scale = scale1[rows, :]
        gains = gains + column_sum(g * hat)
        offsets = offsets + column_sum(g)
        full = jnp.concatenate([scale, scale], axis=1)
        grad_ref[rows, :] = gmid[rows, :] + norm_backward(g, hat, full, vec_at(vec, 0))
    small[0:1, :] = gains
    small[2:3, :] = offsets
    outer[FF : FF + 32, :] = small[...].astype(BF16)


SAVED = [
    ((MB_TOK, D), F32),
    ((MB_TOK, HALF), F32),
    ((2, ATT, D), BF16),
    ((3, ATT, D), BF16),
    ((2 * NGROUP, GROUP, 4 * GROUP), F32),
    ((MB_TOK, D), BF16),
    ((MB_TOK, D), F32),
    ((MB_TOK, HALF), F32),
    ((MB_TOK, D), BF16),
    ((MB_TOK, FF), F32),
    ((MB_TOK, FF), BF16),
]
FORWARD_WORK = [((MB_TOK, D), BF16), ((ATT, D), BF16), ((MB_TOK, D), F32), ((MB_TOK, FF), F32)]
BACKWARD_WORK = [
    ((MB_TOK, D), BF16),
    ((MB_TOK, FF), F32),
    ((MB_TOK, FF), BF16),
    ((MB_TOK, D), F32),
    ((ATT, D), BF16),
    ((2, ATT, 3 * HALF), BF16),
    ((MB_TOK, 3 * D), BF16),
    ((MB_TOK, D), F32),
]


INPUTS = [
    ((MB_TOK, D), BF16),
    ((MB_TOK, D), BF16),
    ((2, 1, VEC), F32),
    ((2, 1, 9 * D), F32),
    ((2, D, 8 * D), BF16),
    ((2, FF, D), BF16),
    ((ATT, MB_TOK), BF16),
    ((ATT, MB_TOK), BF16),
    ((MB_TOK, ATT), BF16),
    ((MB_TOK, ATT), BF16),
    ((2, 5 * GROUP, GROUP), BF16),
    ((2, GROUP, GROUP), F32),
    ((2, GROUP, HALF), F32),
]
RESULTS = [((2, MB_TOK, D), F32), ((2, MB_TOK, D), F32)] + [((2, rows, D), BF16) for rows in PARTS]
OTHER_WORK = [((MB_TOK, D), BF16), ((32, D), F32)]


def section_step(sec_ref, *refs):
    def take(count):
        nonlocal refs
        taken, refs = refs[:count], refs[count:]
        return taken

    x_in, c_in, vec_own, vec_other, ker_own, ker_other, wide_own, wide_other, deep_own, deep_other = take(10)
    table_in = take(7)
    sent = [take(2) for _ in RESULTS]
    held = take(len(INPUTS))
    results = take(len(RESULTS))
    kept = (take(len(SAVED)), take(len(SAVED)))
    forward_work = take(len(FORWARD_WORK))
    backward_work = take(len(BACKWARD_WORK))
    feed, small, in_sems, out_sems = refs
    x, c, vecs, taps, wide, deep = held[:6]
    tables = held[6:]
    sec = sec_ref[0]
    at = pl.multiple_of(sec * MB_TOK, 16)
    moves = [
        ("x", x_in.at[pl.ds(at, MB_TOK)], x),
        ("vec", vec_own, vecs.at[sec]),
        ("vec", vec_other, vecs.at[1 - sec]),
        ("place", table_in[0], tables[0]),
        ("place", table_in[1], tables[1]),
        ("wide", wide_own, wide.at[sec]),
        ("wide", wide_other, wide.at[1 - sec]),
        ("stripe", table_in[4], tables[4]),
        ("stripe", table_in[5], tables[5]),
        ("stripe", table_in[6], tables[6]),
        ("stripe", ker_own, taps.at[sec]),
        ("stripe", ker_other, taps.at[1 - sec]),
        ("place_t", table_in[2], tables[2]),
        ("place_t", table_in[3], tables[3]),
        ("deep", deep_own, deep.at[sec]),
        ("deep", deep_other, deep.at[1 - sec]),
        ("c", c_in.at[pl.ds(at, MB_TOK)], c),
    ]
    pending = {}
    for index, (name, source, target) in enumerate(moves):
        copy = pltpu.make_async_copy(source, target, in_sems.at[index])
        copy.start()
        pending.setdefault(name, []).append(copy)

    def need(*names):
        for name in names:
            for copy in pending.pop(name, []):
                copy.wait()

    leaving = []

    def leave(index):
        for which, slot in enumerate((sec, 1 - sec)):
            copy = pltpu.make_async_copy(results[index].at[slot], sent[index][which], out_sems.at[2 * index + which])
            copy.start()
            leaving.append(copy)

    outs, grads, early, inner, outer = results
    small[...] = jnp.zeros_like(small)
    for part, rows in zip((early, inner, outer), PARTS):
        if rows > FF:
            part[:, FF:, :] = jnp.zeros((2, rows - FF, D), BF16)
    weights = [
        (wide.at[b, :, 0 : 3 * D], wide.at[b, :, 3 * D : 4 * D], wide.at[b, :, 4 * D : 8 * D], deep.at[b])
        for b in range(2)
    ]
    sums = [(early.at[b], inner.at[b], outer.at[b]) for b in range(2)]

    def forward(b, source):
        forward_block(
            source, outs.at[b], vecs.at[b], taps.at[b], weights[b], kept[b], tables, forward_work, need
        )

    def backward(b, source):
        backward_block(
            source, grads.at[b], vecs.at[b], taps.at[b], weights[b], kept[b], tables, backward_work, sums[b], small
        )

    forward(0, x)
    feed[...] = outs[0].astype(BF16)
    forward(1, feed)
    leave(0)
    need("c")
    backward(1, c)
    feed[...] = grads[1].astype(BF16)
    backward(0, feed)
    for index in range(1, len(RESULTS)):
        leave(index)
    for copy in leaving:
        copy.wait()


def run_blocks(sec, *arrays):
    plain, turned = placement_tables()
    shifts, fence, lower = stripe_tables()
    tables = (
        jnp.asarray(plain, BF16),
        jnp.asarray(turned, BF16),
        jnp.asarray(plain.T, BF16),
        jnp.asarray(turned.T, BF16),
        jnp.asarray(shifts, BF16),
        jnp.asarray(fence, F32),
        jnp.asarray(lower, F32),
    )
    spaces = [pltpu.HBM] * 3 + [pltpu.VMEM, pltpu.HBM] * 3 + [pltpu.VMEM] + [pltpu.HBM] * 7
    smem = pl.BlockSpec(memory_space=pltpu.SMEM)
    scratch = INPUTS + RESULTS + SAVED + SAVED + FORWARD_WORK + BACKWARD_WORK + OTHER_WORK
    out_shape = [pltpu.VMEM(shape[1:], kind) for shape, kind in RESULTS for _ in range(2)]
    return pl.pallas_call(
        section_step,
        out_shape=out_shape,
        in_specs=[smem] + [pl.BlockSpec(memory_space=space) for space in spaces],
        out_specs=[pl.BlockSpec(memory_space=pl.ANY)] * len(out_shape),
        scratch_shapes=[pltpu.VMEM(shape, kind) for shape, kind in scratch]
        + [pltpu.SemaphoreType.DMA((17,)), pltpu.SemaphoreType.DMA((2 * len(RESULTS),))],
        compiler_params=pltpu.CompilerParams(vmem_limit_bytes=34 << 20),
        name="blocks",
    )(sec, *kept_in(arrays + tables, spaces))


NARROW = (((D, 3 * D), 0), ((D, D), 3 * D), ((D, FF), 4 * D), ((FF, D), None))


def narrowed(*refs):
    sources, (wide_out, deep_out), held, made, (in_sems, out_sems) = (
        refs[:4],
        refs[4:6],
        refs[6:10],
        refs[10:14],
        refs[14:],
    )
    coming = [pltpu.make_async_copy(sources[k], held[k], in_sems.at[k]) for k in range(4)]
    for copy in coming:
        copy.start()
    going = []
    for k, (shape, first) in enumerate(NARROW):
        coming[k].wait()
        made[k][...] = held[k][...].astype(BF16)
        target = deep_out if first is None else wide_out.at[:, pl.ds(first, shape[1])]
        copy = pltpu.make_async_copy(made[k], target, out_sems.at[k])
        copy.start()
        going.append(copy)
    for copy in going:
        copy.wait()


def run_narrowed(*weights):
    hbm = pl.BlockSpec(memory_space=pltpu.HBM)
    return pl.pallas_call(
        narrowed,
        out_shape=[pltpu.HBM((D, 8 * D), BF16), pltpu.HBM((FF, D), BF16)],
        in_specs=[hbm] * 4,
        out_specs=[hbm] * 2,
        scratch_shapes=[pltpu.VMEM(shape, F32) for shape, _ in NARROW]
        + [pltpu.VMEM(shape, BF16) for shape, _ in NARROW]
        + [pltpu.SemaphoreType.DMA((4,)), pltpu.SemaphoreType.DMA((4,))],
        compiler_params=pltpu.CompilerParams(vmem_limit_bytes=8 << 20),
        name="narrowed",
    )(*kept_in(weights, [pltpu.HBM] * 4))


def square_sum(a_ref, b_ref, c_ref, out_ref):
    total = jnp.zeros((8, D), F32)
    for ref in (a_ref, b_ref, c_ref):
        step = 64
        for start in range(0, ref.shape[0], step):
            rows = ref[start : start + step, :].astype(F32)
            square = rows * rows
            for at in range(0, step, 8):
                total = total + square[at : at + 8]
    total = jnp.sum(jnp.sum(total, axis=0, keepdims=True), axis=1, keepdims=True)
    out_ref[...] = jnp.broadcast_to(total, (8, HALF))


def run_square_sum(a, b, c):
    vmem = pl.BlockSpec(memory_space=pltpu.VMEM)
    return pl.pallas_call(
        square_sum,
        out_shape=jax.ShapeDtypeStruct((8, HALF), F32),
        in_specs=[vmem] * 3,
        out_specs=vmem,
        compiler_params=pltpu.CompilerParams(vmem_limit_bytes=16 << 20),
        name="squares",
    )(a, b, c)


def updated(grad, weight, moment, average, factor):
    decay = min(0.9999, (1.0 + STEP) / (10.0 + STEP))
    clipped = grad * factor
    direction = clipped + WEIGHT_DECAY * weight
    moment_new = MOMENTUM_DECAY * moment + direction
    weight_new = weight - LEARN_RATE * (direction + MOMENTUM_DECAY * moment_new)
    average_new = decay * average + (1.0 - decay) * weight_new
    return clipped, moment_new, weight_new, average_new


SHAPES = ((1, VEC), (1, 9 * D), (D, 3 * D), (D, D), (D, FF), (FF, D))
PIECES = (
    (3, 0, 128),
    (3, 128, 128),
    (2, 0, 128),
    (2, 128, 128),
    (4, 0, 128),
    (4, 128, 128),
    (5, 0, 256),
    (5, 256, 256),
    (5, 512, 256),
    (5, 768, 256),
)
OUT_SHAPES = [(shape, F32) for shape in SHAPES] * 4 + [(shape, BF16) for shape in SHAPES[2:]]
MOVES = 4 + 4 * 2 + 5 * len(PIECES)


def optimizer_step(sec_ref, *refs):
    def take(count):
        nonlocal refs
        taken, refs = refs[:count], refs[count:]
        return taken

    rows_in, (own, other), (a, b, c), states = take(4), take(2), take(3), take(18)
    outs, (norm_ref,), rows_out, made, (sems,) = take(28), take(1), take(2), take(28), take(1)
    sec = sec_ref[0]
    moves = []

    def leave(source, target):
        move = pltpu.make_async_copy(source, target, sems.at[len(moves)])
        move.start()
        moves.append(move)

    for index in range(4):
        first = pl.multiple_of((sec if index % 2 == 0 else 1 - sec) * MB_TOK, 8)
        leave(rows_in[index], rows_out[index // 2].at[pl.ds(first, MB_TOK)])
    norm = jnp.sqrt(own[0:1, 0:1] + other[0:1, 0:1])
    factor = jnp.minimum(1.0, CLIP_LIMIT / (norm + 1e-06))
    norm_ref[...] = norm

    def put(index, rows, lanes, grad):
        weight, moment, average = (states[kind * 6 + index][rows, lanes] for kind in range(3))
        new = updated(grad, weight, moment, average, factor)
        for kind in range(4):
            made[kind * 6 + index][rows, lanes] = new[kind]
        if index >= 2:
            made[24 + index - 2][rows, lanes] = new[2].astype(BF16)

    places = {2: [(a, 0), (a, D), (a, 2 * D)], 3: [(a, 3 * D)], 4: [(b, part * D) for part in range(4)], 5: [(c, 0)]}
    step = 32
    for index, first, count in PIECES:
        for row in range(first, first + count, step):
            for part, (ref, base) in enumerate(places[index]):
                grad = ref[base + row : base + row + step, :].astype(F32)
                put(index, slice(row, row + step), slice(part * D, (part + 1) * D), grad)
        rows = pl.ds(first, count)
        for kind in range(5):
            at = kind * 6 + index if kind < 4 else 24 + index - 2
            leave(made[at].at[rows], outs[at].at[rows])
    rows = c[FF : FF + 32, :].astype(F32)
    whole = slice(0, 1)
    for part in range(13):
        put(0, whole, slice(part * D, (part + 1) * D), rows[part : part + 1, :])
    for part in range(9):
        put(1, whole, slice(part * D, (part + 1) * D), rows[13 + part : 14 + part, :])
    for index in range(2):
        for kind in range(4):
            leave(made[kind * 6 + index], outs[kind * 6 + index])
    for move in moves:
        move.wait()


def run_optimizer(sec, rows_in, own, other, a, b, c, states):
    vmem = pl.BlockSpec(memory_space=pltpu.VMEM)
    hbm = pl.BlockSpec(memory_space=pltpu.HBM)
    return pl.pallas_call(
        optimizer_step,
        out_shape=[pltpu.HBM(shape, kind) for shape, kind in OUT_SHAPES]
        + [jax.ShapeDtypeStruct((1, 1), F32)]
        + [pltpu.HBM((2 * MB_TOK, D), F32)] * 2,
        in_specs=[pl.BlockSpec(memory_space=pltpu.SMEM)] + [vmem] * (4 + 2 + 3 + 18),
        out_specs=[hbm] * 28 + [vmem] + [hbm] * 2,
        scratch_shapes=[pltpu.VMEM(shape, kind) for shape, kind in OUT_SHAPES] + [pltpu.SemaphoreType.DMA((MOVES,))],
        compiler_params=pltpu.CompilerParams(vmem_limit_bytes=20 << 20),
        name="optimizer",
    )(sec, *kept_in((*rows_in, own, other, a, b, c, *states), [pltpu.VMEM] * 27))


def swapped(value):
    return lax.ppermute(value, "section", [(0, 1), (1, 0)])


def exchange_orders(bits):
    if bits == 4:
        return ((0, 1, 2, 3), (1, 2, 0, 3), (2, 0, 1, 3))
    turn = max(1, bits // 3)
    every = tuple(range(bits))
    return tuple(every[turn * part :] + every[: turn * part] for part in range(3))


def exchanged(value, bit, size):
    return lax.ppermute(value, "dp", [(index, index ^ (1 << bit)) for index in range(size)])


def exchange_bits():
    size = lax.axis_size("dp")
    bits = size.bit_length() - 1
    if size < 2 or size != 1 << bits or any(2 * rows % size for rows in PARTS):
        return []
    index = lax.axis_index("dp")
    return [((index >> bit) & 1) == 0 for bit in range(bits)]


def summed_over_dp(parts, clear):
    size = lax.axis_size("dp")
    bits = len(clear)
    if not bits:
        return [lax.psum(part.astype(F32), "dp").astype(BF16) for part in parts]
    orders = exchange_orders(bits)
    shapes = [part.shape for part in parts]
    held = [part.reshape((2,) * (bits - 1) + (2 * part.shape[0] // size, D)) for part in parts]
    for step in range(bits):
        kept, came = held, []
        if step < bits - 1:
            kept = [jnp.where(clear[order[step]], value[0], value[1]) for value, order in zip(held, orders)]
            held = [jnp.where(clear[order[step]], value[1], value[0]) for value, order in zip(held, orders)]
        came = [exchanged(value, order[step], size) for value, order in zip(held, orders)]
        held = [(a.astype(F32) + b.astype(F32)).astype(BF16) for a, b in zip(kept, came)]
    for step in reversed(range(bits - 1)):
        grown = []
        for value, order in zip(held, orders):
            low = clear[order[step]]
            came = exchanged(value, order[step], size)
            grown.append(jnp.stack([jnp.where(low, value, came), jnp.where(low, came, value)]))
        held = grown
    return [value.reshape(shape) for value, shape in zip(held, shapes)]


def per_device(inputs, cotangent, *states):
    states = [array.reshape(1, 9 * D) if array.shape == (1, 9, D) else array for array in states]
    states = [array.reshape(array.shape[1:]) if array.ndim == 3 else array for array in states]
    vectors, kernels = states[:2]
    section = lax.axis_index("section").astype(jnp.int32).reshape(1)
    section, *clear = lax.optimization_barrier((section, *exchange_bits()))
    wide, deep = run_narrowed(*states[2:6])
    results = run_blocks(
        section,
        inputs,
        cotangent,
        vectors,
        swapped(vectors),
        kernels,
        swapped(kernels),
        wide,
        swapped(wide),
        deep,
        swapped(deep),
    )
    totals = [
        (own.astype(F32) + swapped(other).astype(F32)).astype(BF16)
        for own, other in zip(results[4::2], results[5::2])
    ]
    a, b, c = summed_over_dp(totals, clear)
    squares = run_square_sum(a, b, c)
    rows_in = (results[0], swapped(results[1]), results[2], swapped(results[3]))
    new = run_optimizer(section, rows_in, squares, swapped(squares), a, b, c, states)

    def whole(arrays):
        return [
            array if array.shape == (1, VEC) else array.reshape(1, 9, D) if array.shape == (1, 9 * D) else array[None]
            for array in arrays
        ]

    return (new[29][None], new[30][None], *whole(new[0:6]), new[28].reshape(()), *whole(new[6:28]))


def solution(mesh):
    rows = P("dp", None)
    state = (P("section", None),) + (P("section", None, None),) * 5
    return jax.shard_map(
        per_device,
        mesh=mesh,
        in_specs=(rows, rows) + state * 3,
        out_specs=(P("section", "dp", None),) * 2 + state + (P(),) + state * 3 + state[2:],
        check_vma=False,
    )
```

```python
import jax
import jax.numpy as jnp
import numpy as np
from jax import lax
from jax.experimental import pallas as pl
from jax.experimental.pallas import tpu as pltpu
from jax.sharding import PartitionSpec as P

D = 256
HALF = 128
HEADS = 8
HEAD = 32
FF = 1024
BIG_SIDE = 14
SMALL_SIDE = 6
BIG_MB = 1
SMALL_MB = 3
STEP = 8
MB_TOK = 304
VEC = 3328

NORM_EPS = 1e-05
CLIP_LIMIT = 5.0
LEARN_RATE = 4.0
MOMENTUM_DECAY = 0.9
WEIGHT_DECAY = 5e-05

F32 = jnp.float32
BF16 = jnp.bfloat16

GROUP = 128
WINDOWS = ((0, BIG_SIDE, 0, 112), (112, BIG_SIDE, 0, 84), (192, SMALL_SIDE, 4, 108))
NGROUP = len(WINDOWS)
LONG_TOK = 320
SCALE = HEAD ** -0.5
LOG2E = 1.4426950408889634
EXP_SCALE = SCALE * LOG2E
OFF = -1e30
ROWS = ((0, 80), (80, 80), (160, 80), (240, 64))
PARTS = (1024, 1024, 1088)


def turned_table():
    turned = np.zeros((MB_TOK, MB_TOK), np.float32)
    base = 0
    for side, count in ((BIG_SIDE, BIG_MB), (SMALL_SIDE, SMALL_MB)):
        for _ in range(count):
            for row in range(side):
                for col in range(side):
                    turned[base + row * side + col, base + col * side + row] = 1.0
            base += side * side
    return turned


def stripe_tables():
    shifts = np.zeros((NGROUP, 5 * GROUP, GROUP), np.float32)
    fence = np.full((NGROUP, GROUP, GROUP), OFF, np.float32)
    lower = np.zeros((NGROUP, GROUP, HALF), np.float32)
    for kind, (_, side, first, size) in enumerate(WINDOWS):
        stripe = 2 * side
        number = (np.arange(GROUP) - first) // stripe
        number[:first] = -1
        number[first + size :] = GROUP
        fence[kind][number[:, None] == number[None, :]] = 0.0
        for at in range(size):
            own, inner = divmod(at, stripe)
            row, col = divmod(inner, side)
            lower[kind, first + at, :] = float(row)
            moves = ((row, col - 1), (row, col + 1), (1 - row, col - 1), (1 - row, col), (1 - row, col + 1))
            for move, (to_row, to_col) in enumerate(moves):
                if 0 <= to_col < side:
                    target = first + own * stripe + to_row * side + to_col
                    shifts[kind, move * GROUP + first + at, target] = 1.0
    return shifts, fence, lower


def kept_in(arrays, spaces):
    return [pltpu.with_memory_space_constraint(array, space) for array, space in zip(arrays, spaces)]


def dot(a, b):
    return jnp.dot(a, b, preferred_element_type=F32)


def dot_nt(a, b):
    return lax.dot_general(a, b, (((1,), (1,)), ((), ())), preferred_element_type=F32)


def dot_tn(a, b):
    return lax.dot_general(a, b, (((0,), (0,)), ((), ())), preferred_element_type=F32)


def head_masks():
    lane = lax.broadcasted_iota(jnp.int32, (1, HALF), 1) // HEAD
    return [(lane == head).astype(BF16) for head in range(HEADS // 2)]


def stacked_heads(rows, masks):
    return jnp.concatenate([rows * mask for mask in masks], axis=0)


def picked_heads(product):
    return jnp.concatenate(
        [
            product[HEAD * head : HEAD * (head + 1), GROUP * head : GROUP * (head + 1)]
            for head in range(HEADS // 2)
        ],
        axis=0,
    )


def turned_taps(taps):
    turned = [3 * (index % 3) + index // 3 for index in range(9)]
    return [
        jnp.concatenate(
            [taps[:, index * D : index * D + HALF], taps[:, turned[index] * D + HALF : (turned[index] + 1) * D]],
            axis=1,
        )
        for index in range(9)
    ]


def norm_forward(x, gain, offset):
    centre = x - jnp.mean(x, axis=-1, keepdims=True)
    spread = jnp.mean(centre * centre, axis=-1, keepdims=True)
    scale = lax.rsqrt(spread + NORM_EPS)
    hat = centre * scale
    return hat, scale, hat * gain + offset


def norm_backward(grad, hat, scale, gain):
    inner = grad * gain
    mean_inner = jnp.mean(inner, axis=-1, keepdims=True)
    mean_cross = jnp.mean(inner * hat, axis=-1, keepdims=True)
    return scale * (inner - mean_inner - hat * mean_cross)


def column_sum(x):
    return jnp.sum(x.astype(F32), axis=0, keepdims=True)


def window(group):
    return pl.ds(WINDOWS[group][0], GROUP)


def put_window(ref, group, value):
    if group == 0:
        ref[0:112, :] = value[0:112].astype(BF16)
    elif group == 1:
        ref[112:208, :] = value[0:96].astype(BF16)
    else:
        before = lax.broadcasted_iota(jnp.int32, (16, value.shape[1]), 0) < 4
        ref[192:208, :] = jnp.where(before, ref[192:208, :].astype(F32), value[0:16]).astype(BF16)
        ref[208:304, :] = value[16:112].astype(BF16)


def vec_at(vec, index, width=1):
    return vec[:, index * D : (index + width) * D]


def forward_block(x_ref, out_ref, vec_ref, taps_ref, w, saved, tables, work, need):
    wq, wp, w1, w2 = w
    (hat1, scale1, normed, qkv, probs, probs_low, mixed, hat2, scale2, normed2, slope, activ) = saved
    turned, shifts, fence, lower = tables
    mixed_att, middle, hidden, flipped, local = work
    need("x", "vec")
    vec = vec_ref[...]
    for start, size in ROWS:
        rows = pl.ds(start, size)
        hat, scale, y = norm_forward(x_ref[rows, :].astype(F32), vec_at(vec, 0), vec_at(vec, 2))
        hat1[rows, :] = hat
        scale1[rows, :] = jnp.broadcast_to(scale, (size, HALF))
        normed[0, rows, :] = y.astype(BF16)
    need("place", "wide")
    normed[1] = dot(turned[...], normed[0]).astype(BF16)
    biases = (vec_at(vec, 4), None, vec_at(vec, 5))
    for half in range(2):
        lanes = slice(half * HALF, (half + 1) * HALF)
        for part in range(3):
            got = dot(normed[half], wq[:, part * D + half * HALF : part * D + (half + 1) * HALF])
            if biases[part] is not None:
                got = got + biases[part][:, lanes]
            qkv[part, 0:MB_TOK, lanes] = got.astype(BF16)
    masks = head_masks()
    need("stripe")
    taps9 = turned_taps(taps_ref[...])
    bias = vec_at(vec, 7)
    units = [(group, half) for group in range(NGROUP) for half in range(2)]
    for unit, (group, half) in enumerate(units):
        rows = window(group)
        lanes = slice(half * HALF, (half + 1) * HALF)
        probs[unit] = dot_nt(qkv[1, rows, lanes], stacked_heads(qkv[0, rows, lanes], masks))
        flipped[unit] = qkv[2, rows, lanes].T
    for unit, (group, half) in enumerate(units):
        fenced = fence[group]
        for head in range(HEADS // 2):
            cols = slice(head * GROUP, (head + 1) * GROUP)
            s = probs[unit, :, cols] + fenced
            p = jnp.exp2((s - jnp.max(s, axis=0, keepdims=True)) * EXP_SCALE)
            p = p * (1.0 / jnp.sum(p, axis=0, keepdims=True))
            probs[unit, :, cols] = p
            probs_low[unit, :, cols] = p.astype(BF16)
    for group in range(NGROUP):
        rows = window(group)
        v = qkv[2, rows, :]
        moved = dot(shifts[group], v)
        low_row = lower[group] > 0.5
        low_row = jnp.concatenate([low_row, low_row], axis=1)
        lepe = bias + taps9[4] * v.astype(F32)
        lepe = lepe + taps9[3] * moved[0:GROUP] + taps9[5] * moved[GROUP : 2 * GROUP]
        for step in range(3):
            tap = jnp.where(low_row, taps9[step], taps9[6 + step])
            lepe = lepe + tap * moved[(2 + step) * GROUP : (3 + step) * GROUP]
        local[group] = lepe
    for unit, (group, half) in enumerate(units):
        rows = window(group)
        lanes = slice(half * HALF, (half + 1) * HALF)
        attended = picked_heads(dot(flipped[unit], probs_low[unit])).T
        put_window(mixed_att.at[half], group, attended + local[group, :, lanes])
    mixed[:, :HALF] = mixed_att[0]
    mixed[:, HALF:] = dot(turned[...], mixed_att[1]).astype(BF16)
    middle[...] = dot(mixed[...], wp[...])
    for start, size in ROWS:
        rows = pl.ds(start, size)
        mid = x_ref[rows, :].astype(F32) + middle[rows, :] + vec_at(vec, 6)
        middle[rows, :] = mid
        hat, scale, y = norm_forward(mid, vec_at(vec, 1), vec_at(vec, 3))
        hat2[rows, :] = hat
        scale2[rows, :] = jnp.broadcast_to(scale, (size, HALF))
        normed2[rows, :] = y.astype(BF16)
    hidden[...] = dot(normed2[...], w1[...])
    for start, size in ROWS:
        rows = pl.ds(start, size)
        for part in range(4):
            cols = slice(part * D, (part + 1) * D)
            h = hidden[rows, cols] + vec_at(vec, 9 + part)
            cdf = 0.5 * (1.0 + lax.erf(h * 0.7071067811865476))
            pdf = 0.3989422804014327 * jnp.exp(-0.5 * h * h)
            activ[rows, cols] = (h * cdf).astype(BF16)
            slope[rows, cols] = cdf + h * pdf
    need("deep")
    out_ref[...] = dot(activ[...], w2[...])
    for start, size in ROWS:
        rows = pl.ds(start, size)
        out_ref[rows, :] = out_ref[rows, :] + middle[rows, :] + vec_at(vec, 8)


def backward_block(up_ref, grad_ref, vec_ref, taps_ref, w, saved, tables, work, sums, small):
    wq, wp, w1, w2 = w
    (hat1, scale1, normed, qkv, probs, probs_low, mixed, hat2, scale2, normed2, slope, activ) = saved
    turned, shifts, fence, lower = tables
    branch, gact, ghid, gmid, gmix, dqkv, dnat, gnorm, gprobs, gscores, flipped, local = work
    early, inner, outer = sums
    vec = vec_ref[...]
    branch[...] = up_ref[...].astype(BF16)
    outer[0:FF, :] = dot_tn(activ[...], branch[...]).astype(BF16)
    sums = column_sum(branch[...])
    small[8:9, :] = sums
    gact[...] = dot_nt(branch[...], w2[...])
    parts = [jnp.zeros((1, D), F32) for _ in range(4)]
    for start, size in ROWS:
        rows = pl.ds(start, size)
        for part in range(4):
            cols = slice(part * D, (part + 1) * D)
            low = (gact[rows, cols] * slope[rows, cols]).astype(BF16)
            ghid[rows, cols] = low
            parts[part] = parts[part] + column_sum(low)
    for part in range(4):
        small[9 + part : 10 + part, :] = parts[part]
    for part in range(4):
        inner[part * D : (part + 1) * D, :] = dot_tn(
            normed2[...], ghid[:, part * D : (part + 1) * D]
        ).astype(BF16)
    gnorm[...] = dot_nt(ghid[...], w1[...])
    gains, offsets, outs = (jnp.zeros((1, D), F32) for _ in range(3))
    for start, size in ROWS:
        rows = pl.ds(start, size)
        g = gnorm[rows, :]
        hat = hat2[rows, :]
        scale = scale2[rows, :]
        gains = gains + column_sum(g * hat)
        offsets = offsets + column_sum(g)
        full = jnp.concatenate([scale, scale], axis=1)
        total = up_ref[rows, :].astype(F32) + norm_backward(g, hat, full, vec_at(vec, 1))
        gmid[rows, :] = total
        low = total.astype(BF16)
        branch[rows, :] = low
        outs = outs + column_sum(low)
    small[1:2, :] = gains
    small[3:4, :] = offsets
    small[6:7, :] = outs
    early[3 * D : 4 * D, :] = dot_tn(mixed[...], branch[...]).astype(BF16)
    low = dot_nt(branch[...], wp[...]).astype(BF16)
    small[7:8, :] = column_sum(low)
    gmix[0:MB_TOK, :HALF] = low[:, :HALF]
    gmix[0:MB_TOK, HALF:] = dot(turned[...], low[:, HALF:]).astype(BF16)
    masks = head_masks()
    taps9 = turned_taps(taps_ref[...])
    tap_sums = [jnp.zeros((1, D), F32) for _ in range(9)]
    for start, size in ROWS:
        rows = pl.ds(start, size)
        tap_sums[4] = tap_sums[4] + column_sum(qkv[2, rows, :].astype(F32) * gmix[rows, :].astype(F32))
    units = [(group, half) for group in range(NGROUP) for half in range(2)]
    for unit, (group, half) in enumerate(units):
        rows = window(group)
        lanes = slice(half * HALF, (half + 1) * HALF)
        gprobs[unit] = dot_nt(qkv[2, rows, lanes], stacked_heads(gmix[rows, lanes], masks))
        flipped[unit] = qkv[1, rows, lanes].T
    for unit in range(len(units)):
        for head in range(HEADS // 2):
            cols = slice(head * GROUP, (head + 1) * GROUP)
            p = probs[unit, :, cols]
            gp = gprobs[unit, :, cols]
            down = jnp.sum(gp * p, axis=0, keepdims=True)
            gscores[unit, :, cols] = (p * (gp - down)).astype(BF16)
    for group in range(NGROUP):
        rows = window(group)
        g_low = gmix[rows, :]
        moved = dot(shifts[group], g_low)
        low_row = lower[group] > 0.5
        low_row = jnp.concatenate([low_row, low_row], axis=1)
        v32 = qkv[2, rows, :].astype(F32)
        g32 = g_low.astype(F32)
        left, right = moved[0:GROUP], moved[GROUP : 2 * GROUP]
        lepe = taps9[4] * g32 + taps9[3] * right + taps9[5] * left
        tap_sums[3] = tap_sums[3] + column_sum(v32 * right)
        tap_sums[5] = tap_sums[5] + column_sum(v32 * left)
        for step in range(3):
            at = moved[(4 - step) * GROUP : (5 - step) * GROUP]
            lepe = lepe + jnp.where(low_row, taps9[6 + step], taps9[step]) * at
            product = v32 * at
            tap_sums[6 + step] = tap_sums[6 + step] + column_sum(jnp.where(low_row, product, 0.0))
            tap_sums[step] = tap_sums[step] + column_sum(jnp.where(low_row, 0.0, product))
        local[group] = lepe
    for unit, (group, half) in enumerate(units):
        rows = window(group)
        lanes = slice(half * HALF, (half + 1) * HALF)
        low_s = gscores[unit]
        grad_v = dot(probs_low[unit], stacked_heads(gmix[rows, lanes], masks)) + local[group, :, lanes]
        grad_k = dot(low_s, stacked_heads(qkv[0, rows, lanes], masks)) * SCALE
        grad_q = picked_heads(dot(flipped[unit], low_s)).T * SCALE
        put_window(dqkv.at[half], group, jnp.concatenate([grad_q, grad_k, grad_v], axis=1))
    for index in range(9):
        tap = index
        turned_index = 3 * (index % 3) + index // 3
        small[13 + index : 14 + index, :] = jnp.concatenate(
            [tap_sums[tap][:, :HALF], tap_sums[turned_index][:, HALF:]], axis=1
        )
    for half in range(2):
        lanes = slice(half * HALF, (half + 1) * HALF)
        both = dqkv[half]
        small[4:5, lanes] = column_sum(both[:, 0:HALF])
        small[5:6, lanes] = column_sum(both[:, D : 3 * HALF])
        grads = dot_tn(normed[half], both)
        for part in range(3):
            early[part * D : (part + 1) * D, lanes] = grads[:, part * HALF : (part + 1) * HALF].astype(BF16)
        natural = both if half == 0 else dot(turned[...], both).astype(BF16)
        for part in range(3):
            dnat[:, part * D + half * HALF : part * D + (half + 1) * HALF] = natural[
                :, part * HALF : (part + 1) * HALF
            ]
    gnorm[...] = dot_nt(dnat[...], wq[...])
    gains, offsets = (jnp.zeros((1, D), F32) for _ in range(2))
    for start, size in ROWS:
        rows = pl.ds(start, size)
        g = gnorm[rows, :]
        hat = hat1[rows, :]
        scale = scale1[rows, :]
        gains = gains + column_sum(g * hat)
        offsets = offsets + column_sum(g)
        full = jnp.concatenate([scale, scale], axis=1)
        grad_ref[rows, :] = gmid[rows, :] + norm_backward(g, hat, full, vec_at(vec, 0))
    small[0:1, :] = gains
    small[2:3, :] = offsets
    outer[FF : FF + 32, :] = small[...].astype(BF16)


SAVED = [
    ((MB_TOK, D), F32),
    ((MB_TOK, HALF), F32),
    ((2, MB_TOK, D), BF16),
    ((3, LONG_TOK, D), BF16),
    ((2 * NGROUP, GROUP, 4 * GROUP), F32),
    ((2 * NGROUP, GROUP, 4 * GROUP), BF16),
    ((MB_TOK, D), BF16),
    ((MB_TOK, D), F32),
    ((MB_TOK, HALF), F32),
    ((MB_TOK, D), BF16),
    ((MB_TOK, FF), F32),
    ((MB_TOK, FF), BF16),
]
FORWARD_WORK = [
    ((2, MB_TOK, HALF), BF16),
    ((MB_TOK, D), F32),
    ((MB_TOK, FF), F32),
    ((2 * NGROUP, GROUP, GROUP), BF16),
    ((NGROUP, GROUP, D), F32),
]
BACKWARD_WORK = [
    ((MB_TOK, D), BF16),
    ((MB_TOK, FF), F32),
    ((MB_TOK, FF), BF16),
    ((MB_TOK, D), F32),
    ((LONG_TOK, D), BF16),
    ((2, MB_TOK, 3 * HALF), BF16),
    ((MB_TOK, 3 * D), BF16),
    ((MB_TOK, D), F32),
    ((2 * NGROUP, GROUP, 4 * GROUP), F32),
    ((2 * NGROUP, GROUP, 4 * GROUP), BF16),
    ((2 * NGROUP, GROUP, GROUP), BF16),
    ((NGROUP, GROUP, D), F32),
]


INPUTS = [
    ((MB_TOK, D), BF16),
    ((MB_TOK, D), BF16),
    ((2, 1, VEC), F32),
    ((2, 1, 9 * D), F32),
    ((2, D, 8 * D), BF16),
    ((2, FF, D), BF16),
    ((MB_TOK, MB_TOK), BF16),
    ((NGROUP, 5 * GROUP, GROUP), BF16),
    ((NGROUP, GROUP, GROUP), F32),
    ((NGROUP, GROUP, HALF), F32),
]
RESULTS = [((2, MB_TOK, D), F32), ((2, MB_TOK, D), F32)] + [((2, rows, D), BF16) for rows in PARTS]
OTHER_WORK = [((MB_TOK, D), BF16), ((32, D), F32)]


def section_step(sec_ref, *refs):
    def take(count):
        nonlocal refs
        taken, refs = refs[:count], refs[count:]
        return taken

    x_in, c_in, vec_own, vec_other, ker_own, ker_other, wide_own, wide_other, deep_own, deep_other = take(10)
    table_in = take(4)
    sent = [take(2) for _ in RESULTS]
    held = take(len(INPUTS))
    results = take(len(RESULTS))
    kept = (take(len(SAVED)), take(len(SAVED)))
    forward_work = take(len(FORWARD_WORK))
    backward_work = take(len(BACKWARD_WORK))
    feed, small, in_sems, out_sems = refs
    x, c, vecs, taps, wide, deep = held[:6]
    tables = held[6:]
    sec = sec_ref[0]
    at = pl.multiple_of(sec * MB_TOK, 16)
    moves = [
        ("x", x_in.at[pl.ds(at, MB_TOK)], x),
        ("vec", vec_own, vecs.at[sec]),
        ("vec", vec_other, vecs.at[1 - sec]),
        ("place", table_in[0], tables[0]),
        ("wide", wide_own, wide.at[sec]),
        ("wide", wide_other, wide.at[1 - sec]),
        ("stripe", table_in[1], tables[1]),
        ("stripe", table_in[2], tables[2]),
        ("stripe", table_in[3], tables[3]),
        ("stripe", ker_own, taps.at[sec]),
        ("stripe", ker_other, taps.at[1 - sec]),
        ("deep", deep_own, deep.at[sec]),
        ("deep", deep_other, deep.at[1 - sec]),
        ("c", c_in.at[pl.ds(at, MB_TOK)], c),
    ]
    pending = {}
    for index, (name, source, target) in enumerate(moves):
        copy = pltpu.make_async_copy(source, target, in_sems.at[index])
        copy.start()
        pending.setdefault(name, []).append(copy)

    def need(*names):
        for name in names:
            for copy in pending.pop(name, []):
                copy.wait()

    leaving = []

    def leave(index):
        for which, slot in enumerate((sec, 1 - sec)):
            copy = pltpu.make_async_copy(results[index].at[slot], sent[index][which], out_sems.at[2 * index + which])
            copy.start()
            leaving.append(copy)

    outs, grads, early, inner, outer = results
    small[...] = jnp.zeros_like(small)
    for b in range(2):
        kept[b][3][:, MB_TOK:, :] = jnp.zeros((3, LONG_TOK - MB_TOK, D), BF16)
    backward_work[4][MB_TOK:, :] = jnp.zeros((LONG_TOK - MB_TOK, D), BF16)
    for part, rows in zip((early, inner, outer), PARTS):
        if rows > FF:
            part[:, FF:, :] = jnp.zeros((2, rows - FF, D), BF16)
    weights = [
        (wide.at[b, :, 0 : 3 * D], wide.at[b, :, 3 * D : 4 * D], wide.at[b, :, 4 * D : 8 * D], deep.at[b])
        for b in range(2)
    ]
    sums = [(early.at[b], inner.at[b], outer.at[b]) for b in range(2)]

    def forward(b, source):
        forward_block(
            source, outs.at[b], vecs.at[b], taps.at[b], weights[b], kept[b], tables, forward_work, need
        )

    def backward(b, source):
        backward_block(
            source, grads.at[b], vecs.at[b], taps.at[b], weights[b], kept[b], tables, backward_work, sums[b], small
        )

    forward(0, x)
    feed[...] = outs[0].astype(BF16)
    forward(1, feed)
    leave(0)
    need("c")
    backward(1, c)
    feed[...] = grads[1].astype(BF16)
    backward(0, feed)
    for index in range(1, len(RESULTS)):
        leave(index)
    for copy in leaving:
        copy.wait()


def run_blocks(sec, *arrays):
    shifts, fence, lower = stripe_tables()
    tables = (
        jnp.asarray(turned_table(), BF16),
        jnp.asarray(shifts, BF16),
        jnp.asarray(fence, F32),
        jnp.asarray(lower, F32),
    )
    spaces = [pltpu.HBM] * 3 + [pltpu.VMEM, pltpu.HBM] + [pltpu.VMEM] * 5 + [pltpu.HBM] * 4
    smem = pl.BlockSpec(memory_space=pltpu.SMEM)
    scratch = INPUTS + RESULTS + SAVED + SAVED + FORWARD_WORK + BACKWARD_WORK + OTHER_WORK
    out_shape = [pltpu.VMEM(shape[1:], kind) for shape, kind in RESULTS for _ in range(2)]
    return pl.pallas_call(
        section_step,
        out_shape=out_shape,
        in_specs=[smem] + [pl.BlockSpec(memory_space=space) for space in spaces],
        out_specs=[pl.BlockSpec(memory_space=pl.ANY)] * len(out_shape),
        scratch_shapes=[pltpu.VMEM(shape, kind) for shape, kind in scratch]
        + [pltpu.SemaphoreType.DMA((14,)), pltpu.SemaphoreType.DMA((2 * len(RESULTS),))],
        compiler_params=pltpu.CompilerParams(vmem_limit_bytes=34 << 20),
        name="blocks",
    )(sec, *kept_in(arrays + tables, spaces))


NARROW = (((D, 3 * D), 0), ((D, D), 3 * D), ((D, FF), 4 * D), ((FF, D), None))


def narrowed(*refs):
    sources, (wide, deep), held, (sems,) = refs[:4], refs[4:6], refs[6:10], refs[10:]
    coming = [pltpu.make_async_copy(sources[k], held[k], sems.at[k]) for k in range(4)]
    for copy in coming:
        copy.start()
    for k, (shape, first) in enumerate(NARROW):
        coming[k].wait()
        if first is None:
            deep[...] = held[k][...].astype(BF16)
        else:
            wide[:, first : first + shape[1]] = held[k][...].astype(BF16)


def run_narrowed(*weights):
    vmem = pl.BlockSpec(memory_space=pltpu.VMEM)
    return pl.pallas_call(
        narrowed,
        out_shape=[pltpu.VMEM((D, 8 * D), BF16), pltpu.VMEM((FF, D), BF16)],
        in_specs=[pl.BlockSpec(memory_space=pltpu.HBM)] * 4,
        out_specs=[vmem] * 2,
        scratch_shapes=[pltpu.VMEM(shape, F32) for shape, _ in NARROW] + [pltpu.SemaphoreType.DMA((4,))],
        compiler_params=pltpu.CompilerParams(vmem_limit_bytes=8 << 20),
        name="narrowed",
    )(*kept_in(weights, [pltpu.HBM] * 4))


def square_sum(a_ref, b_ref, c_ref, out_ref):
    total = jnp.zeros((8, D), F32)
    for ref in (a_ref, b_ref, c_ref):
        step = 64
        for start in range(0, ref.shape[0], step):
            rows = ref[start : start + step, :].astype(F32)
            square = rows * rows
            for at in range(0, step, 8):
                total = total + square[at : at + 8]
    total = jnp.sum(jnp.sum(total, axis=0, keepdims=True), axis=1, keepdims=True)
    out_ref[...] = jnp.broadcast_to(total, (8, HALF))


def run_square_sum(a, b, c):
    vmem = pl.BlockSpec(memory_space=pltpu.VMEM)
    return pl.pallas_call(
        square_sum,
        out_shape=jax.ShapeDtypeStruct((8, HALF), F32),
        in_specs=[vmem] * 3,
        out_specs=vmem,
        compiler_params=pltpu.CompilerParams(vmem_limit_bytes=16 << 20),
        name="squares",
    )(a, b, c)


def updated(grad, weight, moment, average, factor):
    decay = min(0.9999, (1.0 + STEP) / (10.0 + STEP))
    clipped = grad * factor
    direction = clipped + WEIGHT_DECAY * weight
    moment_new = MOMENTUM_DECAY * moment + direction
    weight_new = weight - LEARN_RATE * (direction + MOMENTUM_DECAY * moment_new)
    average_new = decay * average + (1.0 - decay) * weight_new
    return clipped, moment_new, weight_new, average_new


SHAPES = ((1, VEC), (1, 9 * D), (D, 3 * D), (D, D), (D, FF), (FF, D))
PIECES = (
    (3, 0, 128),
    (3, 128, 128),
    (2, 0, 128),
    (2, 128, 128),
    (4, 0, 128),
    (4, 128, 128),
    (5, 0, 256),
    (5, 256, 256),
    (5, 512, 256),
    (5, 768, 256),
)
OUT_SHAPES = [(shape, F32) for shape in SHAPES] * 4 + [(shape, BF16) for shape in SHAPES[2:]]
MOVES = 4 + 4 * 2 + 5 * len(PIECES)


def optimizer_step(sec_ref, *refs):
    def take(count):
        nonlocal refs
        taken, refs = refs[:count], refs[count:]
        return taken

    rows_in, (own, other), (a, b, c), states = take(4), take(2), take(3), take(18)
    outs, (norm_ref,), rows_out, made, (sems,) = take(28), take(1), take(2), take(28), take(1)
    sec = sec_ref[0]
    moves = []

    def leave(source, target):
        move = pltpu.make_async_copy(source, target, sems.at[len(moves)])
        move.start()
        moves.append(move)

    for index in range(4):
        first = pl.multiple_of((sec if index % 2 == 0 else 1 - sec) * MB_TOK, 8)
        leave(rows_in[index], rows_out[index // 2].at[pl.ds(first, MB_TOK)])
    norm = jnp.sqrt(own[0:1, 0:1] + other[0:1, 0:1])
    factor = jnp.minimum(1.0, CLIP_LIMIT / (norm + 1e-06))
    norm_ref[...] = norm

    def put(index, rows, lanes, grad):
        weight, moment, average = (states[kind * 6 + index][rows, lanes] for kind in range(3))
        new = updated(grad, weight, moment, average, factor)
        for kind in range(4):
            made[kind * 6 + index][rows, lanes] = new[kind]
        if index >= 2:
            made[24 + index - 2][rows, lanes] = new[2].astype(BF16)

    places = {2: [(a, 0), (a, D), (a, 2 * D)], 3: [(a, 3 * D)], 4: [(b, part * D) for part in range(4)], 5: [(c, 0)]}
    step = 32
    for index, first, count in PIECES:
        for row in range(first, first + count, step):
            for part, (ref, base) in enumerate(places[index]):
                grad = ref[base + row : base + row + step, :].astype(F32)
                put(index, slice(row, row + step), slice(part * D, (part + 1) * D), grad)
        rows = pl.ds(first, count)
        for kind in range(5):
            at = kind * 6 + index if kind < 4 else 24 + index - 2
            leave(made[at].at[rows], outs[at].at[rows])
    rows = c[FF : FF + 32, :].astype(F32)
    whole = slice(0, 1)
    for part in range(13):
        put(0, whole, slice(part * D, (part + 1) * D), rows[part : part + 1, :])
    for part in range(9):
        put(1, whole, slice(part * D, (part + 1) * D), rows[13 + part : 14 + part, :])
    for index in range(2):
        for kind in range(4):
            leave(made[kind * 6 + index], outs[kind * 6 + index])
    for move in moves:
        move.wait()


def run_optimizer(sec, rows_in, own, other, a, b, c, states):
    vmem = pl.BlockSpec(memory_space=pltpu.VMEM)
    hbm = pl.BlockSpec(memory_space=pltpu.HBM)
    return pl.pallas_call(
        optimizer_step,
        out_shape=[pltpu.HBM(shape, kind) for shape, kind in OUT_SHAPES]
        + [jax.ShapeDtypeStruct((1, 1), F32)]
        + [pltpu.HBM((2 * MB_TOK, D), F32)] * 2,
        in_specs=[pl.BlockSpec(memory_space=pltpu.SMEM)] + [vmem] * (4 + 2 + 3 + 18),
        out_specs=[hbm] * 28 + [vmem] + [hbm] * 2,
        scratch_shapes=[pltpu.VMEM(shape, kind) for shape, kind in OUT_SHAPES] + [pltpu.SemaphoreType.DMA((MOVES,))],
        compiler_params=pltpu.CompilerParams(vmem_limit_bytes=20 << 20),
        name="optimizer",
    )(sec, *kept_in((*rows_in, own, other, a, b, c, *states), [pltpu.VMEM] * 27))


def swapped(value):
    return lax.ppermute(value, "section", [(0, 1), (1, 0)])


def exchange_orders(bits):
    if bits == 4:
        return ((0, 1, 2, 3), (1, 2, 0, 3), (2, 0, 1, 3))
    turn = max(1, bits // 3)
    every = tuple(range(bits))
    return tuple(every[turn * part :] + every[: turn * part] for part in range(3))


def exchanged(value, bit, size):
    return lax.ppermute(value, "dp", [(index, index ^ (1 << bit)) for index in range(size)])


def exchange_bits():
    size = lax.axis_size("dp")
    bits = size.bit_length() - 1
    if size < 2 or size != 1 << bits or any(2 * rows % size for rows in PARTS):
        return []
    index = lax.axis_index("dp")
    return [((index >> bit) & 1) == 0 for bit in range(bits)]


def summed_over_dp(parts, clear):
    size = lax.axis_size("dp")
    bits = len(clear)
    if not bits:
        return [lax.psum(part.astype(F32), "dp").astype(BF16) for part in parts]
    orders = exchange_orders(bits)
    shapes = [part.shape for part in parts]
    held = [part.reshape((2,) * (bits - 1) + (2 * part.shape[0] // size, D)) for part in parts]
    for step in range(bits):
        kept, came = held, []
        if step < bits - 1:
            kept = [jnp.where(clear[order[step]], value[0], value[1]) for value, order in zip(held, orders)]
            held = [jnp.where(clear[order[step]], value[1], value[0]) for value, order in zip(held, orders)]
        came = [exchanged(value, order[step], size) for value, order in zip(held, orders)]
        held = [(a.astype(F32) + b.astype(F32)).astype(BF16) for a, b in zip(kept, came)]
    for step in reversed(range(bits - 1)):
        grown = []
        for value, order in zip(held, orders):
            low = clear[order[step]]
            came = exchanged(value, order[step], size)
            grown.append(jnp.stack([jnp.where(low, value, came), jnp.where(low, came, value)]))
        held = grown
    return [value.reshape(shape) for value, shape in zip(held, shapes)]


def per_device(inputs, cotangent, *states):
    states = [array.reshape(1, 9 * D) if array.shape == (1, 9, D) else array for array in states]
    states = [array.reshape(array.shape[1:]) if array.ndim == 3 else array for array in states]
    vectors, kernels = states[:2]
    section = lax.axis_index("section").astype(jnp.int32).reshape(1)
    section, *clear = lax.optimization_barrier((section, *exchange_bits()))
    wide, deep = run_narrowed(*states[2:6])
    results = run_blocks(
        section,
        inputs,
        cotangent,
        vectors,
        swapped(vectors),
        kernels,
        swapped(kernels),
        wide,
        swapped(wide),
        deep,
        swapped(deep),
    )
    totals = [
        (own.astype(F32) + swapped(other).astype(F32)).astype(BF16)
        for own, other in zip(results[4::2], results[5::2])
    ]
    a, b, c = summed_over_dp(totals, clear)
    squares = run_square_sum(a, b, c)
    rows_in = (results[0], swapped(results[1]), results[2], swapped(results[3]))
    new = run_optimizer(section, rows_in, squares, swapped(squares), a, b, c, states)

    def whole(arrays):
        return [
            array if array.shape == (1, VEC) else array.reshape(1, 9, D) if array.shape == (1, 9 * D) else array[None]
            for array in arrays
        ]

    return (new[29][None], new[30][None], *whole(new[0:6]), new[28].reshape(()), *whole(new[6:28]))


def solution(mesh):
    rows = P("dp", None)
    state = (P("section", None),) + (P("section", None, None),) * 5
    return jax.shard_map(
        per_device,
        mesh=mesh,
        in_specs=(rows, rows) + state * 3,
        out_specs=(P("section", "dp", None),) * 2 + state + (P(),) + state * 3 + state[2:],
        check_vma=False,
    )
```

```python
import jax
import jax.numpy as jnp
import numpy as np
from jax import lax
from jax.experimental import pallas as pl
from jax.experimental.pallas import tpu as pltpu
from jax.sharding import PartitionSpec as P

D = 256
HALF = 128
HEADS = 8
HEAD = 32
FF = 1024
BIG_SIDE = 14
SMALL_SIDE = 6
BIG_MB = 1
SMALL_MB = 3
STEP = 8
MB_TOK = 304
VEC = 3328

NORM_EPS = 1e-05
CLIP_LIMIT = 5.0
LEARN_RATE = 4.0
MOMENTUM_DECAY = 0.9
WEIGHT_DECAY = 5e-05

F32 = jnp.float32
BF16 = jnp.bfloat16

GROUP = 128
WINDOWS = ((0, BIG_SIDE, 0, 112), (112, BIG_SIDE, 0, 84), (192, SMALL_SIDE, 4, 108))
NGROUP = len(WINDOWS)
LONG_TOK = 320
SCALE = HEAD ** -0.5
LOG2E = 1.4426950408889634
EXP_SCALE = SCALE * LOG2E
OFF = -1e30
ROWS = ((0, 80), (80, 80), (160, 80), (240, 64))
PARTS = (1024, 1024, 1088)


def turned_table():
    turned = np.zeros((MB_TOK, MB_TOK), np.float32)
    base = 0
    for side, count in ((BIG_SIDE, BIG_MB), (SMALL_SIDE, SMALL_MB)):
        for _ in range(count):
            for row in range(side):
                for col in range(side):
                    turned[base + row * side + col, base + col * side + row] = 1.0
            base += side * side
    return turned


def stripe_tables():
    shifts = np.zeros((NGROUP, 5 * GROUP, GROUP), np.float32)
    fence = np.full((NGROUP, GROUP, GROUP), OFF, np.float32)
    lower = np.zeros((NGROUP, GROUP, HALF), np.float32)
    for kind, (_, side, first, size) in enumerate(WINDOWS):
        stripe = 2 * side
        number = (np.arange(GROUP) - first) // stripe
        number[:first] = -1
        number[first + size :] = GROUP
        fence[kind][number[:, None] == number[None, :]] = 0.0
        for at in range(size):
            own, inner = divmod(at, stripe)
            row, col = divmod(inner, side)
            lower[kind, first + at, :] = float(row)
            moves = ((row, col - 1), (row, col + 1), (1 - row, col - 1), (1 - row, col), (1 - row, col + 1))
            for move, (to_row, to_col) in enumerate(moves):
                if 0 <= to_col < side:
                    target = first + own * stripe + to_row * side + to_col
                    shifts[kind, move * GROUP + first + at, target] = 1.0
    return shifts, fence, lower


def kept_in(arrays, spaces):
    return [pltpu.with_memory_space_constraint(array, space) for array, space in zip(arrays, spaces)]


def dot(a, b):
    return jnp.dot(a, b, preferred_element_type=F32)


def dot_nt(a, b):
    return lax.dot_general(a, b, (((1,), (1,)), ((), ())), preferred_element_type=F32)


def dot_tn(a, b):
    return lax.dot_general(a, b, (((0,), (0,)), ((), ())), preferred_element_type=F32)


def head_masks():
    lane = lax.broadcasted_iota(jnp.int32, (1, HALF), 1) // HEAD
    return [(lane == head).astype(BF16) for head in range(HEADS // 2)]


def stacked_heads(rows, masks):
    return jnp.concatenate([rows * mask for mask in masks], axis=0)


def picked_heads(product):
    return jnp.concatenate(
        [
            product[HEAD * head : HEAD * (head + 1), GROUP * head : GROUP * (head + 1)]
            for head in range(HEADS // 2)
        ],
        axis=0,
    )


def turned_taps(taps):
    turned = [3 * (index % 3) + index // 3 for index in range(9)]
    return [
        jnp.concatenate(
            [taps[:, index * D : index * D + HALF], taps[:, turned[index] * D + HALF : (turned[index] + 1) * D]],
            axis=1,
        )
        for index in range(9)
    ]


def norm_forward(x, gain, offset):
    centre = x - jnp.mean(x, axis=-1, keepdims=True)
    spread = jnp.mean(centre * centre, axis=-1, keepdims=True)
    scale = lax.rsqrt(spread + NORM_EPS)
    hat = centre * scale
    return hat, scale, hat * gain + offset


def norm_backward(grad, hat, scale, gain):
    inner = grad * gain
    mean_inner = jnp.mean(inner, axis=-1, keepdims=True)
    mean_cross = jnp.mean(inner * hat, axis=-1, keepdims=True)
    return scale * (inner - mean_inner - hat * mean_cross)


def column_sum(x):
    return jnp.sum(x.astype(F32), axis=0, keepdims=True)


def window(group):
    return pl.ds(WINDOWS[group][0], GROUP)


def put_window(ref, group, value):
    if group == 0:
        ref[0:112, :] = value[0:112].astype(BF16)
    elif group == 1:
        ref[112:208, :] = value[0:96].astype(BF16)
    else:
        before = lax.broadcasted_iota(jnp.int32, (16, value.shape[1]), 0) < 4
        ref[192:208, :] = jnp.where(before, ref[192:208, :].astype(F32), value[0:16]).astype(BF16)
        ref[208:304, :] = value[16:112].astype(BF16)


def vec_at(vec, index, width=1):
    return vec[:, index * D : (index + width) * D]


def forward_block(x_ref, out_ref, vec_ref, taps_ref, w, saved, tables, work, need):
    wq, wp, w1, w2 = w
    (hat1, scale1, normed, qkv, probs, probs_low, mixed, hat2, scale2, normed2, slope, activ) = saved
    turned, shifts, fence, lower = tables
    mixed_att, middle, hidden, flipped, local = work
    need("x", "vec")
    vec = vec_ref[...]
    for start, size in ROWS:
        rows = pl.ds(start, size)
        hat, scale, y = norm_forward(x_ref[rows, :].astype(F32), vec_at(vec, 0), vec_at(vec, 2))
        hat1[rows, :] = hat
        scale1[rows, :] = jnp.broadcast_to(scale, (size, HALF))
        normed[0, rows, :] = y.astype(BF16)
    need("place", "wide")
    normed[1] = dot(turned[...], normed[0]).astype(BF16)
    biases = (vec_at(vec, 4), None, vec_at(vec, 5))
    for half in range(2):
        lanes = slice(half * HALF, (half + 1) * HALF)
        for part in range(3):
            got = dot(normed[half], wq[:, part * D + half * HALF : part * D + (half + 1) * HALF])
            if biases[part] is not None:
                got = got + biases[part][:, lanes]
            qkv[part, 0:MB_TOK, lanes] = got.astype(BF16)
    masks = head_masks()
    need("stripe")
    taps9 = turned_taps(taps_ref[...])
    bias = vec_at(vec, 7)
    units = [(group, half) for group in range(NGROUP) for half in range(2)]
    for unit, (group, half) in enumerate(units):
        rows = window(group)
        lanes = slice(half * HALF, (half + 1) * HALF)
        probs[unit] = dot_nt(qkv[1, rows, lanes], stacked_heads(qkv[0, rows, lanes], masks))
        flipped[unit] = qkv[2, rows, lanes].T
    for group in range(NGROUP):
        fenced = fence[group]
        for unit in (2 * group, 2 * group + 1):
            for head in range(HEADS // 2):
                cols = slice(head * GROUP, (head + 1) * GROUP)
                s = probs[unit, :, cols] + fenced
                p = jnp.exp2((s - jnp.max(s, axis=0, keepdims=True)) * EXP_SCALE)
                p = p * (1.0 / jnp.sum(p, axis=0, keepdims=True))
                probs[unit, :, cols] = p
                probs_low[unit, :, cols] = p.astype(BF16)
        rows = window(group)
        v = qkv[2, rows, :]
        moved = dot(shifts[group], v)
        low_row = lower[group] > 0.5
        low_row = jnp.concatenate([low_row, low_row], axis=1)
        lepe = bias + taps9[4] * v.astype(F32)
        lepe = lepe + taps9[3] * moved[0:GROUP] + taps9[5] * moved[GROUP : 2 * GROUP]
        for step in range(3):
            tap = jnp.where(low_row, taps9[step], taps9[6 + step])
            lepe = lepe + tap * moved[(2 + step) * GROUP : (3 + step) * GROUP]
        local[group] = lepe
    for unit, (group, half) in enumerate(units):
        rows = window(group)
        lanes = slice(half * HALF, (half + 1) * HALF)
        attended = picked_heads(dot(flipped[unit], probs_low[unit])).T
        put_window(mixed_att.at[half], group, attended + local[group, :, lanes])
    mixed[:, :HALF] = mixed_att[0]
    mixed[:, HALF:] = dot(turned[...], mixed_att[1]).astype(BF16)
    middle[...] = dot(mixed[...], wp[...])
    need("deep")
    sides = ((slice(0, 160), ROWS[:2]), (slice(160, MB_TOK), ROWS[2:]))
    for side, chunks in sides:
        for start, size in chunks:
            rows = pl.ds(start, size)
            mid = x_ref[rows, :].astype(F32) + middle[rows, :] + vec_at(vec, 6)
            middle[rows, :] = mid
            hat, scale, y = norm_forward(mid, vec_at(vec, 1), vec_at(vec, 3))
            hat2[rows, :] = hat
            scale2[rows, :] = jnp.broadcast_to(scale, (size, HALF))
            normed2[rows, :] = y.astype(BF16)
        hidden[side, :] = dot(normed2[side, :], w1[...])
    for side, chunks in sides:
        for start, size in chunks:
            rows = pl.ds(start, size)
            for part in range(4):
                cols = slice(part * D, (part + 1) * D)
                h = hidden[rows, cols] + vec_at(vec, 9 + part)
                cdf = 0.5 * (1.0 + lax.erf(h * 0.7071067811865476))
                pdf = 0.3989422804014327 * jnp.exp(-0.5 * h * h)
                activ[rows, cols] = (h * cdf).astype(BF16)
                slope[rows, cols] = cdf + h * pdf
        out_ref[side, :] = dot(activ[side, :], w2[...]) + middle[side, :] + vec_at(vec, 8)


def backward_block(up_ref, grad_ref, vec_ref, taps_ref, w, saved, tables, work, sums, small):
    wq, wp, w1, w2 = w
    (hat1, scale1, normed, qkv, probs, probs_low, mixed, hat2, scale2, normed2, slope, activ) = saved
    turned, shifts, fence, lower = tables
    branch, gact, ghid, gmid, gmix, dqkv, dnat, gnorm, gprobs, gscores, flipped, local = work
    early, inner, outer = sums
    vec = vec_ref[...]
    branch[...] = up_ref[...].astype(BF16)
    sums = column_sum(branch[...])
    small[8:9, :] = sums
    gact[...] = dot_nt(branch[...], w2[...])
    parts = [jnp.zeros((1, D), F32) for _ in range(4)]
    for turn, (start, size) in enumerate(ROWS):
        rows = pl.ds(start, size)
        outer[turn * D : (turn + 1) * D, :] = dot_tn(activ[:, turn * D : (turn + 1) * D], branch[...]).astype(BF16)
        for part in range(4):
            cols = slice(part * D, (part + 1) * D)
            low = (gact[rows, cols] * slope[rows, cols]).astype(BF16)
            ghid[rows, cols] = low
            parts[part] = parts[part] + column_sum(low)
    for part in range(4):
        small[9 + part : 10 + part, :] = parts[part]
    gnorm[...] = dot_nt(ghid[...], w1[...])
    gains, offsets, outs = (jnp.zeros((1, D), F32) for _ in range(3))
    for turn, (start, size) in enumerate(ROWS):
        rows = pl.ds(start, size)
        inner[turn * D : (turn + 1) * D, :] = dot_tn(normed2[...], ghid[:, turn * D : (turn + 1) * D]).astype(BF16)
        g = gnorm[rows, :]
        hat = hat2[rows, :]
        scale = scale2[rows, :]
        gains = gains + column_sum(g * hat)
        offsets = offsets + column_sum(g)
        full = jnp.concatenate([scale, scale], axis=1)
        total = up_ref[rows, :].astype(F32) + norm_backward(g, hat, full, vec_at(vec, 1))
        gmid[rows, :] = total
        low = total.astype(BF16)
        branch[rows, :] = low
        outs = outs + column_sum(low)
    small[1:2, :] = gains
    small[3:4, :] = offsets
    small[6:7, :] = outs
    low = dot_nt(branch[...], wp[...]).astype(BF16)
    small[7:8, :] = column_sum(low)
    gmix[0:MB_TOK, :HALF] = low[:, :HALF]
    gmix[0:MB_TOK, HALF:] = dot(turned[...], low[:, HALF:]).astype(BF16)
    masks = head_masks()
    taps9 = turned_taps(taps_ref[...])
    tap_sums = [jnp.zeros((1, D), F32) for _ in range(9)]
    for start, size in ROWS:
        rows = pl.ds(start, size)
        tap_sums[4] = tap_sums[4] + column_sum(qkv[2, rows, :].astype(F32) * gmix[rows, :].astype(F32))
    units = [(group, half) for group in range(NGROUP) for half in range(2)]
    for unit, (group, half) in enumerate(units):
        rows = window(group)
        lanes = slice(half * HALF, (half + 1) * HALF)
        gprobs[unit] = dot_nt(qkv[2, rows, lanes], stacked_heads(gmix[rows, lanes], masks))
        flipped[unit] = qkv[1, rows, lanes].T
    for group in range(NGROUP):
        if group < 2:
            lanes = slice(group * HALF, (group + 1) * HALF)
            early[3 * D + group * HALF : 3 * D + (group + 1) * HALF, :] = dot_tn(mixed[:, lanes], branch[...]).astype(BF16)
        for unit in (2 * group, 2 * group + 1):
            for head in range(HEADS // 2):
                cols = slice(head * GROUP, (head + 1) * GROUP)
                p = probs[unit, :, cols]
                gp = gprobs[unit, :, cols]
                down = jnp.sum(gp * p, axis=0, keepdims=True)
                gscores[unit, :, cols] = (p * (gp - down)).astype(BF16)
        rows = window(group)
        g_low = gmix[rows, :]
        moved = dot(shifts[group], g_low)
        low_row = lower[group] > 0.5
        low_row = jnp.concatenate([low_row, low_row], axis=1)
        v32 = qkv[2, rows, :].astype(F32)
        g32 = g_low.astype(F32)
        left, right = moved[0:GROUP], moved[GROUP : 2 * GROUP]
        lepe = taps9[4] * g32 + taps9[3] * right + taps9[5] * left
        tap_sums[3] = tap_sums[3] + column_sum(v32 * right)
        tap_sums[5] = tap_sums[5] + column_sum(v32 * left)
        for step in range(3):
            at = moved[(4 - step) * GROUP : (5 - step) * GROUP]
            lepe = lepe + jnp.where(low_row, taps9[6 + step], taps9[step]) * at
            product = v32 * at
            tap_sums[6 + step] = tap_sums[6 + step] + column_sum(jnp.where(low_row, product, 0.0))
            tap_sums[step] = tap_sums[step] + column_sum(jnp.where(low_row, 0.0, product))
        local[group] = lepe
    for unit, (group, half) in enumerate(units):
        rows = window(group)
        lanes = slice(half * HALF, (half + 1) * HALF)
        low_s = gscores[unit]
        grad_v = dot(probs_low[unit], stacked_heads(gmix[rows, lanes], masks)) + local[group, :, lanes]
        grad_k = dot(low_s, stacked_heads(qkv[0, rows, lanes], masks)) * SCALE
        grad_q = picked_heads(dot(flipped[unit], low_s)).T * SCALE
        put_window(dqkv.at[half], group, jnp.concatenate([grad_q, grad_k, grad_v], axis=1))
    for index in range(9):
        tap = index
        turned_index = 3 * (index % 3) + index // 3
        small[13 + index : 14 + index, :] = jnp.concatenate(
            [tap_sums[tap][:, :HALF], tap_sums[turned_index][:, HALF:]], axis=1
        )
    for half in range(2):
        both = dqkv[half]
        natural = both if half == 0 else dot(turned[...], both).astype(BF16)
        for part in range(3):
            dnat[:, part * D + half * HALF : part * D + (half + 1) * HALF] = natural[
                :, part * HALF : (part + 1) * HALF
            ]
    gnorm[...] = dot_nt(dnat[...], wq[...])
    gains, offsets = (jnp.zeros((1, D), F32) for _ in range(2))
    for turn, (start, size) in enumerate(ROWS):
        rows = pl.ds(start, size)
        if turn < 2:
            both = dqkv[turn]
            lanes = slice(turn * HALF, (turn + 1) * HALF)
            small[4:5, lanes] = column_sum(both[:, 0:HALF])
            small[5:6, lanes] = column_sum(both[:, D : 3 * HALF])
            grads = dot_tn(normed[turn], both)
            for part in range(3):
                early[part * D : (part + 1) * D, lanes] = grads[:, part * HALF : (part + 1) * HALF].astype(BF16)
        g = gnorm[rows, :]
        hat = hat1[rows, :]
        scale = scale1[rows, :]
        gains = gains + column_sum(g * hat)
        offsets = offsets + column_sum(g)
        full = jnp.concatenate([scale, scale], axis=1)
        grad_ref[rows, :] = gmid[rows, :] + norm_backward(g, hat, full, vec_at(vec, 0))
    small[0:1, :] = gains
    small[2:3, :] = offsets
    outer[FF : FF + 32, :] = small[...].astype(BF16)


SAVED = [
    ((MB_TOK, D), F32),
    ((MB_TOK, HALF), F32),
    ((2, MB_TOK, D), BF16),
    ((3, LONG_TOK, D), BF16),
    ((2 * NGROUP, GROUP, 4 * GROUP), F32),
    ((2 * NGROUP, GROUP, 4 * GROUP), BF16),
    ((MB_TOK, D), BF16),
    ((MB_TOK, D), F32),
    ((MB_TOK, HALF), F32),
    ((MB_TOK, D), BF16),
    ((MB_TOK, FF), F32),
    ((MB_TOK, FF), BF16),
]
FORWARD_WORK = [
    ((2, MB_TOK, HALF), BF16),
    ((MB_TOK, D), F32),
    ((MB_TOK, FF), F32),
    ((2 * NGROUP, GROUP, GROUP), BF16),
    ((NGROUP, GROUP, D), F32),
]
BACKWARD_WORK = [
    ((MB_TOK, D), BF16),
    ((MB_TOK, FF), F32),
    ((MB_TOK, FF), BF16),
    ((MB_TOK, D), F32),
    ((LONG_TOK, D), BF16),
    ((2, MB_TOK, 3 * HALF), BF16),
    ((MB_TOK, 3 * D), BF16),
    ((MB_TOK, D), F32),
    ((2 * NGROUP, GROUP, 4 * GROUP), F32),
    ((2 * NGROUP, GROUP, 4 * GROUP), BF16),
    ((2 * NGROUP, GROUP, GROUP), BF16),
    ((NGROUP, GROUP, D), F32),
]


INPUTS = [
    ((MB_TOK, D), BF16),
    ((MB_TOK, D), BF16),
    ((2, 1, VEC), F32),
    ((2, 1, 9 * D), F32),
    ((2, D, 8 * D), BF16),
    ((2, FF, D), BF16),
    ((MB_TOK, MB_TOK), BF16),
    ((NGROUP, 5 * GROUP, GROUP), BF16),
    ((NGROUP, GROUP, GROUP), F32),
    ((NGROUP, GROUP, HALF), F32),
]
RESULTS = [((2, MB_TOK, D), F32), ((2, MB_TOK, D), F32)] + [((2, rows, D), BF16) for rows in PARTS]
OTHER_WORK = [((MB_TOK, D), BF16), ((32, D), F32)]


def section_step(sec_ref, *refs):
    def take(count):
        nonlocal refs
        taken, refs = refs[:count], refs[count:]
        return taken

    x_in, c_in, vec_own, vec_other, ker_own, ker_other, wide_own, wide_other, deep_own, deep_other = take(10)
    table_in = take(4)
    sent = [take(2) for _ in RESULTS]
    held = take(len(INPUTS))
    results = take(len(RESULTS))
    kept = (take(len(SAVED)), take(len(SAVED)))
    forward_work = take(len(FORWARD_WORK))
    backward_work = take(len(BACKWARD_WORK))
    feed, small, in_sems, out_sems = refs
    x, c, vecs, taps, wide, deep = held[:6]
    tables = held[6:]
    sec = sec_ref[0]
    at = pl.multiple_of(sec * MB_TOK, 16)
    moves = [
        ("x", x_in.at[pl.ds(at, MB_TOK)], x),
        ("vec", vec_own, vecs.at[sec]),
        ("vec", vec_other, vecs.at[1 - sec]),
        ("place", table_in[0], tables[0]),
        ("wide", wide_own, wide.at[sec]),
        ("wide", wide_other, wide.at[1 - sec]),
        ("stripe", table_in[1], tables[1]),
        ("stripe", table_in[2], tables[2]),
        ("stripe", table_in[3], tables[3]),
        ("stripe", ker_own, taps.at[sec]),
        ("stripe", ker_other, taps.at[1 - sec]),
        ("deep", deep_own, deep.at[sec]),
        ("deep", deep_other, deep.at[1 - sec]),
        ("c", c_in.at[pl.ds(at, MB_TOK)], c),
    ]
    pending = {}
    for index, (name, source, target) in enumerate(moves):
        copy = pltpu.make_async_copy(source, target, in_sems.at[index])
        copy.start()
        pending.setdefault(name, []).append(copy)

    def need(*names):
        for name in names:
            for copy in pending.pop(name, []):
                copy.wait()

    leaving = []

    def leave(index):
        for which, slot in enumerate((sec, 1 - sec)):
            copy = pltpu.make_async_copy(results[index].at[slot], sent[index][which], out_sems.at[2 * index + which])
            copy.start()
            leaving.append(copy)

    outs, grads, early, inner, outer = results
    small[...] = jnp.zeros_like(small)
    for b in range(2):
        kept[b][3][:, MB_TOK:, :] = jnp.zeros((3, LONG_TOK - MB_TOK, D), BF16)
    backward_work[4][MB_TOK:, :] = jnp.zeros((LONG_TOK - MB_TOK, D), BF16)
    for part, rows in zip((early, inner, outer), PARTS):
        if rows > FF:
            part[:, FF:, :] = jnp.zeros((2, rows - FF, D), BF16)
    weights = [
        (wide.at[b, :, 0 : 3 * D], wide.at[b, :, 3 * D : 4 * D], wide.at[b, :, 4 * D : 8 * D], deep.at[b])
        for b in range(2)
    ]
    sums = [(early.at[b], inner.at[b], outer.at[b]) for b in range(2)]

    def forward(b, source):
        forward_block(
            source, outs.at[b], vecs.at[b], taps.at[b], weights[b], kept[b], tables, forward_work, need
        )

    def backward(b, source):
        backward_block(
            source, grads.at[b], vecs.at[b], taps.at[b], weights[b], kept[b], tables, backward_work, sums[b], small
        )

    forward(0, x)
    feed[...] = outs[0].astype(BF16)
    forward(1, feed)
    leave(0)
    need("c")
    backward(1, c)
    feed[...] = grads[1].astype(BF16)
    backward(0, feed)
    for index in range(1, len(RESULTS)):
        leave(index)
    for copy in leaving:
        copy.wait()


def run_blocks(sec, *arrays):
    shifts, fence, lower = stripe_tables()
    tables = (
        jnp.asarray(turned_table(), BF16),
        jnp.asarray(shifts, BF16),
        jnp.asarray(fence, F32),
        jnp.asarray(lower, F32),
    )
    spaces = [pltpu.HBM] * 3 + [pltpu.VMEM, pltpu.HBM] + [pltpu.VMEM] * 5 + [pltpu.HBM] * 4
    smem = pl.BlockSpec(memory_space=pltpu.SMEM)
    scratch = INPUTS + RESULTS + SAVED + SAVED + FORWARD_WORK + BACKWARD_WORK + OTHER_WORK
    out_shape = [pltpu.VMEM(shape[1:], kind) for shape, kind in RESULTS for _ in range(2)]
    return pl.pallas_call(
        section_step,
        out_shape=out_shape,
        in_specs=[smem] + [pl.BlockSpec(memory_space=space) for space in spaces],
        out_specs=[pl.BlockSpec(memory_space=pl.ANY)] * len(out_shape),
        scratch_shapes=[pltpu.VMEM(shape, kind) for shape, kind in scratch]
        + [pltpu.SemaphoreType.DMA((14,)), pltpu.SemaphoreType.DMA((2 * len(RESULTS),))],
        compiler_params=pltpu.CompilerParams(vmem_limit_bytes=34 << 20),
        name="blocks",
    )(sec, *kept_in(arrays + tables, spaces))


NARROW = (((D, 3 * D), 0), ((D, D), 3 * D), ((D, FF), 4 * D), ((FF, D), None))


def narrowed(*refs):
    sources, (wide, deep), held, (sems,) = refs[:4], refs[4:6], refs[6:10], refs[10:]
    coming = [pltpu.make_async_copy(sources[k], held[k], sems.at[k]) for k in range(4)]
    for copy in coming:
        copy.start()
    for k, (shape, first) in enumerate(NARROW):
        coming[k].wait()
        if first is None:
            deep[...] = held[k][...].astype(BF16)
        else:
            wide[:, first : first + shape[1]] = held[k][...].astype(BF16)


def run_narrowed(*weights):
    vmem = pl.BlockSpec(memory_space=pltpu.VMEM)
    return pl.pallas_call(
        narrowed,
        out_shape=[pltpu.VMEM((D, 8 * D), BF16), pltpu.VMEM((FF, D), BF16)],
        in_specs=[pl.BlockSpec(memory_space=pltpu.HBM)] * 4,
        out_specs=[vmem] * 2,
        scratch_shapes=[pltpu.VMEM(shape, F32) for shape, _ in NARROW] + [pltpu.SemaphoreType.DMA((4,))],
        compiler_params=pltpu.CompilerParams(vmem_limit_bytes=8 << 20),
        name="narrowed",
    )(*kept_in(weights, [pltpu.HBM] * 4))


def square_sum(a_ref, b_ref, c_ref, out_ref):
    total = jnp.zeros((8, D), F32)
    for ref in (a_ref, b_ref, c_ref):
        step = 64
        for start in range(0, ref.shape[0], step):
            rows = ref[start : start + step, :].astype(F32)
            square = rows * rows
            for at in range(0, step, 8):
                total = total + square[at : at + 8]
    total = jnp.sum(jnp.sum(total, axis=0, keepdims=True), axis=1, keepdims=True)
    out_ref[...] = jnp.broadcast_to(total, (8, HALF))


def run_square_sum(a, b, c):
    vmem = pl.BlockSpec(memory_space=pltpu.VMEM)
    return pl.pallas_call(
        square_sum,
        out_shape=jax.ShapeDtypeStruct((8, HALF), F32),
        in_specs=[vmem] * 3,
        out_specs=vmem,
        compiler_params=pltpu.CompilerParams(vmem_limit_bytes=16 << 20),
        name="squares",
    )(a, b, c)


def updated(grad, weight, moment, average, factor):
    decay = min(0.9999, (1.0 + STEP) / (10.0 + STEP))
    clipped = grad * factor
    direction = clipped + WEIGHT_DECAY * weight
    moment_new = MOMENTUM_DECAY * moment + direction
    weight_new = weight - LEARN_RATE * (direction + MOMENTUM_DECAY * moment_new)
    average_new = decay * average + (1.0 - decay) * weight_new
    return clipped, moment_new, weight_new, average_new


SHAPES = ((1, VEC), (1, 9 * D), (D, 3 * D), (D, D), (D, FF), (FF, D))
PIECES = (
    (3, 0, 128),
    (3, 128, 128),
    (2, 0, 128),
    (2, 128, 128),
    (4, 0, 128),
    (4, 128, 128),
    (5, 0, 256),
    (5, 256, 256),
    (5, 512, 256),
    (5, 768, 256),
)
OUT_SHAPES = [(shape, F32) for shape in SHAPES] * 4 + [(shape, BF16) for shape in SHAPES[2:]]
MOVES = 4 + 4 * 2 + 5 * len(PIECES)


def optimizer_step(sec_ref, *refs):
    def take(count):
        nonlocal refs
        taken, refs = refs[:count], refs[count:]
        return taken

    rows_in, (own, other), (a, b, c), states = take(4), take(2), take(3), take(18)
    outs, (norm_ref,), rows_out, made, (sems,) = take(28), take(1), take(2), take(28), take(1)
    sec = sec_ref[0]
    moves = []

    def leave(source, target):
        move = pltpu.make_async_copy(source, target, sems.at[len(moves)])
        move.start()
        moves.append(move)

    for index in range(4):
        first = pl.multiple_of((sec if index % 2 == 0 else 1 - sec) * MB_TOK, 8)
        leave(rows_in[index], rows_out[index // 2].at[pl.ds(first, MB_TOK)])
    norm = jnp.sqrt(own[0:1, 0:1] + other[0:1, 0:1])
    factor = jnp.minimum(1.0, CLIP_LIMIT / (norm + 1e-06))
    norm_ref[...] = norm

    def put(index, rows, lanes, grad):
        weight, moment, average = (states[kind * 6 + index][rows, lanes] for kind in range(3))
        new = updated(grad, weight, moment, average, factor)
        for kind in range(4):
            made[kind * 6 + index][rows, lanes] = new[kind]
        if index >= 2:
            made[24 + index - 2][rows, lanes] = new[2].astype(BF16)

    places = {2: [(a, 0), (a, D), (a, 2 * D)], 3: [(a, 3 * D)], 4: [(b, part * D) for part in range(4)], 5: [(c, 0)]}
    step = 32
    for index, first, count in PIECES:
        for row in range(first, first + count, step):
            for part, (ref, base) in enumerate(places[index]):
                grad = ref[base + row : base + row + step, :].astype(F32)
                put(index, slice(row, row + step), slice(part * D, (part + 1) * D), grad)
        rows = pl.ds(first, count)
        for kind in range(5):
            at = kind * 6 + index if kind < 4 else 24 + index - 2
            leave(made[at].at[rows], outs[at].at[rows])
    rows = c[FF : FF + 32, :].astype(F32)
    whole = slice(0, 1)
    for part in range(13):
        put(0, whole, slice(part * D, (part + 1) * D), rows[part : part + 1, :])
    for part in range(9):
        put(1, whole, slice(part * D, (part + 1) * D), rows[13 + part : 14 + part, :])
    for index in range(2):
        for kind in range(4):
            leave(made[kind * 6 + index], outs[kind * 6 + index])
    for move in moves:
        move.wait()


def run_optimizer(sec, rows_in, own, other, a, b, c, states):
    vmem = pl.BlockSpec(memory_space=pltpu.VMEM)
    hbm = pl.BlockSpec(memory_space=pltpu.HBM)
    return pl.pallas_call(
        optimizer_step,
        out_shape=[pltpu.HBM(shape, kind) for shape, kind in OUT_SHAPES]
        + [jax.ShapeDtypeStruct((1, 1), F32)]
        + [pltpu.HBM((2 * MB_TOK, D), F32)] * 2,
        in_specs=[pl.BlockSpec(memory_space=pltpu.SMEM)] + [vmem] * (4 + 2 + 3 + 18),
        out_specs=[hbm] * 28 + [vmem] + [hbm] * 2,
        scratch_shapes=[pltpu.VMEM(shape, kind) for shape, kind in OUT_SHAPES] + [pltpu.SemaphoreType.DMA((MOVES,))],
        compiler_params=pltpu.CompilerParams(vmem_limit_bytes=20 << 20),
        name="optimizer",
    )(sec, *kept_in((*rows_in, own, other, a, b, c, *states), [pltpu.VMEM] * 27))


def swapped(value):
    return lax.ppermute(value, "section", [(0, 1), (1, 0)])


def exchange_orders(bits):
    if bits == 4:
        return ((0, 1, 2, 3), (1, 2, 0, 3), (2, 0, 1, 3))
    turn = max(1, bits // 3)
    every = tuple(range(bits))
    return tuple(every[turn * part :] + every[: turn * part] for part in range(3))


def exchanged(value, bit, size):
    return lax.ppermute(value, "dp", [(index, index ^ (1 << bit)) for index in range(size)])


def exchange_bits():
    size = lax.axis_size("dp")
    bits = size.bit_length() - 1
    if size < 2 or size != 1 << bits or any(2 * rows % size for rows in PARTS):
        return []
    index = lax.axis_index("dp")
    return [((index >> bit) & 1) == 0 for bit in range(bits)]


def summed_over_dp(parts, clear):
    size = lax.axis_size("dp")
    bits = len(clear)
    if not bits:
        return [lax.psum(part.astype(F32), "dp").astype(BF16) for part in parts]
    orders = exchange_orders(bits)
    shapes = [part.shape for part in parts]
    held = [part.reshape((2,) * (bits - 1) + (2 * part.shape[0] // size, D)) for part in parts]
    for step in range(bits):
        kept, came = held, []
        if step < bits - 1:
            kept = [jnp.where(clear[order[step]], value[0], value[1]) for value, order in zip(held, orders)]
            held = [jnp.where(clear[order[step]], value[1], value[0]) for value, order in zip(held, orders)]
        came = [exchanged(value, order[step], size) for value, order in zip(held, orders)]
        held = [(a.astype(F32) + b.astype(F32)).astype(BF16) for a, b in zip(kept, came)]
    for step in reversed(range(bits - 1)):
        grown = []
        for value, order in zip(held, orders):
            low = clear[order[step]]
            came = exchanged(value, order[step], size)
            grown.append(jnp.stack([jnp.where(low, value, came), jnp.where(low, came, value)]))
        held = grown
    return [value.reshape(shape) for value, shape in zip(held, shapes)]


def per_device(inputs, cotangent, *states):
    states = [array.reshape(1, 9 * D) if array.shape == (1, 9, D) else array for array in states]
    states = [array.reshape(array.shape[1:]) if array.ndim == 3 else array for array in states]
    vectors, kernels = states[:2]
    section = lax.axis_index("section").astype(jnp.int32).reshape(1)
    section, *clear = lax.optimization_barrier((section, *exchange_bits()))
    wide, deep = run_narrowed(*states[2:6])
    results = run_blocks(
        section,
        inputs,
        cotangent,
        vectors,
        swapped(vectors),
        kernels,
        swapped(kernels),
        wide,
        swapped(wide),
        deep,
        swapped(deep),
    )
    totals = [
        (own.astype(F32) + swapped(other).astype(F32)).astype(BF16)
        for own, other in zip(results[4::2], results[5::2])
    ]
    a, b, c = summed_over_dp(totals, clear)
    squares = run_square_sum(a, b, c)
    rows_in = (results[0], swapped(results[1]), results[2], swapped(results[3]))
    new = run_optimizer(section, rows_in, squares, swapped(squares), a, b, c, states)

    def whole(arrays):
        return [
            array if array.shape == (1, VEC) else array.reshape(1, 9, D) if array.shape == (1, 9 * D) else array[None]
            for array in arrays
        ]

    return (new[29][None], new[30][None], *whole(new[0:6]), new[28].reshape(()), *whole(new[6:28]))


def solution(mesh):
    rows = P("dp", None)
    state = (P("section", None),) + (P("section", None, None),) * 5
    return jax.shard_map(
        per_device,
        mesh=mesh,
        in_specs=(rows, rows) + state * 3,
        out_specs=(P("section", "dp", None),) * 2 + state + (P(),) + state * 3 + state[2:],
        check_vma=False,
    )
```

```python
import jax
import jax.numpy as jnp
import numpy as np
from jax import lax
from jax.experimental import pallas as pl
from jax.experimental.pallas import tpu as pltpu
from jax.sharding import PartitionSpec as P

D = 256
HALF = 128
HEADS = 8
HEAD = 32
FF = 1024
BIG_SIDE = 14
SMALL_SIDE = 6
BIG_MB = 1
SMALL_MB = 3
STEP = 8
MB_TOK = 304
VEC = 3328

NORM_EPS = 1e-05
CLIP_LIMIT = 5.0
LEARN_RATE = 4.0
MOMENTUM_DECAY = 0.9
WEIGHT_DECAY = 5e-05

F32 = jnp.float32
BF16 = jnp.bfloat16

GROUP = 128
WINDOWS = ((0, BIG_SIDE, 0, 112), (112, BIG_SIDE, 0, 84), (192, SMALL_SIDE, 4, 108))
NGROUP = len(WINDOWS)
LONG_TOK = 320
SCALE = HEAD ** -0.5
LOG2E = 1.4426950408889634
EXP_SCALE = SCALE * LOG2E
OFF = -1e30
ROWS = ((0, 80), (80, 80), (160, 80), (240, 64))
PARTS = (1024, 1024, 1088)


def turned_table():
    turned = np.zeros((MB_TOK, MB_TOK), np.float32)
    base = 0
    for side, count in ((BIG_SIDE, BIG_MB), (SMALL_SIDE, SMALL_MB)):
        for _ in range(count):
            for row in range(side):
                for col in range(side):
                    turned[base + row * side + col, base + col * side + row] = 1.0
            base += side * side
    return turned


def stripe_tables():
    shifts = np.zeros((NGROUP, 5 * GROUP, GROUP), np.float32)
    fence = np.full((NGROUP, GROUP, GROUP), OFF, np.float32)
    lower = np.zeros((NGROUP, GROUP, HALF), np.float32)
    for kind, (_, side, first, size) in enumerate(WINDOWS):
        stripe = 2 * side
        number = (np.arange(GROUP) - first) // stripe
        number[:first] = -1
        number[first + size :] = GROUP
        fence[kind][number[:, None] == number[None, :]] = 0.0
        for at in range(size):
            own, inner = divmod(at, stripe)
            row, col = divmod(inner, side)
            lower[kind, first + at, :] = float(row)
            moves = ((row, col - 1), (row, col + 1), (1 - row, col - 1), (1 - row, col), (1 - row, col + 1))
            for move, (to_row, to_col) in enumerate(moves):
                if 0 <= to_col < side:
                    target = first + own * stripe + to_row * side + to_col
                    shifts[kind, move * GROUP + first + at, target] = 1.0
    return shifts, fence, lower


def kept_in(arrays, spaces):
    return [pltpu.with_memory_space_constraint(array, space) for array, space in zip(arrays, spaces)]


def dot(a, b):
    return jnp.dot(a, b, preferred_element_type=F32)


def dot_nt(a, b):
    return lax.dot_general(a, b, (((1,), (1,)), ((), ())), preferred_element_type=F32)


def dot_tn(a, b):
    return lax.dot_general(a, b, (((0,), (0,)), ((), ())), preferred_element_type=F32)


def head_masks():
    lane = lax.broadcasted_iota(jnp.int32, (1, HALF), 1) // HEAD
    return [(lane == head).astype(BF16) for head in range(HEADS // 2)]


def stacked_heads(rows, masks):
    return jnp.concatenate([rows * mask for mask in masks], axis=0)


def picked_heads(product):
    return jnp.concatenate(
        [
            product[HEAD * head : HEAD * (head + 1), GROUP * head : GROUP * (head + 1)]
            for head in range(HEADS // 2)
        ],
        axis=0,
    )


def turned_taps(taps):
    turned = [3 * (index % 3) + index // 3 for index in range(9)]
    return [
        jnp.concatenate(
            [taps[:, index * D : index * D + HALF], taps[:, turned[index] * D + HALF : (turned[index] + 1) * D]],
            axis=1,
        )
        for index in range(9)
    ]


def norm_forward(x, gain, offset):
    centre = x - jnp.mean(x, axis=-1, keepdims=True)
    spread = jnp.mean(centre * centre, axis=-1, keepdims=True)
    scale = lax.rsqrt(spread + NORM_EPS)
    hat = centre * scale
    return hat, scale, hat * gain + offset


def norm_backward(grad, hat, scale, gain):
    inner = grad * gain
    mean_inner = jnp.mean(inner, axis=-1, keepdims=True)
    mean_cross = jnp.mean(inner * hat, axis=-1, keepdims=True)
    return scale * (inner - mean_inner - hat * mean_cross)


def column_sum(x):
    return jnp.sum(x.astype(F32), axis=0, keepdims=True)


def window(group):
    return pl.ds(WINDOWS[group][0], GROUP)


def put_window(ref, group, value):
    if group == 0:
        ref[0:112, :] = value[0:112].astype(BF16)
    elif group == 1:
        ref[112:208, :] = value[0:96].astype(BF16)
    else:
        before = lax.broadcasted_iota(jnp.int32, (16, value.shape[1]), 0) < 4
        ref[192:208, :] = jnp.where(before, ref[192:208, :].astype(F32), value[0:16]).astype(BF16)
        ref[208:304, :] = value[16:112].astype(BF16)


def vec_at(vec, index, width=1):
    return vec[:, index * D : (index + width) * D]


def forward_block(x_ref, out_ref, vec_ref, taps_ref, w, saved, tables, work, need):
    wq, wp, w1, w2 = w
    (hat1, scale1, normed, qkv, probs, probs_low, mixed, hat2, scale2, normed2, slope, activ) = saved
    turned, shifts, fence, lower = tables
    mixed_att, middle, hidden, flipped, local = work
    need("x", "vec")
    vec = vec_ref[...]
    for start, size in ROWS:
        rows = pl.ds(start, size)
        hat, scale, y = norm_forward(x_ref[rows, :].astype(F32), vec_at(vec, 0), vec_at(vec, 2))
        hat1[rows, :] = hat
        scale1[rows, :] = jnp.broadcast_to(scale, (size, HALF))
        normed[0, rows, :] = y.astype(BF16)
    need("rest")
    normed[1] = dot(turned[...], normed[0]).astype(BF16)
    biases = (vec_at(vec, 4), None, vec_at(vec, 5))
    for half in range(2):
        lanes = slice(half * HALF, (half + 1) * HALF)
        for part in range(3):
            got = dot(normed[half], wq[:, part * D + half * HALF : part * D + (half + 1) * HALF])
            if biases[part] is not None:
                got = got + biases[part][:, lanes]
            qkv[part, 0:MB_TOK, lanes] = got.astype(BF16)
    masks = head_masks()
    taps9 = turned_taps(taps_ref[...])
    bias = vec_at(vec, 7)
    units = [(group, half) for group in range(NGROUP) for half in range(2)]
    for unit, (group, half) in enumerate(units):
        rows = window(group)
        lanes = slice(half * HALF, (half + 1) * HALF)
        probs[unit] = dot_nt(qkv[1, rows, lanes], stacked_heads(qkv[0, rows, lanes], masks))
        flipped[unit] = qkv[2, rows, lanes].T
    for group in range(NGROUP):
        fenced = fence[group]
        for unit in (2 * group, 2 * group + 1):
            for head in range(HEADS // 2):
                cols = slice(head * GROUP, (head + 1) * GROUP)
                s = probs[unit, :, cols] + fenced
                p = jnp.exp2((s - jnp.max(s, axis=0, keepdims=True)) * EXP_SCALE)
                p = p * (1.0 / jnp.sum(p, axis=0, keepdims=True))
                probs[unit, :, cols] = p
                probs_low[unit, :, cols] = p.astype(BF16)
        rows = window(group)
        v = qkv[2, rows, :]
        moved = dot(shifts[group], v)
        low_row = lower[group] > 0.5
        low_row = jnp.concatenate([low_row, low_row], axis=1)
        lepe = bias + taps9[4] * v.astype(F32)
        lepe = lepe + taps9[3] * moved[0:GROUP] + taps9[5] * moved[GROUP : 2 * GROUP]
        for step in range(3):
            tap = jnp.where(low_row, taps9[step], taps9[6 + step])
            lepe = lepe + tap * moved[(2 + step) * GROUP : (3 + step) * GROUP]
        local[group] = lepe
    for unit, (group, half) in enumerate(units):
        rows = window(group)
        lanes = slice(half * HALF, (half + 1) * HALF)
        attended = picked_heads(dot(flipped[unit], probs_low[unit])).T
        put_window(mixed_att.at[half], group, attended + local[group, :, lanes])
    mixed[:, :HALF] = mixed_att[0]
    mixed[:, HALF:] = dot(turned[...], mixed_att[1]).astype(BF16)
    middle[...] = dot(mixed[...], wp[...])
    sides = ((slice(0, 160), ROWS[:2]), (slice(160, MB_TOK), ROWS[2:]))
    for side, chunks in sides:
        for start, size in chunks:
            rows = pl.ds(start, size)
            mid = x_ref[rows, :].astype(F32) + middle[rows, :] + vec_at(vec, 6)
            middle[rows, :] = mid
            hat, scale, y = norm_forward(mid, vec_at(vec, 1), vec_at(vec, 3))
            hat2[rows, :] = hat
            scale2[rows, :] = jnp.broadcast_to(scale, (size, HALF))
            normed2[rows, :] = y.astype(BF16)
        hidden[side, :] = dot(normed2[side, :], w1[...])
    for side, chunks in sides:
        for start, size in chunks:
            rows = pl.ds(start, size)
            for part in range(4):
                cols = slice(part * D, (part + 1) * D)
                h = hidden[rows, cols] + vec_at(vec, 9 + part)
                cdf = 0.5 * (1.0 + lax.erf(h * 0.7071067811865476))
                pdf = 0.3989422804014327 * jnp.exp(-0.5 * h * h)
                activ[rows, cols] = (h * cdf).astype(BF16)
                slope[rows, cols] = cdf + h * pdf
        out_ref[side, :] = dot(activ[side, :], w2[...]) + middle[side, :] + vec_at(vec, 8)


def backward_block(up_ref, grad_ref, vec_ref, taps_ref, w, saved, tables, work, sums, small):
    wq, wp, w1, w2 = w
    (hat1, scale1, normed, qkv, probs, probs_low, mixed, hat2, scale2, normed2, slope, activ) = saved
    turned, shifts, fence, lower = tables
    branch, gact, ghid, gmid, gmix, dqkv, dnat, gnorm, gprobs, gscores, flipped, local = work
    early, inner, outer = sums
    vec = vec_ref[...]
    branch[...] = up_ref[...].astype(BF16)
    sums = column_sum(branch[...])
    small[8:9, :] = sums
    gact[...] = dot_nt(branch[...], w2[...])
    parts = [jnp.zeros((1, D), F32) for _ in range(4)]
    for turn, (start, size) in enumerate(ROWS):
        rows = pl.ds(start, size)
        outer[turn * D : (turn + 1) * D, :] = dot_tn(activ[:, turn * D : (turn + 1) * D], branch[...]).astype(BF16)
        for part in range(4):
            cols = slice(part * D, (part + 1) * D)
            low = (gact[rows, cols] * slope[rows, cols]).astype(BF16)
            ghid[rows, cols] = low
            parts[part] = parts[part] + column_sum(low)
    for part in range(4):
        small[9 + part : 10 + part, :] = parts[part]
    gnorm[...] = dot_nt(ghid[...], w1[...])
    gains, offsets, outs = (jnp.zeros((1, D), F32) for _ in range(3))
    for turn, (start, size) in enumerate(ROWS):
        rows = pl.ds(start, size)
        inner[turn * D : (turn + 1) * D, :] = dot_tn(normed2[...], ghid[:, turn * D : (turn + 1) * D]).astype(BF16)
        g = gnorm[rows, :]
        hat = hat2[rows, :]
        scale = scale2[rows, :]
        gains = gains + column_sum(g * hat)
        offsets = offsets + column_sum(g)
        full = jnp.concatenate([scale, scale], axis=1)
        total = up_ref[rows, :].astype(F32) + norm_backward(g, hat, full, vec_at(vec, 1))
        gmid[rows, :] = total
        low = total.astype(BF16)
        branch[rows, :] = low
        outs = outs + column_sum(low)
    small[1:2, :] = gains
    small[3:4, :] = offsets
    small[6:7, :] = outs
    low = dot_nt(branch[...], wp[...]).astype(BF16)
    small[7:8, :] = column_sum(low)
    gmix[0:MB_TOK, :HALF] = low[:, :HALF]
    gmix[0:MB_TOK, HALF:] = dot(turned[...], low[:, HALF:]).astype(BF16)
    masks = head_masks()
    taps9 = turned_taps(taps_ref[...])
    tap_sums = [jnp.zeros((1, D), F32) for _ in range(9)]
    for start, size in ROWS:
        rows = pl.ds(start, size)
        tap_sums[4] = tap_sums[4] + column_sum(qkv[2, rows, :].astype(F32) * gmix[rows, :].astype(F32))
    units = [(group, half) for group in range(NGROUP) for half in range(2)]
    for unit, (group, half) in enumerate(units):
        rows = window(group)
        lanes = slice(half * HALF, (half + 1) * HALF)
        gprobs[unit] = dot_nt(qkv[2, rows, lanes], stacked_heads(gmix[rows, lanes], masks))
        flipped[unit] = qkv[1, rows, lanes].T
    for group in range(NGROUP):
        if group < 2:
            lanes = slice(group * HALF, (group + 1) * HALF)
            early[3 * D + group * HALF : 3 * D + (group + 1) * HALF, :] = dot_tn(mixed[:, lanes], branch[...]).astype(BF16)
        for unit in (2 * group, 2 * group + 1):
            for head in range(HEADS // 2):
                cols = slice(head * GROUP, (head + 1) * GROUP)
                p = probs[unit, :, cols]
                gp = gprobs[unit, :, cols]
                down = jnp.sum(gp * p, axis=0, keepdims=True)
                gscores[unit, :, cols] = (p * (gp - down)).astype(BF16)
        rows = window(group)
        g_low = gmix[rows, :]
        moved = dot(shifts[group], g_low)
        low_row = lower[group] > 0.5
        low_row = jnp.concatenate([low_row, low_row], axis=1)
        v32 = qkv[2, rows, :].astype(F32)
        g32 = g_low.astype(F32)
        left, right = moved[0:GROUP], moved[GROUP : 2 * GROUP]
        lepe = taps9[4] * g32 + taps9[3] * right + taps9[5] * left
        tap_sums[3] = tap_sums[3] + column_sum(v32 * right)
        tap_sums[5] = tap_sums[5] + column_sum(v32 * left)
        for step in range(3):
            at = moved[(4 - step) * GROUP : (5 - step) * GROUP]
            lepe = lepe + jnp.where(low_row, taps9[6 + step], taps9[step]) * at
            product = v32 * at
            tap_sums[6 + step] = tap_sums[6 + step] + column_sum(jnp.where(low_row, product, 0.0))
            tap_sums[step] = tap_sums[step] + column_sum(jnp.where(low_row, 0.0, product))
        local[group] = lepe
    for unit, (group, half) in enumerate(units):
        rows = window(group)
        lanes = slice(half * HALF, (half + 1) * HALF)
        low_s = gscores[unit]
        grad_v = dot(probs_low[unit], stacked_heads(gmix[rows, lanes], masks)) + local[group, :, lanes]
        grad_k = dot(low_s, stacked_heads(qkv[0, rows, lanes], masks)) * SCALE
        grad_q = picked_heads(dot(flipped[unit], low_s)).T * SCALE
        put_window(dqkv.at[half], group, jnp.concatenate([grad_q, grad_k, grad_v], axis=1))
    for index in range(9):
        tap = index
        turned_index = 3 * (index % 3) + index // 3
        small[13 + index : 14 + index, :] = jnp.concatenate(
            [tap_sums[tap][:, :HALF], tap_sums[turned_index][:, HALF:]], axis=1
        )
    for half in range(2):
        both = dqkv[half]
        natural = both if half == 0 else dot(turned[...], both).astype(BF16)
        for part in range(3):
            dnat[:, part * D + half * HALF : part * D + (half + 1) * HALF] = natural[
                :, part * HALF : (part + 1) * HALF
            ]
    gnorm[...] = dot_nt(dnat[...], wq[...])
    gains, offsets = (jnp.zeros((1, D), F32) for _ in range(2))
    for turn, (start, size) in enumerate(ROWS):
        rows = pl.ds(start, size)
        if turn < 2:
            both = dqkv[turn]
            lanes = slice(turn * HALF, (turn + 1) * HALF)
            small[4:5, lanes] = column_sum(both[:, 0:HALF])
            small[5:6, lanes] = column_sum(both[:, D : 3 * HALF])
            grads = dot_tn(normed[turn], both)
            for part in range(3):
                early[part * D : (part + 1) * D, lanes] = grads[:, part * HALF : (part + 1) * HALF].astype(BF16)
        g = gnorm[rows, :]
        hat = hat1[rows, :]
        scale = scale1[rows, :]
        gains = gains + column_sum(g * hat)
        offsets = offsets + column_sum(g)
        full = jnp.concatenate([scale, scale], axis=1)
        grad_ref[rows, :] = gmid[rows, :] + norm_backward(g, hat, full, vec_at(vec, 0))
    small[0:1, :] = gains
    small[2:3, :] = offsets
    outer[FF : FF + 32, :] = small[...].astype(BF16)


SAVED = [
    ((MB_TOK, D), F32),
    ((MB_TOK, HALF), F32),
    ((2, MB_TOK, D), BF16),
    ((3, LONG_TOK, D), BF16),
    ((2 * NGROUP, GROUP, 4 * GROUP), F32),
    ((2 * NGROUP, GROUP, 4 * GROUP), BF16),
    ((MB_TOK, D), BF16),
    ((MB_TOK, D), F32),
    ((MB_TOK, HALF), F32),
    ((MB_TOK, D), BF16),
    ((MB_TOK, FF), F32),
    ((MB_TOK, FF), BF16),
]
FORWARD_WORK = [
    ((2, MB_TOK, HALF), BF16),
    ((MB_TOK, D), F32),
    ((MB_TOK, FF), F32),
    ((2 * NGROUP, GROUP, GROUP), BF16),
    ((NGROUP, GROUP, D), F32),
]
BACKWARD_WORK = [
    ((MB_TOK, D), BF16),
    ((MB_TOK, FF), F32),
    ((MB_TOK, FF), BF16),
    ((MB_TOK, D), F32),
    ((LONG_TOK, D), BF16),
    ((2, MB_TOK, 3 * HALF), BF16),
    ((MB_TOK, 3 * D), BF16),
    ((MB_TOK, D), F32),
    ((2 * NGROUP, GROUP, 4 * GROUP), F32),
    ((2 * NGROUP, GROUP, 4 * GROUP), BF16),
    ((2 * NGROUP, GROUP, GROUP), BF16),
    ((NGROUP, GROUP, D), F32),
]


INPUTS = [
    ((MB_TOK, D), BF16),
    ((MB_TOK, D), BF16),
    ((2, 1, VEC), F32),
    ((2, 1, 9 * D), F32),
    ((2, D, 8 * D), BF16),
    ((2, FF, D), BF16),
    ((MB_TOK, MB_TOK), BF16),
    ((NGROUP, 5 * GROUP, GROUP), BF16),
    ((NGROUP, GROUP, GROUP), F32),
    ((NGROUP, GROUP, HALF), F32),
]
RESULTS = [((2, MB_TOK, D), F32), ((2, MB_TOK, D), F32)] + [((2, rows, D), BF16) for rows in PARTS]
OTHER_WORK = [((MB_TOK, D), BF16), ((32, D), F32)]


def section_step(sec_ref, *refs):
    def take(count):
        nonlocal refs
        taken, refs = refs[:count], refs[count:]
        return taken

    x_in, c_in, vec_own, vec_other, ker_own, ker_other, wide_own, wide_other, deep_own, deep_other = take(10)
    table_in = take(4)
    rows_out, (rows_sent,), sent = take(2), take(1), [take(2) for _ in PARTS]
    held = take(len(INPUTS))
    results = take(len(RESULTS))
    kept = (take(len(SAVED)), take(len(SAVED)))
    forward_work = take(len(FORWARD_WORK))
    backward_work = take(len(BACKWARD_WORK))
    feed, small, in_sems, out_sems = refs
    x, c, vecs, taps, wide, deep = held[:6]
    tables = held[6:]
    sec = sec_ref[0]
    at = pl.multiple_of(sec * MB_TOK, 16)
    moves = [
        ("x", x_in.at[pl.ds(at, MB_TOK)], x),
        ("vec", vec_own, vecs.at[sec]),
        ("vec", vec_other, vecs.at[1 - sec]),
        ("rest", table_in[0], tables[0]),
        ("rest", wide_own, wide.at[sec]),
        ("rest", wide_other, wide.at[1 - sec]),
        ("rest", table_in[1], tables[1]),
        ("rest", table_in[2], tables[2]),
        ("rest", table_in[3], tables[3]),
        ("rest", ker_own, taps.at[sec]),
        ("rest", ker_other, taps.at[1 - sec]),
        ("rest", deep_own, deep.at[sec]),
        ("rest", deep_other, deep.at[1 - sec]),
        ("rest", c_in.at[pl.ds(at, MB_TOK)], c),
    ]
    pending = {}
    for index, (name, source, target) in enumerate(moves):
        copy = pltpu.make_async_copy(source, target, in_sems.at[index])
        copy.start()
        pending.setdefault(name, []).append(copy)

    def need(*names):
        for name in names:
            for copy in pending.pop(name, []):
                copy.wait()

    leaving = []

    def leave(index):
        targets = (rows_out[index].at[pl.ds(at, MB_TOK)], rows_sent.at[index]) if index < 2 else sent[index - 2]
        for which, slot in enumerate((sec, 1 - sec)):
            copy = pltpu.make_async_copy(results[index].at[slot], targets[which], out_sems.at[2 * index + which])
            copy.start()
            leaving.append(copy)

    outs, grads, early, inner, outer = results
    small[...] = jnp.zeros_like(small)
    for b in range(2):
        kept[b][3][:, MB_TOK:, :] = jnp.zeros((3, LONG_TOK - MB_TOK, D), BF16)
    backward_work[4][MB_TOK:, :] = jnp.zeros((LONG_TOK - MB_TOK, D), BF16)
    for part, rows in zip((early, inner, outer), PARTS):
        if rows > FF:
            part[:, FF:, :] = jnp.zeros((2, rows - FF, D), BF16)
    weights = [
        (wide.at[b, :, 0 : 3 * D], wide.at[b, :, 3 * D : 4 * D], wide.at[b, :, 4 * D : 8 * D], deep.at[b])
        for b in range(2)
    ]
    sums = [(early.at[b], inner.at[b], outer.at[b]) for b in range(2)]

    def forward(b, source):
        forward_block(
            source, outs.at[b], vecs.at[b], taps.at[b], weights[b], kept[b], tables, forward_work, need
        )

    def backward(b, source):
        backward_block(
            source, grads.at[b], vecs.at[b], taps.at[b], weights[b], kept[b], tables, backward_work, sums[b], small
        )

    forward(0, x)
    feed[...] = outs[0].astype(BF16)
    forward(1, feed)
    backward(1, c)
    feed[...] = grads[1].astype(BF16)
    backward(0, feed)
    for index in range(len(RESULTS)):
        leave(index)
    for copy in leaving:
        copy.wait()


def run_blocks(sec, *arrays):
    shifts, fence, lower = stripe_tables()
    tables = (
        jnp.asarray(turned_table(), BF16),
        jnp.asarray(shifts, BF16),
        jnp.asarray(fence, F32),
        jnp.asarray(lower, F32),
    )
    spaces = [pltpu.HBM] * 3 + [pltpu.VMEM, pltpu.HBM] + [pltpu.VMEM] * 5 + [pltpu.HBM] * 4
    smem = pl.BlockSpec(memory_space=pltpu.SMEM)
    scratch = INPUTS + RESULTS + SAVED + SAVED + FORWARD_WORK + BACKWARD_WORK + OTHER_WORK
    out_shape = [pltpu.HBM((2 * MB_TOK, D), F32)] * 2 + [pltpu.VMEM((2, MB_TOK, D), F32)]
    out_shape += [pltpu.VMEM((rows, D), BF16) for rows in PARTS for _ in range(2)]
    return pl.pallas_call(
        section_step,
        out_shape=out_shape,
        in_specs=[smem] + [pl.BlockSpec(memory_space=space) for space in spaces],
        out_specs=[pl.BlockSpec(memory_space=pltpu.HBM)] * 2 + [pl.BlockSpec(memory_space=pl.ANY)] * 7,
        scratch_shapes=[pltpu.VMEM(shape, kind) for shape, kind in scratch]
        + [pltpu.SemaphoreType.DMA((14,)), pltpu.SemaphoreType.DMA((2 * len(RESULTS),))],
        compiler_params=pltpu.CompilerParams(vmem_limit_bytes=34 << 20),
        name="blocks",
    )(sec, *kept_in(arrays + tables, spaces))


NARROW = (((D, 3 * D), 0), ((D, D), 3 * D), ((D, FF), 4 * D), ((FF, D), None))


def narrowed(*refs):
    sources, (wide, deep), held, (sems,) = refs[:4], refs[4:6], refs[6:10], refs[10:]
    coming = [pltpu.make_async_copy(sources[k], held[k], sems.at[k]) for k in range(4)]
    for copy in coming:
        copy.start()
    for k, (shape, first) in enumerate(NARROW):
        coming[k].wait()
        if first is None:
            deep[...] = held[k][...].astype(BF16)
        else:
            wide[:, first : first + shape[1]] = held[k][...].astype(BF16)


def run_narrowed(*weights):
    vmem = pl.BlockSpec(memory_space=pltpu.VMEM)
    return pl.pallas_call(
        narrowed,
        out_shape=[pltpu.VMEM((D, 8 * D), BF16), pltpu.VMEM((FF, D), BF16)],
        in_specs=[pl.BlockSpec(memory_space=pltpu.HBM)] * 4,
        out_specs=[vmem] * 2,
        scratch_shapes=[pltpu.VMEM(shape, F32) for shape, _ in NARROW] + [pltpu.SemaphoreType.DMA((4,))],
        compiler_params=pltpu.CompilerParams(vmem_limit_bytes=8 << 20),
        name="narrowed",
    )(*kept_in(weights, [pltpu.HBM] * 4))


def square_sum(a_ref, b_ref, c_ref, out_ref):
    total = jnp.zeros((8, D), F32)
    for ref in (a_ref, b_ref, c_ref):
        step = 64
        for start in range(0, ref.shape[0], step):
            rows = ref[start : start + step, :].astype(F32)
            square = rows * rows
            for at in range(0, step, 8):
                total = total + square[at : at + 8]
    total = jnp.sum(jnp.sum(total, axis=0, keepdims=True), axis=1, keepdims=True)
    out_ref[...] = jnp.broadcast_to(total, (8, HALF))


def run_square_sum(a, b, c):
    vmem = pl.BlockSpec(memory_space=pltpu.VMEM)
    return pl.pallas_call(
        square_sum,
        out_shape=jax.ShapeDtypeStruct((8, HALF), F32),
        in_specs=[vmem] * 3,
        out_specs=vmem,
        compiler_params=pltpu.CompilerParams(vmem_limit_bytes=16 << 20),
        name="squares",
    )(a, b, c)


def updated(grad, weight, moment, average, factor):
    decay = min(0.9999, (1.0 + STEP) / (10.0 + STEP))
    clipped = grad * factor
    direction = clipped + WEIGHT_DECAY * weight
    moment_new = MOMENTUM_DECAY * moment + direction
    weight_new = weight - LEARN_RATE * (direction + MOMENTUM_DECAY * moment_new)
    average_new = decay * average + (1.0 - decay) * weight_new
    return clipped, moment_new, weight_new, average_new


SHAPES = ((1, VEC), (1, 9 * D), (D, 3 * D), (D, D), (D, FF), (FF, D))
PIECES = ((3, 0, D), (2, 0, D), (4, 0, D), (5, 0, FF))
OUT_SHAPES = [(shape, F32) for shape in SHAPES] * 4 + [(shape, BF16) for shape in SHAPES[2:]]
MOVES = 2 + 4 * 2 + 5 * len(PIECES)


def optimizer_step(sec_ref, *refs):
    def take(count):
        nonlocal refs
        taken, refs = refs[:count], refs[count:]
        return taken

    (_, _, came), (own, other), (a, b, c), states = take(3), take(2), take(3), take(18)
    outs, (norm_ref,), rows_out, made, (sems,) = take(28), take(1), take(2), take(28), take(1)
    sec = sec_ref[0]
    moves = []

    def leave(source, target):
        move = pltpu.make_async_copy(source, target, sems.at[len(moves)])
        move.start()
        moves.append(move)

    first = pl.multiple_of((1 - sec) * MB_TOK, 8)
    for index in range(2):
        leave(came.at[index], rows_out[index].at[pl.ds(first, MB_TOK)])
    norm = jnp.sqrt(own[0:1, 0:1] + other[0:1, 0:1])
    factor = jnp.minimum(1.0, CLIP_LIMIT / (norm + 1e-06))
    norm_ref[...] = norm

    def put(index, rows, lanes, grad):
        weight, moment, average = (states[kind * 6 + index][rows, lanes] for kind in range(3))
        new = updated(grad, weight, moment, average, factor)
        for kind in range(4):
            made[kind * 6 + index][rows, lanes] = new[kind]
        if index >= 2:
            made[24 + index - 2][rows, lanes] = new[2].astype(BF16)

    places = {2: [(a, 0), (a, D), (a, 2 * D)], 3: [(a, 3 * D)], 4: [(b, part * D) for part in range(4)], 5: [(c, 0)]}
    step = 32
    for index, first, count in PIECES:
        for row in range(first, first + count, step):
            for part, (ref, base) in enumerate(places[index]):
                grad = ref[base + row : base + row + step, :].astype(F32)
                put(index, slice(row, row + step), slice(part * D, (part + 1) * D), grad)
        rows = pl.ds(first, count)
        for kind in range(5):
            at = kind * 6 + index if kind < 4 else 24 + index - 2
            leave(made[at].at[rows], outs[at].at[rows])
    rows = c[FF : FF + 32, :].astype(F32)
    whole = slice(0, 1)
    for part in range(13):
        put(0, whole, slice(part * D, (part + 1) * D), rows[part : part + 1, :])
    for part in range(9):
        put(1, whole, slice(part * D, (part + 1) * D), rows[13 + part : 14 + part, :])
    for index in range(2):
        for kind in range(4):
            leave(made[kind * 6 + index], outs[kind * 6 + index])
    for move in moves:
        move.wait()


def run_optimizer(sec, rows, came, own, other, a, b, c, states):
    vmem = pl.BlockSpec(memory_space=pltpu.VMEM)
    hbm = pl.BlockSpec(memory_space=pltpu.HBM)
    return pl.pallas_call(
        optimizer_step,
        out_shape=[pltpu.HBM(shape, kind) for shape, kind in OUT_SHAPES]
        + [jax.ShapeDtypeStruct((1, 1), F32)]
        + [pltpu.HBM((2 * MB_TOK, D), F32)] * 2,
        in_specs=[pl.BlockSpec(memory_space=pltpu.SMEM)] + [hbm] * 2 + [vmem] * (1 + 2 + 3 + 18),
        out_specs=[hbm] * 28 + [vmem] + [hbm] * 2,
        scratch_shapes=[pltpu.VMEM(shape, kind) for shape, kind in OUT_SHAPES] + [pltpu.SemaphoreType.DMA((MOVES,))],
        compiler_params=pltpu.CompilerParams(vmem_limit_bytes=20 << 20),
        input_output_aliases={1: 29, 2: 30},
        name="optimizer",
    )(sec, *kept_in((*rows, came, own, other, a, b, c, *states), [pltpu.HBM] * 2 + [pltpu.VMEM] * 24))


def swapped(value):
    return lax.ppermute(value, "section", [(0, 1), (1, 0)])


def exchange_orders(bits):
    if bits == 4:
        return ((0, 1, 2, 3), (1, 2, 0, 3), (2, 0, 1, 3))
    turn = max(1, bits // 3)
    every = tuple(range(bits))
    return tuple(every[turn * part :] + every[: turn * part] for part in range(3))


def exchanged(value, bit, size):
    return lax.ppermute(value, "dp", [(index, index ^ (1 << bit)) for index in range(size)])


def exchange_bits():
    size = lax.axis_size("dp")
    bits = size.bit_length() - 1
    if size < 2 or size != 1 << bits or any(2 * rows % size for rows in PARTS):
        return []
    index = lax.axis_index("dp")
    return [((index >> bit) & 1) == 0 for bit in range(bits)]


def summed_over_dp(parts, clear):
    size = lax.axis_size("dp")
    bits = len(clear)
    if not bits:
        return [lax.psum(part.astype(F32), "dp").astype(BF16) for part in parts]
    orders = exchange_orders(bits)
    shapes = [part.shape for part in parts]
    held = [part.reshape((2,) * (bits - 1) + (2 * part.shape[0] // size, D)) for part in parts]
    for step in range(bits):
        kept, came = held, []
        if step < bits - 1:
            kept = [jnp.where(clear[order[step]], value[0], value[1]) for value, order in zip(held, orders)]
            held = [jnp.where(clear[order[step]], value[1], value[0]) for value, order in zip(held, orders)]
        came = [exchanged(value, order[step], size) for value, order in zip(held, orders)]
        held = [(a.astype(F32) + b.astype(F32)).astype(BF16) for a, b in zip(kept, came)]
    for step in reversed(range(bits - 1)):
        grown = []
        for value, order in zip(held, orders):
            low = clear[order[step]]
            came = exchanged(value, order[step], size)
            grown.append(jnp.stack([jnp.where(low, value, came), jnp.where(low, came, value)]))
        held = grown
    return [value.reshape(shape) for value, shape in zip(held, shapes)]


def per_device(inputs, cotangent, *states):
    states = [array.reshape(1, 9 * D) if array.shape == (1, 9, D) else array for array in states]
    states = [array.reshape(array.shape[1:]) if array.ndim == 3 else array for array in states]
    vectors, kernels = states[:2]
    section = lax.axis_index("section").astype(jnp.int32).reshape(1)
    section, *clear = lax.optimization_barrier((section, *exchange_bits()))
    wide, deep = run_narrowed(*states[2:6])
    results = run_blocks(
        section,
        inputs,
        cotangent,
        vectors,
        swapped(vectors),
        kernels,
        swapped(kernels),
        wide,
        swapped(wide),
        deep,
        swapped(deep),
    )
    totals = [
        (own.astype(F32) + swapped(other).astype(F32)).astype(BF16)
        for own, other in zip(results[3::2], results[4::2])
    ]
    a, b, c = summed_over_dp(totals, clear)
    squares = run_square_sum(a, b, c)
    new = run_optimizer(section, results[:2], swapped(results[2]), squares, swapped(squares), a, b, c, states)

    def whole(arrays):
        return [
            array if array.shape == (1, VEC) else array.reshape(1, 9, D) if array.shape == (1, 9 * D) else array[None]
            for array in arrays
        ]

    return (new[29][None], new[30][None], *whole(new[0:6]), new[28].reshape(()), *whole(new[6:28]))


def solution(mesh):
    rows = P("dp", None)
    state = (P("section", None),) + (P("section", None, None),) * 5
    return jax.shard_map(
        per_device,
        mesh=mesh,
        in_specs=(rows, rows) + state * 3,
        out_specs=(P("section", "dp", None),) * 2 + state + (P(),) + state * 3 + state[2:],
        check_vma=False,
    )
```

```python
import jax
import jax.numpy as jnp
import numpy as np
from jax import lax
from jax.experimental import pallas as pl
from jax.experimental.pallas import tpu as pltpu
from jax.sharding import PartitionSpec as P

D = 256
HALF = 128
HEADS = 8
HEAD = 32
FF = 1024
BIG_SIDE = 14
SMALL_SIDE = 6
BIG_MB = 1
SMALL_MB = 3
STEP = 8
MB_TOK = 304
VEC = 3328

NORM_EPS = 1e-05
CLIP_LIMIT = 5.0
LEARN_RATE = 4.0
MOMENTUM_DECAY = 0.9
WEIGHT_DECAY = 5e-05

F32 = jnp.float32
BF16 = jnp.bfloat16

GROUP = 128
WINDOWS = ((0, BIG_SIDE, 0, 112), (112, BIG_SIDE, 0, 84), (192, SMALL_SIDE, 4, 108))
NGROUP = len(WINDOWS)
LONG_TOK = 320
SCALE = HEAD ** -0.5
LOG2E = 1.4426950408889634
EXP_SCALE = SCALE * LOG2E
OFF = -1e30
ROWS = ((0, 80), (80, 80), (160, 80), (240, 64))
PARTS = (1024, 1024, 1088)


def turned_table():
    turned = np.zeros((MB_TOK, MB_TOK), np.float32)
    base = 0
    for side, count in ((BIG_SIDE, BIG_MB), (SMALL_SIDE, SMALL_MB)):
        for _ in range(count):
            for row in range(side):
                for col in range(side):
                    turned[base + row * side + col, base + col * side + row] = 1.0
            base += side * side
    return turned


def stripe_tables():
    shifts = np.zeros((NGROUP, 5 * GROUP, GROUP), np.float32)
    fence = np.full((NGROUP, GROUP, GROUP), OFF, np.float32)
    lower = np.zeros((NGROUP, GROUP, HALF), np.float32)
    for kind, (_, side, first, size) in enumerate(WINDOWS):
        stripe = 2 * side
        number = (np.arange(GROUP) - first) // stripe
        number[:first] = -1
        number[first + size :] = GROUP
        fence[kind][number[:, None] == number[None, :]] = 0.0
        for at in range(size):
            own, inner = divmod(at, stripe)
            row, col = divmod(inner, side)
            lower[kind, first + at, :] = float(row)
            moves = ((row, col - 1), (row, col + 1), (1 - row, col - 1), (1 - row, col), (1 - row, col + 1))
            for move, (to_row, to_col) in enumerate(moves):
                if 0 <= to_col < side:
                    target = first + own * stripe + to_row * side + to_col
                    shifts[kind, move * GROUP + first + at, target] = 1.0
    return shifts, fence, lower


def kept_in(arrays, spaces):
    return [pltpu.with_memory_space_constraint(array, space) for array, space in zip(arrays, spaces)]


def dot(a, b):
    return jnp.dot(a, b, preferred_element_type=F32)


def dot_nt(a, b):
    return lax.dot_general(a, b, (((1,), (1,)), ((), ())), preferred_element_type=F32)


def dot_tn(a, b):
    return lax.dot_general(a, b, (((0,), (0,)), ((), ())), preferred_element_type=F32)


def head_masks():
    lane = lax.broadcasted_iota(jnp.int32, (1, HALF), 1) // HEAD
    return [(lane == head).astype(BF16) for head in range(HEADS // 2)]


def stacked_heads(rows, masks):
    return jnp.concatenate([rows * mask for mask in masks], axis=0)


def picked_heads(product):
    return jnp.concatenate(
        [
            product[HEAD * head : HEAD * (head + 1), GROUP * head : GROUP * (head + 1)]
            for head in range(HEADS // 2)
        ],
        axis=0,
    )


def turned_taps(taps):
    turned = [3 * (index % 3) + index // 3 for index in range(9)]
    return [
        jnp.concatenate(
            [taps[:, index * D : index * D + HALF], taps[:, turned[index] * D + HALF : (turned[index] + 1) * D]],
            axis=1,
        )
        for index in range(9)
    ]


def norm_forward(x, gain, offset):
    centre = x - jnp.mean(x, axis=-1, keepdims=True)
    spread = jnp.mean(centre * centre, axis=-1, keepdims=True)
    scale = lax.rsqrt(spread + NORM_EPS)
    hat = centre * scale
    return hat, scale, hat * gain + offset


def norm_backward(grad, hat, scale, gain):
    inner = grad * gain
    mean_inner = jnp.mean(inner, axis=-1, keepdims=True)
    mean_cross = jnp.mean(inner * hat, axis=-1, keepdims=True)
    return scale * (inner - mean_inner - hat * mean_cross)


def column_sum(x):
    return jnp.sum(x.astype(F32), axis=0, keepdims=True)


def window(group):
    return pl.ds(WINDOWS[group][0], GROUP)


def put_window(ref, group, value):
    if group == 0:
        ref[0:112, :] = value[0:112].astype(BF16)
    elif group == 1:
        ref[112:208, :] = value[0:96].astype(BF16)
    else:
        before = lax.broadcasted_iota(jnp.int32, (16, value.shape[1]), 0) < 4
        ref[192:208, :] = jnp.where(before, ref[192:208, :].astype(F32), value[0:16]).astype(BF16)
        ref[208:304, :] = value[16:112].astype(BF16)


def vec_at(vec, index, width=1):
    return vec[:, index * D : (index + width) * D]


def forward_block(x_ref, out_ref, vec_ref, taps_ref, w, saved, tables, work, need):
    wq, wp, w1, w2 = w
    (hat1, scale1, normed, qkv, probs, probs_low, mixed, hat2, scale2, normed2, slope, activ) = saved
    turned, shifts, fence, lower = tables
    mixed_att, middle, hidden, flipped, local = work
    need("x", "vec")
    vec = vec_ref[...]
    for start, size in ROWS:
        rows = pl.ds(start, size)
        hat, scale, y = norm_forward(x_ref[rows, :].astype(F32), vec_at(vec, 0), vec_at(vec, 2))
        hat1[rows, :] = hat
        scale1[rows, :] = jnp.broadcast_to(scale, (size, HALF))
        normed[0, rows, :] = y.astype(BF16)
    need("rest")
    normed[1] = dot(turned[...], normed[0]).astype(BF16)
    biases = (vec_at(vec, 4), None, vec_at(vec, 5))
    for half in range(2):
        lanes = slice(half * HALF, (half + 1) * HALF)
        for part in range(3):
            got = dot(normed[half], wq[:, part * D + half * HALF : part * D + (half + 1) * HALF])
            if biases[part] is not None:
                got = got + biases[part][:, lanes]
            qkv[part, 0:MB_TOK, lanes] = got.astype(BF16)
    masks = head_masks()
    taps9 = turned_taps(taps_ref[...])
    bias = vec_at(vec, 7)
    units = [(group, half) for group in range(NGROUP) for half in range(2)]
    for unit, (group, half) in enumerate(units):
        rows = window(group)
        lanes = slice(half * HALF, (half + 1) * HALF)
        probs[unit] = dot_nt(qkv[1, rows, lanes], stacked_heads(qkv[0, rows, lanes], masks))
        flipped[unit] = qkv[2, rows, lanes].T
    for group in range(NGROUP):
        fenced = fence[group]
        for unit in (2 * group, 2 * group + 1):
            for head in range(HEADS // 2):
                cols = slice(head * GROUP, (head + 1) * GROUP)
                s = probs[unit, :, cols] + fenced
                p = jnp.exp2((s - jnp.max(s, axis=0, keepdims=True)) * EXP_SCALE)
                p = p * (1.0 / jnp.sum(p, axis=0, keepdims=True))
                probs[unit, :, cols] = p
                probs_low[unit, :, cols] = p.astype(BF16)
        rows = window(group)
        v = qkv[2, rows, :]
        moved = dot(shifts[group], v)
        low_row = lower[group] > 0.5
        low_row = jnp.concatenate([low_row, low_row], axis=1)
        lepe = bias + taps9[4] * v.astype(F32)
        lepe = lepe + taps9[3] * moved[0:GROUP] + taps9[5] * moved[GROUP : 2 * GROUP]
        for step in range(3):
            tap = jnp.where(low_row, taps9[step], taps9[6 + step])
            lepe = lepe + tap * moved[(2 + step) * GROUP : (3 + step) * GROUP]
        local[group] = lepe
    for unit, (group, half) in enumerate(units):
        rows = window(group)
        lanes = slice(half * HALF, (half + 1) * HALF)
        attended = picked_heads(dot(flipped[unit], probs_low[unit])).T
        put_window(mixed_att.at[half], group, attended + local[group, :, lanes])
    mixed[:, :HALF] = mixed_att[0]
    mixed[:, HALF:] = dot(turned[...], mixed_att[1]).astype(BF16)
    middle[...] = dot(mixed[...], wp[...])
    sides = ((slice(0, 160), ROWS[:2]), (slice(160, MB_TOK), ROWS[2:]))
    for side, chunks in sides:
        for start, size in chunks:
            rows = pl.ds(start, size)
            mid = x_ref[rows, :].astype(F32) + middle[rows, :] + vec_at(vec, 6)
            middle[rows, :] = mid
            hat, scale, y = norm_forward(mid, vec_at(vec, 1), vec_at(vec, 3))
            hat2[rows, :] = hat
            scale2[rows, :] = jnp.broadcast_to(scale, (size, HALF))
            normed2[rows, :] = y.astype(BF16)
        hidden[side, :] = dot(normed2[side, :], w1[...])
    for side, chunks in sides:
        for start, size in chunks:
            rows = pl.ds(start, size)
            for part in range(4):
                cols = slice(part * D, (part + 1) * D)
                h = hidden[rows, cols] + vec_at(vec, 9 + part)
                cdf = 0.5 * (1.0 + lax.erf(h * 0.7071067811865476))
                pdf = 0.3989422804014327 * jnp.exp(-0.5 * h * h)
                activ[rows, cols] = (h * cdf).astype(BF16)
                slope[rows, cols] = cdf + h * pdf
        out_ref[side, :] = dot(activ[side, :], w2[...]) + middle[side, :] + vec_at(vec, 8)


def backward_block(up_ref, grad_ref, vec_ref, taps_ref, w, saved, tables, work, sums, small):
    wq, wp, w1, w2 = w
    (hat1, scale1, normed, qkv, probs, probs_low, mixed, hat2, scale2, normed2, slope, activ) = saved
    turned, shifts, fence, lower = tables
    branch, gact, ghid, gmid, gmix, dqkv, dnat, gnorm, gprobs, gscores, flipped, local = work
    early, inner, outer = sums
    vec = vec_ref[...]
    branch[...] = up_ref[...].astype(BF16)
    sums = column_sum(branch[...])
    small[8:9, :] = sums
    gact[...] = dot_nt(branch[...], w2[...])
    parts = [jnp.zeros((1, D), F32) for _ in range(4)]
    for turn, (start, size) in enumerate(ROWS):
        rows = pl.ds(start, size)
        outer[turn * D : (turn + 1) * D, :] = dot_tn(activ[:, turn * D : (turn + 1) * D], branch[...]).astype(BF16)
        for part in range(4):
            cols = slice(part * D, (part + 1) * D)
            low = (gact[rows, cols] * slope[rows, cols]).astype(BF16)
            ghid[rows, cols] = low
            parts[part] = parts[part] + column_sum(low)
    for part in range(4):
        small[9 + part : 10 + part, :] = parts[part]
    gnorm[...] = dot_nt(ghid[...], w1[...])
    gains, offsets, outs = (jnp.zeros((1, D), F32) for _ in range(3))
    for turn, (start, size) in enumerate(ROWS):
        rows = pl.ds(start, size)
        inner[turn * D : (turn + 1) * D, :] = dot_tn(normed2[...], ghid[:, turn * D : (turn + 1) * D]).astype(BF16)
        g = gnorm[rows, :]
        hat = hat2[rows, :]
        scale = scale2[rows, :]
        gains = gains + column_sum(g * hat)
        offsets = offsets + column_sum(g)
        full = jnp.concatenate([scale, scale], axis=1)
        total = up_ref[rows, :].astype(F32) + norm_backward(g, hat, full, vec_at(vec, 1))
        gmid[rows, :] = total
        low = total.astype(BF16)
        branch[rows, :] = low
        outs = outs + column_sum(low)
    small[1:2, :] = gains
    small[3:4, :] = offsets
    small[6:7, :] = outs
    low = dot_nt(branch[...], wp[...]).astype(BF16)
    small[7:8, :] = column_sum(low)
    gmix[0:MB_TOK, :HALF] = low[:, :HALF]
    gmix[0:MB_TOK, HALF:] = dot(turned[...], low[:, HALF:]).astype(BF16)
    masks = head_masks()
    taps9 = turned_taps(taps_ref[...])
    tap_sums = [jnp.zeros((1, D), F32) for _ in range(9)]
    for start, size in ROWS:
        rows = pl.ds(start, size)
        tap_sums[4] = tap_sums[4] + column_sum(qkv[2, rows, :].astype(F32) * gmix[rows, :].astype(F32))
    units = [(group, half) for group in range(NGROUP) for half in range(2)]
    for unit, (group, half) in enumerate(units):
        rows = window(group)
        lanes = slice(half * HALF, (half + 1) * HALF)
        gprobs[unit] = dot_nt(qkv[2, rows, lanes], stacked_heads(gmix[rows, lanes], masks))
        flipped[unit] = qkv[1, rows, lanes].T
    for group in range(NGROUP):
        if group < 2:
            lanes = slice(group * HALF, (group + 1) * HALF)
            early[3 * D + group * HALF : 3 * D + (group + 1) * HALF, :] = dot_tn(mixed[:, lanes], branch[...]).astype(BF16)
        for unit in (2 * group, 2 * group + 1):
            for head in range(HEADS // 2):
                cols = slice(head * GROUP, (head + 1) * GROUP)
                p = probs[unit, :, cols]
                gp = gprobs[unit, :, cols]
                down = jnp.sum(gp * p, axis=0, keepdims=True)
                gscores[unit, :, cols] = (p * (gp - down)).astype(BF16)
        rows = window(group)
        g_low = gmix[rows, :]
        moved = dot(shifts[group], g_low)
        low_row = lower[group] > 0.5
        low_row = jnp.concatenate([low_row, low_row], axis=1)
        v32 = qkv[2, rows, :].astype(F32)
        g32 = g_low.astype(F32)
        left, right = moved[0:GROUP], moved[GROUP : 2 * GROUP]
        lepe = taps9[4] * g32 + taps9[3] * right + taps9[5] * left
        tap_sums[3] = tap_sums[3] + column_sum(v32 * right)
        tap_sums[5] = tap_sums[5] + column_sum(v32 * left)
        for step in range(3):
            at = moved[(4 - step) * GROUP : (5 - step) * GROUP]
            lepe = lepe + jnp.where(low_row, taps9[6 + step], taps9[step]) * at
            product = v32 * at
            tap_sums[6 + step] = tap_sums[6 + step] + column_sum(jnp.where(low_row, product, 0.0))
            tap_sums[step] = tap_sums[step] + column_sum(jnp.where(low_row, 0.0, product))
        local[group] = lepe
    for unit, (group, half) in enumerate(units):
        rows = window(group)
        lanes = slice(half * HALF, (half + 1) * HALF)
        low_s = gscores[unit]
        grad_v = dot(probs_low[unit], stacked_heads(gmix[rows, lanes], masks)) + local[group, :, lanes]
        grad_k = dot(low_s, stacked_heads(qkv[0, rows, lanes], masks)) * SCALE
        grad_q = picked_heads(dot(flipped[unit], low_s)).T * SCALE
        put_window(dqkv.at[half], group, jnp.concatenate([grad_q, grad_k, grad_v], axis=1))
    for index in range(9):
        tap = index
        turned_index = 3 * (index % 3) + index // 3
        small[13 + index : 14 + index, :] = jnp.concatenate(
            [tap_sums[tap][:, :HALF], tap_sums[turned_index][:, HALF:]], axis=1
        )
    for half in range(2):
        both = dqkv[half]
        natural = both if half == 0 else dot(turned[...], both).astype(BF16)
        for part in range(3):
            dnat[:, part * D + half * HALF : part * D + (half + 1) * HALF] = natural[
                :, part * HALF : (part + 1) * HALF
            ]
    gnorm[...] = dot_nt(dnat[...], wq[...])
    gains, offsets = (jnp.zeros((1, D), F32) for _ in range(2))
    for turn, (start, size) in enumerate(ROWS):
        rows = pl.ds(start, size)
        if turn < 2:
            both = dqkv[turn]
            lanes = slice(turn * HALF, (turn + 1) * HALF)
            small[4:5, lanes] = column_sum(both[:, 0:HALF])
            small[5:6, lanes] = column_sum(both[:, D : 3 * HALF])
            grads = dot_tn(normed[turn], both)
            for part in range(3):
                early[part * D : (part + 1) * D, lanes] = grads[:, part * HALF : (part + 1) * HALF].astype(BF16)
        g = gnorm[rows, :]
        hat = hat1[rows, :]
        scale = scale1[rows, :]
        gains = gains + column_sum(g * hat)
        offsets = offsets + column_sum(g)
        full = jnp.concatenate([scale, scale], axis=1)
        grad_ref[rows, :] = gmid[rows, :] + norm_backward(g, hat, full, vec_at(vec, 0))
    small[0:1, :] = gains
    small[2:3, :] = offsets
    outer[FF : FF + 32, :] = small[...].astype(BF16)


SAVED = [
    ((MB_TOK, D), F32),
    ((MB_TOK, HALF), F32),
    ((2, MB_TOK, D), BF16),
    ((3, LONG_TOK, D), BF16),
    ((2 * NGROUP, GROUP, 4 * GROUP), F32),
    ((2 * NGROUP, GROUP, 4 * GROUP), BF16),
    ((MB_TOK, D), BF16),
    ((MB_TOK, D), F32),
    ((MB_TOK, HALF), F32),
    ((MB_TOK, D), BF16),
    ((MB_TOK, FF), F32),
    ((MB_TOK, FF), BF16),
]
FORWARD_WORK = [
    ((2, MB_TOK, HALF), BF16),
    ((MB_TOK, D), F32),
    ((MB_TOK, FF), F32),
    ((2 * NGROUP, GROUP, GROUP), BF16),
    ((NGROUP, GROUP, D), F32),
]
BACKWARD_WORK = [
    ((MB_TOK, D), BF16),
    ((MB_TOK, FF), F32),
    ((MB_TOK, FF), BF16),
    ((MB_TOK, D), F32),
    ((LONG_TOK, D), BF16),
    ((2, MB_TOK, 3 * HALF), BF16),
    ((MB_TOK, 3 * D), BF16),
    ((MB_TOK, D), F32),
    ((2 * NGROUP, GROUP, 4 * GROUP), F32),
    ((2 * NGROUP, GROUP, 4 * GROUP), BF16),
    ((2 * NGROUP, GROUP, GROUP), BF16),
    ((NGROUP, GROUP, D), F32),
]


INPUTS = [
    ((MB_TOK, D), BF16),
    ((MB_TOK, D), BF16),
    ((2, 1, VEC), F32),
    ((2, 1, 9 * D), F32),
    ((2, D, 8 * D), BF16),
    ((2, FF, D), BF16),
    ((MB_TOK, MB_TOK), BF16),
    ((NGROUP, 5 * GROUP, GROUP), BF16),
    ((NGROUP, GROUP, GROUP), F32),
    ((NGROUP, GROUP, HALF), F32),
]
RESULTS = [((2, MB_TOK, D), F32), ((2, MB_TOK, D), F32)] + [((2, rows, D), BF16) for rows in PARTS]
OTHER_WORK = [((MB_TOK, D), BF16), ((32, D), F32)]


def section_step(sec_ref, *refs):
    def take(count):
        nonlocal refs
        taken, refs = refs[:count], refs[count:]
        return taken

    x_in, c_in, vec_own, vec_other, ker_own, ker_other, wide_own, wide_other, deep_own, deep_other = take(10)
    table_in = take(4)
    rows_out, (rows_sent,), sent = take(2), take(1), [take(2) for _ in PARTS]
    held = take(len(INPUTS))
    results = take(len(RESULTS))
    kept = (take(len(SAVED)), take(len(SAVED)))
    forward_work = take(len(FORWARD_WORK))
    backward_work = take(len(BACKWARD_WORK))
    feed, small, in_sems, out_sems = refs
    x, c, vecs, taps, wide, deep = held[:6]
    tables = held[6:]
    sec = sec_ref[0]
    at = pl.multiple_of(sec * MB_TOK, 16)
    moves = [
        ("x", x_in.at[pl.ds(at, MB_TOK)], x),
        ("vec", vec_own, vecs.at[sec]),
        ("vec", vec_other, vecs.at[1 - sec]),
        ("rest", table_in[0], tables[0]),
        ("rest", wide_own, wide.at[sec]),
        ("rest", wide_other, wide.at[1 - sec]),
        ("rest", table_in[1], tables[1]),
        ("rest", table_in[2], tables[2]),
        ("rest", table_in[3], tables[3]),
        ("rest", ker_own, taps.at[sec]),
        ("rest", ker_other, taps.at[1 - sec]),
        ("rest", deep_own, deep.at[sec]),
        ("rest", deep_other, deep.at[1 - sec]),
        ("rest", c_in.at[pl.ds(at, MB_TOK)], c),
    ]
    pending = {}
    for index, (name, source, target) in enumerate(moves):
        copy = pltpu.make_async_copy(source, target, in_sems.at[index])
        copy.start()
        pending.setdefault(name, []).append(copy)

    def need(*names):
        for name in names:
            for copy in pending.pop(name, []):
                copy.wait()

    leaving = []

    def leave(index):
        targets = (rows_out[index].at[pl.ds(at, MB_TOK)], rows_sent.at[index]) if index < 2 else sent[index - 2]
        for which, slot in enumerate((sec, 1 - sec)):
            copy = pltpu.make_async_copy(results[index].at[slot], targets[which], out_sems.at[2 * index + which])
            copy.start()
            leaving.append(copy)

    outs, grads, early, inner, outer = results
    small[...] = jnp.zeros_like(small)
    for b in range(2):
        kept[b][3][:, MB_TOK:, :] = jnp.zeros((3, LONG_TOK - MB_TOK, D), BF16)
    backward_work[4][MB_TOK:, :] = jnp.zeros((LONG_TOK - MB_TOK, D), BF16)
    for part, rows in zip((early, inner, outer), PARTS):
        if rows > FF:
            part[:, FF:, :] = jnp.zeros((2, rows - FF, D), BF16)
    weights = [
        (wide.at[b, :, 0 : 3 * D], wide.at[b, :, 3 * D : 4 * D], wide.at[b, :, 4 * D : 8 * D], deep.at[b])
        for b in range(2)
    ]
    sums = [(early.at[b], inner.at[b], outer.at[b]) for b in range(2)]

    def forward(b, source):
        forward_block(
            source, outs.at[b], vecs.at[b], taps.at[b], weights[b], kept[b], tables, forward_work, need
        )

    def backward(b, source):
        backward_block(
            source, grads.at[b], vecs.at[b], taps.at[b], weights[b], kept[b], tables, backward_work, sums[b], small
        )

    forward(0, x)
    feed[...] = outs[0].astype(BF16)
    forward(1, feed)
    backward(1, c)
    feed[...] = grads[1].astype(BF16)
    backward(0, feed)
    for index in range(len(RESULTS)):
        leave(index)
    for copy in leaving:
        copy.wait()


def run_blocks(sec, *arrays):
    shifts, fence, lower = stripe_tables()
    tables = (
        jnp.asarray(turned_table(), BF16),
        jnp.asarray(shifts, BF16),
        jnp.asarray(fence, F32),
        jnp.asarray(lower, F32),
    )
    spaces = [pltpu.HBM] * 3 + [pltpu.VMEM, pltpu.HBM] + [pltpu.VMEM] * 5 + [pltpu.HBM] * 4
    smem = pl.BlockSpec(memory_space=pltpu.SMEM)
    scratch = INPUTS + RESULTS + SAVED + SAVED + FORWARD_WORK + BACKWARD_WORK + OTHER_WORK
    out_shape = [pltpu.HBM((2 * MB_TOK, D), F32)] * 2 + [pltpu.VMEM((2, MB_TOK, D), F32)]
    out_shape += [pltpu.VMEM((rows, D), BF16) for rows in PARTS for _ in range(2)]
    return pl.pallas_call(
        section_step,
        out_shape=out_shape,
        in_specs=[smem] + [pl.BlockSpec(memory_space=space) for space in spaces],
        out_specs=[pl.BlockSpec(memory_space=pltpu.HBM)] * 2 + [pl.BlockSpec(memory_space=pl.ANY)] * 7,
        scratch_shapes=[pltpu.VMEM(shape, kind) for shape, kind in scratch]
        + [pltpu.SemaphoreType.DMA((14,)), pltpu.SemaphoreType.DMA((2 * len(RESULTS),))],
        compiler_params=pltpu.CompilerParams(vmem_limit_bytes=34 << 20),
        name="blocks",
    )(sec, *kept_in(arrays + tables, spaces))


NARROW = (((D, 3 * D), 0), ((D, D), 3 * D), ((D, FF), 4 * D), ((FF, D), None))


def narrowed(*refs):
    sources, (wide, deep), held, (sems,) = refs[:4], refs[4:6], refs[6:10], refs[10:]
    coming = [pltpu.make_async_copy(sources[k], held[k], sems.at[k]) for k in range(4)]
    for copy in coming:
        copy.start()
    for k, (shape, first) in enumerate(NARROW):
        coming[k].wait()
        if first is None:
            deep[...] = held[k][...].astype(BF16)
        else:
            wide[:, first : first + shape[1]] = held[k][...].astype(BF16)


def run_narrowed(*weights):
    vmem = pl.BlockSpec(memory_space=pltpu.VMEM)
    return pl.pallas_call(
        narrowed,
        out_shape=[pltpu.VMEM((D, 8 * D), BF16), pltpu.VMEM((FF, D), BF16)],
        in_specs=[pl.BlockSpec(memory_space=pltpu.HBM)] * 4,
        out_specs=[vmem] * 2,
        scratch_shapes=[pltpu.VMEM(shape, F32) for shape, _ in NARROW] + [pltpu.SemaphoreType.DMA((4,))],
        compiler_params=pltpu.CompilerParams(vmem_limit_bytes=8 << 20),
        name="narrowed",
    )(*kept_in(weights, [pltpu.HBM] * 4))


def square_sum(a_ref, b_ref, c_ref, out_ref):
    total = jnp.zeros((8, D), F32)
    for ref in (a_ref, b_ref, c_ref):
        step = 64
        for start in range(0, ref.shape[0], step):
            rows = ref[start : start + step, :].astype(F32)
            square = rows * rows
            for at in range(0, step, 8):
                total = total + square[at : at + 8]
    total = jnp.sum(jnp.sum(total, axis=0, keepdims=True), axis=1, keepdims=True)
    out_ref[...] = jnp.broadcast_to(total, (8, HALF))


def run_square_sum(a, b, c):
    vmem = pl.BlockSpec(memory_space=pltpu.VMEM)
    return pl.pallas_call(
        square_sum,
        out_shape=jax.ShapeDtypeStruct((8, HALF), F32),
        in_specs=[vmem] * 3,
        out_specs=vmem,
        compiler_params=pltpu.CompilerParams(vmem_limit_bytes=16 << 20),
        name="squares",
    )(a, b, c)


def updated(grad, weight, moment, average, factor):
    decay = min(0.9999, (1.0 + STEP) / (10.0 + STEP))
    clipped = grad * factor
    direction = clipped + WEIGHT_DECAY * weight
    moment_new = MOMENTUM_DECAY * moment + direction
    weight_new = weight - LEARN_RATE * (direction + MOMENTUM_DECAY * moment_new)
    average_new = decay * average + (1.0 - decay) * weight_new
    return clipped, moment_new, weight_new, average_new


SHAPES = ((1, VEC), (1, 9 * D), (D, 3 * D), (D, D), (D, FF), (FF, D))
PIECES = ((3, 0, D), (2, 0, D), (4, 0, D), (5, 0, FF))
OUT_SHAPES = [(shape, F32) for shape in SHAPES] * 4 + [(shape, BF16) for shape in SHAPES[2:]]
MOVES = 2 + 4 * 2 + 5 * len(PIECES)


def optimizer_step(sec_ref, *refs):
    def take(count):
        nonlocal refs
        taken, refs = refs[:count], refs[count:]
        return taken

    (_, _, came), (own, other), (a, b, c), states = take(3), take(2), take(3), take(18)
    outs, (norm_ref,), rows_out, made, (sems,) = take(28), take(1), take(2), take(28), take(1)
    sec = sec_ref[0]
    moves = []

    def leave(source, target):
        move = pltpu.make_async_copy(source, target, sems.at[len(moves)])
        move.start()
        moves.append(move)

    first = pl.multiple_of((1 - sec) * MB_TOK, 8)
    for index in range(2):
        leave(came.at[index], rows_out[index].at[pl.ds(first, MB_TOK)])
    norm = jnp.sqrt(own[0:1, 0:1] + other[0:1, 0:1])
    factor = jnp.minimum(1.0, CLIP_LIMIT / (norm + 1e-06))
    norm_ref[...] = norm

    def put(index, rows, lanes, grad):
        weight, moment, average = (states[kind * 6 + index][rows, lanes] for kind in range(3))
        new = updated(grad, weight, moment, average, factor)
        for kind in range(4):
            made[kind * 6 + index][rows, lanes] = new[kind]
        if index >= 2:
            made[24 + index - 2][rows, lanes] = new[2].astype(BF16)

    places = {2: [(a, 0), (a, D), (a, 2 * D)], 3: [(a, 3 * D)], 4: [(b, part * D) for part in range(4)], 5: [(c, 0)]}
    step = 32
    for index, first, count in PIECES:
        for row in range(first, first + count, step):
            for part, (ref, base) in enumerate(places[index]):
                grad = ref[base + row : base + row + step, :].astype(F32)
                put(index, slice(row, row + step), slice(part * D, (part + 1) * D), grad)
        rows = pl.ds(first, count)
        for kind in range(5):
            at = kind * 6 + index if kind < 4 else 24 + index - 2
            leave(made[at].at[rows], outs[at].at[rows])
    rows = c[FF : FF + 32, :].astype(F32)
    whole = slice(0, 1)
    for part in range(13):
        put(0, whole, slice(part * D, (part + 1) * D), rows[part : part + 1, :])
    for part in range(9):
        put(1, whole, slice(part * D, (part + 1) * D), rows[13 + part : 14 + part, :])
    for index in range(2):
        for kind in range(4):
            leave(made[kind * 6 + index], outs[kind * 6 + index])
    for move in moves:
        move.wait()


def run_optimizer(sec, rows, came, own, other, a, b, c, states):
    vmem = pl.BlockSpec(memory_space=pltpu.VMEM)
    hbm = pl.BlockSpec(memory_space=pltpu.HBM)
    return pl.pallas_call(
        optimizer_step,
        out_shape=[pltpu.HBM(shape, kind) for shape, kind in OUT_SHAPES]
        + [jax.ShapeDtypeStruct((1, 1), F32)]
        + [pltpu.HBM((2 * MB_TOK, D), F32)] * 2,
        in_specs=[pl.BlockSpec(memory_space=pltpu.SMEM)] + [hbm] * 2 + [vmem] * (1 + 2 + 3 + 18),
        out_specs=[hbm] * 28 + [vmem] + [hbm] * 2,
        scratch_shapes=[pltpu.VMEM(shape, kind) for shape, kind in OUT_SHAPES] + [pltpu.SemaphoreType.DMA((MOVES,))],
        compiler_params=pltpu.CompilerParams(vmem_limit_bytes=20 << 20),
        input_output_aliases={1: 29, 2: 30},
        name="optimizer",
    )(sec, *kept_in((*rows, came, own, other, a, b, c, *states), [pltpu.HBM] * 2 + [pltpu.VMEM] * 24))


def swapped(value):
    return lax.ppermute(value, "section", [(0, 1), (1, 0)])


def exchange_orders(bits):
    if bits == 4:
        return ((1, 2, 0, 3), (2, 0, 1, 3), (0, 1, 2, 3))
    turn = max(1, bits // 3)
    every = tuple(range(bits))
    return tuple(every[turn * part :] + every[: turn * part] for part in range(3))


def exchanged(value, bit, size):
    return lax.ppermute(value, "dp", [(index, index ^ (1 << bit)) for index in range(size)])


def exchange_bits():
    size = lax.axis_size("dp")
    bits = size.bit_length() - 1
    if size < 2 or size != 1 << bits or any(2 * rows % size for rows in PARTS):
        return []
    index = lax.axis_index("dp")
    return [((index >> bit) & 1) == 0 for bit in range(bits)]


def summed_over_dp(parts, clear):
    size = lax.axis_size("dp")
    bits = len(clear)
    if not bits:
        return [lax.psum(part.astype(F32), "dp").astype(BF16) for part in parts]
    orders = exchange_orders(bits)
    shapes = [part.shape for part in parts]
    held = [part.reshape((2,) * (bits - 1) + (2 * part.shape[0] // size, D)) for part in parts]
    for step in range(bits):
        kept, came = held, []
        if step < bits - 1:
            kept = [jnp.where(clear[order[step]], value[0], value[1]) for value, order in zip(held, orders)]
            held = [jnp.where(clear[order[step]], value[1], value[0]) for value, order in zip(held, orders)]
        came = [exchanged(value, order[step], size) for value, order in zip(held, orders)]
        held = [(a.astype(F32) + b.astype(F32)).astype(BF16) for a, b in zip(kept, came)]
    for step in reversed(range(bits - 1)):
        grown = []
        for value, order in zip(held, orders):
            low = clear[order[step]]
            came = exchanged(value, order[step], size)
            grown.append(jnp.stack([jnp.where(low, value, came), jnp.where(low, came, value)]))
        held = grown
    return [value.reshape(shape) for value, shape in zip(held, shapes)]


def per_device(inputs, cotangent, *states):
    states = [array.reshape(1, 9 * D) if array.shape == (1, 9, D) else array for array in states]
    states = [array.reshape(array.shape[1:]) if array.ndim == 3 else array for array in states]
    vectors, kernels = states[:2]
    section = lax.axis_index("section").astype(jnp.int32).reshape(1)
    section, *clear = lax.optimization_barrier((section, *exchange_bits()))
    wide, deep = run_narrowed(*states[2:6])
    results = run_blocks(
        section,
        inputs,
        cotangent,
        vectors,
        swapped(vectors),
        kernels,
        swapped(kernels),
        wide,
        swapped(wide),
        deep,
        swapped(deep),
    )
    totals = [
        (own.astype(F32) + swapped(other).astype(F32)).astype(BF16)
        for own, other in zip(results[3::2], results[4::2])
    ]
    a, b, c = summed_over_dp(totals, clear)
    squares = run_square_sum(a, b, c)
    new = run_optimizer(section, results[:2], swapped(results[2]), squares, swapped(squares), a, b, c, states)

    def whole(arrays):
        return [
            array if array.shape == (1, VEC) else array.reshape(1, 9, D) if array.shape == (1, 9 * D) else array[None]
            for array in arrays
        ]

    return (new[29][None], new[30][None], *whole(new[0:6]), new[28].reshape(()), *whole(new[6:28]))


def solution(mesh):
    rows = P("dp", None)
    state = (P("section", None),) + (P("section", None, None),) * 5
    return jax.shard_map(
        per_device,
        mesh=mesh,
        in_specs=(rows, rows) + state * 3,
        out_specs=(P("section", "dp", None),) * 2 + state + (P(),) + state * 3 + state[2:],
        check_vma=False,
    )
```
